128 devices in a mesh: mem: 16 (over z, y), cell: 8 (over x, core).
Axes of the slice: x: 4, y: 4, z: 4, core: 2. Of those that a mesh axis runs over, the one named last changes fastest.
Arguments:
- turnover_effect: float32 [1024, 65536], P('mem', 'cell'), may hold values from -3 to 3
- base_rate: float32 [65536], P('cell'), may hold values from 0.05 to 0.5
- fast_rate: float32 [65536], P('cell'), may hold values from 0.02 to 0.2
- slow_rate: float32 [65536], P('cell'), may hold values from 0.005 to 0.05
- init_pools: float32 [3, 65536], P(None, 'cell'), may hold values from 1 to 6
- litterfall: float32 [6, 65536], P(None, 'cell'), may hold values from 0.1 to 1
- obs_taps: int32 [16384, 4], P('cell'), may hold values from 0 to 127
- obs_weights: float32 [16384, 4], P('cell'), may hold values from 0.05 to 0.5
- observed: float32 [16384], P('cell'), may hold values from 0.5 to 4
- obs_var: float32 [16384], P('cell'), may hold values from 0.008 to 0.11, as said below
- obs_noise: float32 [1024, 16384], P('mem', 'cell'), may hold values from -6 to 6
Outputs:
- updated_effect: float32 [1024, 65536], P('mem', 'cell')
The draws below stay inside these ranges and needn't reach their ends.
Inputs may be any that keep to these rules, and one draw needn't show every extreme that they name: `obs_var`: positive variances.
All inputs are finite; a program needn't handle non-finite values.
Results may differ from the reference program's by a relative error of at most 0.00025.
Values sent between devices are 32-bit elements; how exact they have to be, the bound alone decides.
No kernel may reach another device: no remote copies, remote signals or barrier semaphores. Data moves between devices by JAX's collectives and lax.ppermute only.
A program may use at most 192 MiB of HBM per device.

```python
import math
import jax
import jax.numpy as jnp
from jax import lax

STEPS = 6
BLOCK = 128
TAPS = 4
MEMBERS = 1024
CELLS = 65536
OBS = 16384


def draw_obs_var(key, part):
    index = jnp.arange(OBS, dtype=jnp.float32)
    falling = 0.05 * jnp.exp(-jnp.log(3.0) * index / OBS)
    rough = jnp.exp(jax.random.uniform(key, (OBS,), jnp.float32, -0.6, 0.6))
    return (falling * rough).astype(jnp.float32)


def draw_turnover_effect(key, part):
    mode_count = 20
    subkeys = jax.random.split(jax.random.fold_in(key, 7), 5)
    frequency = jax.random.randint(subkeys[0], (mode_count,), 1, 9).astype(jnp.float32)
    phases = jax.random.uniform(subkeys[1], (mode_count,), jnp.float32, -math.pi, math.pi)
    position = jnp.arange(CELLS, dtype=jnp.float32) / CELLS
    factors = jax.random.normal(subkeys[2], (mode_count, MEMBERS), jnp.float32)
    effect_field = 0.4 * jax.random.normal(subkeys[4], (MEMBERS, CELLS), jnp.float32)
    for mode_index in range(mode_count):
        pattern = math.sqrt(2.0) * jnp.cos(2.0 * math.pi * frequency[mode_index] * position + phases[mode_index])
        effect_field = effect_field + 0.25 * 0.8 ** mode_index * factors[mode_index][:, None] * pattern[None, :]
    return jnp.clip(effect_field, -3.0, 3.0).astype(jnp.float32)


def plant(drawn, stream_key, least, largest):
    longest = drawn.shape.index(max(drawn.shape))
    spots = []
    for shift in (0, 1):
        where = [jax.random.randint(jax.random.fold_in(stream_key, axis), (), 0, length) for axis, length in enumerate(drawn.shape)]
        where[longest] = (where[longest] + shift) % drawn.shape[longest]
        spots.append(tuple(where))
    return drawn.at[spots[0]].set(least).at[spots[1]].set(largest)


def block_scale(stream_key, dims, shards, smallest, high):
    def one(axis_at, blocks):
        steps = jax.random.uniform(jax.random.fold_in(jax.random.fold_in(stream_key, 6), axis_at), (blocks,), jnp.float32, smallest / len(shards), high / len(shards))
        return jnp.repeat(jnp.exp(steps), dims[axis_at] // blocks).reshape((-1,) + (1,) * (len(dims) - axis_at - 1))

    gain = one(*shards[0])
    for cut in shards[1:]:
        gain = gain * one(*cut)
    return gain


def noise(own_key, shape, spread, limit, cuts=(), held_as=jnp.bfloat16):
    drawn = jax.random.normal(own_key, shape, jnp.float32) * spread
    if len(cuts) > 0:
        drawn = block_scale(own_key, shape, cuts, -0.22, 0.18) * drawn
    return jnp.clip(drawn, min=-limit, max=limit).astype(held_as)


def setup_inputs(seed: int = 0) -> dict:
    seeds = jax.random.split(jax.random.key(seed), 12)
    turnover_effect = draw_turnover_effect(jax.random.fold_in(seeds[11], 71), 0)
    base_rate = jnp.clip(jnp.exp(math.log(0.5) - 2.3025851 * jax.random.uniform(seeds[1], (CELLS,), jnp.float32) ** block_scale(seeds[1], (CELLS,), ((0, 8),), -0.2, 0.2)), 0.05, 0.5)
    fast_rate = jnp.clip(jnp.exp(math.log(0.2) - 2.3025851 * jax.random.uniform(seeds[2], (CELLS,), jnp.float32) ** block_scale(seeds[2], (CELLS,), ((0, 8),), -0.2, 0.2)), 0.02, 0.2)
    slow_rate = jnp.clip(jnp.exp(math.log(0.05) - 2.3025851 * jax.random.uniform(seeds[3], (CELLS,), jnp.float32) ** block_scale(seeds[3], (CELLS,), ((0, 8),), -0.2, 0.2)), 0.005, 0.05)
    init_pools = jnp.clip(1.0 + 5.0 * jax.random.uniform(seeds[4], (3, CELLS), jnp.float32) ** block_scale(seeds[4], (3, CELLS), ((1, 8),), -0.2, 0.2), 1.0, 6.0)
    litterfall = jnp.clip(0.1 + 0.9 * jax.random.uniform(seeds[5], (STEPS, CELLS), jnp.float32) ** block_scale(seeds[5], (STEPS, CELLS), ((1, 8),), -0.2, 0.2), 0.1, 1.0)
    obs_taps = plant(jax.random.randint(seeds[6], (OBS, TAPS), 0, BLOCK), jax.random.fold_in(seeds[6], 1), 0, BLOCK - 1).astype(jnp.int32)
    obs_weights = jnp.clip(0.05 + 0.45 * jax.random.uniform(seeds[7], (OBS, TAPS), jnp.float32) ** block_scale(seeds[7], (OBS, TAPS), ((0, 8),), -0.2, 0.2), 0.05, 0.5)
    observed = jnp.clip(0.5 + 3.5 * jax.random.uniform(seeds[8], (OBS,), jnp.float32) ** block_scale(seeds[8], (OBS,), ((0, 8),), -0.2, 0.2), 0.5, 4.0)
    obs_var = draw_obs_var(jax.random.fold_in(seeds[11], 71), 0)
    obs_noise = noise(seeds[10], (MEMBERS, OBS), 1.0, 6.0, ((0, 16), (1, 8)), jnp.float32)
    return dict(turnover_effect=turnover_effect, base_rate=base_rate, fast_rate=fast_rate, slow_rate=slow_rate, init_pools=init_pools, litterfall=litterfall, obs_taps=obs_taps, obs_weights=obs_weights, observed=observed, obs_var=obs_var, obs_noise=obs_noise)


highest = lax.Precision.HIGHEST

def forward(turnover_effect, base_rate, fast_rate, slow_rate, init_pools, litterfall):
    decayed = 1.0 - jnp.exp(-base_rate[None, :] * jnp.exp(turnover_effect))
    litter = jnp.broadcast_to(init_pools[0][None, :], turnover_effect.shape)
    fast_pool = jnp.broadcast_to(init_pools[1][None, :], turnover_effect.shape)
    slow_pool = jnp.broadcast_to(init_pools[2][None, :], turnover_effect.shape)
    resp_total = jnp.zeros(turnover_effect.shape, jnp.float32)
    for month in range(STEPS):
        litter_out = decayed * litter
        fast_out = fast_rate[None, :] * fast_pool
        slow_out = slow_rate[None, :] * slow_pool
        resp_total = resp_total + 0.6 * litter_out + 0.7 * fast_out + slow_out
        litter = litter - litter_out + litterfall[month][None, :]
        fast_pool = fast_pool + 0.4 * litter_out - fast_out
        slow_pool = slow_pool + 0.3 * fast_out - slow_out
    return resp_total

def observe(resp_total, obs_taps, obs_weights):
    member_count = resp_total.shape[0]
    block_count = resp_total.shape[1] // BLOCK
    positions = jnp.arange(BLOCK, dtype=jnp.int32)
    operator_table = jnp.zeros((obs_taps.shape[0], BLOCK), jnp.float32)
    for tap_index in range(TAPS):
        hits = (obs_taps[:, tap_index][:, None] == positions[None, :]).astype(jnp.float32)
        operator_table = operator_table + obs_weights[:, tap_index][:, None] * hits
    operator_table = operator_table.reshape(block_count, -1, BLOCK)
    blocked = resp_total.reshape(member_count, block_count, BLOCK)
    predicted = jnp.einsum('jbc,boc->jbo', blocked, operator_table, precision=highest)
    return predicted.reshape(member_count, -1)

def spd_solve(matrix, right_side):
    factor = jnp.linalg.cholesky(matrix)
    halfway = lax.linalg.triangular_solve(factor, right_side, left_side=True, lower=True)
    return lax.linalg.triangular_solve(factor, halfway, left_side=True, lower=True, transpose_a=True)

def reference(turnover_effect, base_rate, fast_rate, slow_rate, init_pools, litterfall, obs_taps, obs_weights, observed, obs_var, obs_noise):
    resp_total = forward(turnover_effect, base_rate, fast_rate, slow_rate, init_pools, litterfall)
    predicted = observe(resp_total, obs_taps, obs_weights)
    member_count = turnover_effect.shape[0]
    inv_root = 1.0 / jnp.sqrt(jnp.float32(member_count - 1))
    anomaly = (turnover_effect - lax.optimization_barrier(jnp.mean(turnover_effect, axis=0))[None, :]) * inv_root
    pred_anomaly = (predicted - lax.optimization_barrier(jnp.mean(predicted, axis=0))[None, :]) * inv_root
    residual = observed[None, :] - predicted
    misfit = jnp.sum(residual * residual / obs_var[None, :]) / (member_count * predicted.shape[1])
    step_size = 1.0 / misfit
    departure = observed[None, :] + jnp.sqrt(obs_var)[None, :] * obs_noise - predicted
    weighted = pred_anomaly / obs_var[None, :]
    gram = jnp.dot(weighted, pred_anomaly.T, precision=highest)
    rhs = jnp.dot(weighted, departure.T, precision=highest)
    system = jnp.eye(member_count, dtype=jnp.float32) + step_size * gram
    solve = spd_solve(system, step_size * rhs)
    return turnover_effect + jnp.dot(solve.T, anomaly, precision=highest)
```

```python
import math

import jax
import jax.numpy as jnp
from jax import lax
from jax.experimental import pallas as pl
from jax.experimental.pallas import tpu as pltpu
from jax.sharding import Mesh, PartitionSpec as P

STEPS = 6
BLOCK = 128
TAPS = 4
Z = 4
Y = 4
X = 4
LANES = 128
HALF = 128
TILE = 256
CHUNK = 1024
f32 = jnp.float32

ANY_VMEM = pl.BlockSpec(memory_space=pltpu.VMEM)
ANY_SMEM = pl.BlockSpec(memory_space=pltpu.SMEM)


def mm(left, right):
    return jnp.dot(left, right, precision=lax.Precision.HIGHEST, preferred_element_type=f32)


def mm_last(left, right):
    return lax.dot_general(
        left, right, (((1,), (1,)), ((), ())),
        precision=lax.Precision.HIGHEST, preferred_element_type=f32,
    )


def forward_kernel(
    effect, base, fast, slow, init, fall, taps, weights, observed, var, pred, small, resp, coef
):
    step = pl.program_id(0)
    members, cells = effect.shape
    w = slow[...]
    f = fast[...]
    left_slow = [jnp.zeros_like(w)]
    left_fast = [jnp.zeros_like(w)]
    for _ in range(STEPS):
        left_fast.append(0.7 * f + 0.3 * f * left_slow[-1] + (1.0 - f) * left_fast[-1])
        left_slow.append(w + (1.0 - w) * left_slow[-1])
    share = [0.6 + 0.4 * left_fast[STEPS - 1 - t] for t in range(STEPS)]
    for power in range(STEPS):
        total = share[power] * init[0:1, :]
        for t in range(power + 1, STEPS):
            total = total + share[t] * fall[t - 1 - power : t - power, :]
        coef[power : power + 1, :] = total
    coef[6:7, :] = init[1:2, :] * left_fast[STEPS] + init[2:3, :] * left_slow[STEPS]
    coef[7:8, :] = -base[...]

    def rows(i, _):
        at = pl.ds(pl.multiple_of(i * 8, 8), 8)
        kept = jnp.exp(coef[7:8, :] * jnp.exp(effect[at, :]))
        total = coef[5:6, :]
        for power in range(4, -1, -1):
            total = total * kept + coef[power : power + 1, :]
        resp[at, :] = coef[6:7, :] + (1.0 - kept) * total
        return 0

    lax.fori_loop(0, members // 8, rows, 0)
    position = lax.broadcasted_iota(jnp.int32, (BLOCK, LANES), 0)
    owner = lax.broadcasted_iota(jnp.int32, (members, LANES), 1) // 32
    spread = jnp.zeros((1, LANES), f32)
    for group in range(cells // (4 * BLOCK)):
        lanes = slice(group * LANES, (group + 1) * LANES)
        table = jnp.zeros((BLOCK, LANES), f32)
        for k in range(TAPS):
            table = table + jnp.where(taps[k : k + 1, lanes] == position, weights[k : k + 1, lanes], 0.0)
        stacked = jnp.concatenate(
            [resp[:, (4 * group + b) * BLOCK : (4 * group + b + 1) * BLOCK] for b in range(4)], axis=0
        )
        product = mm(stacked, table)
        out = product[:members]
        for b in range(1, 4):
            out = jnp.where(owner == b, product[b * members : (b + 1) * members], out)
        pred[:, lanes] = out
        small[0:1, pl.ds(pl.multiple_of(step * (cells // 4) + group * LANES, LANES), LANES)] = jnp.sum(
            out, axis=0, keepdims=True
        )
        residual = observed[:, lanes] - out
        spread = spread + jnp.sum(residual * residual, axis=0, keepdims=True) / var[:, lanes]
    spread = jnp.broadcast_to(jnp.sum(spread, axis=1, keepdims=True), (1, LANES))
    tail = pl.ds(small.shape[1] - LANES, LANES)

    @pl.when(step == 0)
    def _():
        small[0:1, tail] = spread

    @pl.when(step > 0)
    def _():
        small[0:1, tail] = small[0:1, tail] + spread


def forward(effect, base, fast, slow, init, fall, taps, weights, observed, var):
    members, cells = effect.shape
    obs = taps.shape[1]
    obs_chunk = CHUNK // 4

    def wide(rows, width):
        return pl.BlockSpec((rows, width), lambda i: (0, i))

    return pl.pallas_call(
        forward_kernel,
        grid=(cells // CHUNK,),
        in_specs=[
            wide(members, CHUNK), wide(1, CHUNK), wide(1, CHUNK), wide(1, CHUNK),
            wide(3, CHUNK), wide(STEPS, CHUNK), wide(TAPS, obs_chunk), wide(TAPS, obs_chunk),
            wide(1, obs_chunk), wide(1, obs_chunk),
        ],
        out_specs=[wide(members, obs_chunk), pl.BlockSpec((1, obs + LANES), lambda i: (0, 0))],
        out_shape=[
            jax.ShapeDtypeStruct((members, obs), f32),
            jax.ShapeDtypeStruct((1, obs + LANES), f32),
        ],
        scratch_shapes=[pltpu.VMEM((members, CHUNK), f32), pltpu.VMEM((8, CHUNK), f32)],
        name="forward",
    )(effect, base, fast, slow, init, fall, taps, weights, observed, var)


def gram_kernel(
    where, p0, p1, p2, p3, c1, c2, c3, n0, n1, n2, n3, observed, var, sums, misfit, out,
    left, right, total,
):
    step = pl.program_id(0)
    zid, yid = where[0], where[1]
    members = p0.shape[0]
    member_count = members * Z * Y
    inv_root = 1.0 / math.sqrt(member_count - 1)
    mean = sums[...] / member_count
    inv_var = 1.0 / var[...]
    root_var = jnp.sqrt(var[...])
    for a, (p, n) in enumerate(((p0, n0), (p1, n1), (p2, n2), (p3, n3))):
        at = pl.multiple_of((yid ^ a) * members, members)
        left[pl.ds(at, members), :] = (p[...] - mean) * inv_root
        left[pl.ds(at + Y * members, members), :] = observed[...] + root_var * n[...] - p[...]
    for b, c in enumerate((p0, c1, c2, c3)):
        at = pl.multiple_of((zid ^ b) * members, members)
        right[pl.ds(at, members), :] = (c[...] - mean) * inv_root * inv_var

    product = mm_last(left[...], right[...])

    @pl.when(step == 0)
    def _():
        total[...] = product

    @pl.when(step > 0)
    def _():
        total[...] = total[...] + product

    @pl.when(step == pl.num_programs(0) - 1)
    def _():
        for c in range(8):
            out[c, 0:32, 0:TILE] = total[c * 32 : c * 32 + 32, :]
            out[c, 0:32, TILE : 2 * TILE] = total[TILE + c * 32 : TILE + c * 32 + 32, :]
            out[c, 32:40, :] = jnp.broadcast_to(misfit[0:1, 0:1], (8, 2 * TILE))


def gram_block(where, rows, columns, noises, observed, var, sums, misfit):
    members, obs = rows[0].shape
    width = 512

    def chunk(n):
        return pl.BlockSpec((n, width), lambda i: (0, i))

    return pl.pallas_call(
        gram_kernel,
        grid=(obs // width,),
        in_specs=[ANY_SMEM] + [chunk(members)] * 11 + [chunk(1)] * 3
        + [pl.BlockSpec((1, LANES), lambda i: (0, 0))],
        out_specs=pl.BlockSpec((8, 40, 2 * TILE), lambda i: (0, 0, 0)),
        out_shape=jax.ShapeDtypeStruct((8, 40, 2 * TILE), f32),
        scratch_shapes=[
            pltpu.VMEM((2 * TILE, width), f32),
            pltpu.VMEM((TILE, width), f32),
            pltpu.VMEM((2 * TILE, TILE), f32),
        ],
        name="gram",
    )(where, *rows, *columns, *noises, observed, var, sums, misfit)


def invert_block(rows):
    width = HALF
    count = width // 8
    rows = list(rows)
    lane = lax.broadcasted_iota(jnp.int32, (8, width), 1)
    sub = lax.broadcasted_iota(jnp.int32, (8, width), 0)

    def row(value, r):
        return jnp.broadcast_to(value[r : r + 1, :], (8, width))

    for block in range(count):
        low = 8 * block
        panel = rows[block]
        inside = (lane >= low) & (lane < low + 8)
        pivots = [jnp.broadcast_to(panel[:, low + p : low + p + 1], (8, width)) for p in range(8)]
        for r in range(8):
            heads = [row(pivots[p], r) for p in range(8)]
            inverse = 1.0 / heads[r]
            here = sub == r
            column = jnp.where(here, 0.0, pivots[r])
            for p in range(8):
                if p != r:
                    scaled = heads[p] * inverse
                    pivots[p] = jnp.where(here, scaled, pivots[p] - column * scaled)
            pivots[r] = jnp.where(here, inverse, -column * inverse)
        panel = jnp.where(inside, jnp.where(lane - low == sub, 1.0, 0.0), panel)
        terms = [pivots[p] * row(panel, p) for p in range(8)]
        while len(terms) > 1:
            terms = [terms[i] + terms[i + 1] for i in range(0, len(terms), 2)]
        solved = terms[0]
        heads = [row(solved, p) for p in range(8)]
        for step in range(1, count):
            i = (block + step) % count
            terms = [
                jnp.broadcast_to(rows[i][:, low + p : low + p + 1], (8, width)) * heads[p]
                for p in range(8)
            ]
            while len(terms) > 1:
                terms = [terms[j] + terms[j + 1] for j in range(0, len(terms), 2)]
            rows[i] = jnp.where(inside, 0.0, rows[i]) - terms[0]
        rows[block] = solved
    return rows


def factor_kernel(where, mine, other, misfit, system, inverses, halves, ahead, behind):
    core = where[2]
    scale = (f32(1024 * 16384) / misfit[0:1, 0:1])
    for z in range(Z):
        for y in range(Y):
            for x in range(X):
                piece = slice(((z * Y + y) * X + x) * 32, ((z * Y + y) * X + x) * 32 + 32)
                at = x * TILE + z * 64
                lanes = slice(y * TILE, (y + 1) * TILE)
                system[pl.ds(pl.multiple_of(at + core * 32, 32), 32), lanes] = mine[piece, :] * scale
                system[pl.ds(pl.multiple_of(at + 32 - core * 32, 32), 32), lanes] = other[piece, :] * scale
    eye = jnp.where(
        lax.broadcasted_iota(jnp.int32, (HALF, HALF), 0) == lax.broadcasted_iota(jnp.int32, (HALF, HALF), 1),
        1.0, 0.0,
    )
    for d in range(system.shape[0] // HALF):
        at = slice(d * HALF, (d + 1) * HALF)
        system[at, at] = system[at, at] + eye
    tiles = system.shape[0] // TILE

    def outer(k, _):
        top = pl.multiple_of(k * TILE, TILE)
        low = pl.multiple_of(k * TILE + HALF, HALF)

        def half(h, _):
            at = pl.multiple_of(top + h * HALF, HALF)
            block = [system[pl.ds(at + 8 * j, 8), pl.ds(at, HALF)] for j in range(HALF // 8)]
            block = invert_block(block)
            for j in range(HALF // 8):
                halves[pl.ds(pl.multiple_of(h * HALF + 8 * j, 8), 8), :] = block[j]

            @pl.when(h == 0)
            def _():
                first = halves[0:HALF, :]
                upper = system[pl.ds(top, HALF), pl.ds(low, HALF)]
                ahead[...] = mm(first, upper)
                behind[...] = mm(system[pl.ds(low, HALF), pl.ds(top, HALF)], first)
                system[pl.ds(low, HALF), pl.ds(low, HALF)] = (
                    system[pl.ds(low, HALF), pl.ds(low, HALF)] - mm(behind[...], upper)
                )

            return 0

        lax.fori_loop(0, 2, half, 0)
        second = halves[HALF:, :]
        corner = mm(second, behind[...])
        inverses[pl.ds(top, HALF), 0:HALF] = halves[0:HALF, :] + mm(ahead[...], corner)
        inverses[pl.ds(top, HALF), HALF:] = -mm(ahead[...], second)
        inverses[pl.ds(low, HALF), 0:HALF] = -corner
        inverses[pl.ds(low, HALF), HALF:] = second

        def across(t, _):
            lanes = pl.ds(pl.multiple_of(t * TILE, TILE), TILE)
            solved = mm(inverses[pl.ds(top, TILE), :], system[pl.ds(top, TILE), lanes])
            system[pl.ds(top, TILE), lanes] = solved

            def down(i, _):
                at = pl.ds(pl.multiple_of(i * TILE, TILE), TILE)
                system[at, lanes] = system[at, lanes] - mm(
                    system[at, pl.ds(top, TILE)], system[pl.ds(top, TILE), lanes]
                )
                return 0

            lax.fori_loop(k + 1, tiles, down, 0)
            return 0

        lax.fori_loop(k + 1, tiles, across, 0)
        return 0

    lax.fori_loop(0, tiles, outer, 0)


def factor(where, mine, other, misfit):
    n = TILE * Y
    return pl.pallas_call(
        factor_kernel,
        in_specs=[ANY_SMEM, ANY_VMEM, ANY_VMEM, ANY_VMEM],
        out_specs=[ANY_VMEM, ANY_VMEM],
        out_shape=[jax.ShapeDtypeStruct((n, n), f32), jax.ShapeDtypeStruct((n, TILE), f32)],
        scratch_shapes=[
            pltpu.VMEM((TILE, HALF), f32), pltpu.VMEM((HALF, HALF), f32), pltpu.VMEM((HALF, HALF), f32),
        ],
        cost_estimate=pl.CostEstimate(flops=int(2e10), bytes_accessed=int(1e7), transcendentals=0),
        name="factor",
    )(where, mine, other, misfit)


def update_kernel(where, system, inverses, rhs, misfit, *refs):
    blocks, out, value, work = refs[:4], refs[4], refs[5], refs[6]
    zid, yid = where[0], where[1]
    n = system.shape[0]
    tiles = n // TILE
    scale = (f32(1024 * 16384) / misfit[0:1, 0:1])
    for a in range(Y):
        for b in range(Z):
            at = pl.multiple_of((yid ^ a) * TILE + (zid ^ b) * 64, 64)
            value[pl.ds(at, 64), :] = blocks[a][b * 64 : (b + 1) * 64, :]
    mean = jnp.sum(value[...], axis=0, keepdims=True) / n
    inv_root = 1.0 / math.sqrt(n - 1)
    work[...] = (value[...] - mean) * inv_root
    for k in range(tiles):
        at = slice(k * TILE, (k + 1) * TILE)
        work[at, :] = mm(inverses[at, :], work[at, :])
        for i in range(k + 1, tiles):
            down = slice(i * TILE, (i + 1) * TILE)
            work[down, :] = work[down, :] - mm(system[down, at], work[at, :])
    for k in range(tiles - 2, -1, -1):
        at = slice(k * TILE, (k + 1) * TILE)
        rest = slice((k + 1) * TILE, n)
        work[at, :] = work[at, :] - mm(system[at, rest], work[rest, :])
    for z in range(Z):
        total = mm(rhs[z * Y * TILE : (z * Y + 1) * TILE, :], work[0:TILE, :])
        for y in range(1, Y):
            total = total + mm(
                rhs[(z * Y + y) * TILE : (z * Y + y + 1) * TILE, :], work[y * TILE : (y + 1) * TILE, :]
            )
        for y in range(Y):
            out[z * TILE + y * 64 : z * TILE + (y + 1) * 64, :] = (
                value[y * TILE + z * 64 : y * TILE + (z + 1) * 64, :] + scale * total[y * 64 : (y + 1) * 64, :]
            )


def update(where, system, inverses, rhs, misfit, blocks):
    n = system.shape[0]
    width = blocks[0].shape[1]
    return pl.pallas_call(
        update_kernel,
        in_specs=[ANY_SMEM] + [ANY_VMEM] * 8,
        out_specs=ANY_VMEM,
        out_shape=jax.ShapeDtypeStruct((n, width), f32),
        scratch_shapes=[pltpu.VMEM((n, width), f32), pltpu.VMEM((n, width), f32)],
        cost_estimate=pl.CostEstimate(flops=int(1e10), bytes_accessed=int(1e7), transcendentals=0),
        name="update",
    )(where, system, inverses, rhs, misfit, *blocks)


def swap(value, axis, size, bit):
    return lax.ppermute(value, axis, [(i, i ^ bit) for i in range(size)])


def body(
    turnover_effect,
    base_rate,
    fast_rate,
    slow_rate,
    init_pools,
    litterfall,
    obs_taps,
    obs_weights,
    observed,
    obs_var,
    obs_noise,
):
    members, cells = turnover_effect.shape
    obs = obs_taps.shape[0]
    zid, yid, core = lax.axis_index("z"), lax.axis_index("y"), lax.axis_index("core")
    where = jnp.stack([zid, yid, core]).astype(jnp.int32)
    observed = observed[None, :]
    obs_var = obs_var[None, :]
    noises = [obs_noise] + [swap(obs_noise, "y", Y, a) for a in range(1, Y)]
    predicted, small = forward(
        turnover_effect, base_rate[None, :], fast_rate[None, :], slow_rate[None, :],
        init_pools, litterfall, obs_taps.T, obs_weights.T, observed, obs_var,
    )
    rows = [predicted] + [swap(predicted, "y", Y, a) for a in range(1, Y)]
    columns = [swap(predicted, "z", Z, b) for b in range(1, Z)]
    for axis in ("y", "z"):
        for bit in (1, 2):
            small = small + swap(small, axis, 4, bit)
    block = gram_block(where, rows, columns, noises, observed, obs_var, small[:, :obs], small[:, obs:])
    effect, block = lax.optimization_barrier((turnover_effect, block))
    wide = cells // Z
    strip = [lax.dynamic_slice_in_dim(effect, (zid ^ b) * wide, wide, 1) for b in range(Z)]
    strip = jnp.concatenate([strip[0]] + [swap(strip[b], "z", Z, b) for b in range(1, Z)], axis=0)
    shared = jnp.sum(lax.all_to_all(block, ("x", "core"), 0, 0, tiled=False), axis=0)
    piece, right, misfit = shared[:32, :TILE], shared[:32, TILE:], shared[32:, :LANES]
    rhs = lax.all_gather(right, ("z", "y", "x", "core"), axis=0, tiled=True)
    mine = lax.all_to_all(
        jnp.broadcast_to(piece[None], (Z * Y * X, 32, TILE)), ("z", "y", "x"), 0, 0, tiled=True
    ).reshape(Z * Y * X * 32, TILE)
    other = swap(mine, "core", 2, 1)
    strip, other = lax.optimization_barrier((strip, other))
    narrow = wide // Y
    cut = [lax.dynamic_slice_in_dim(strip, (yid ^ a) * narrow, narrow, 1) for a in range(Y)]
    cut = [cut[0]] + [swap(cut[a], "y", Y, a) for a in range(1, Y)]
    system, inverses = factor(where, mine, other, misfit)
    changed = update(where, system, inverses, rhs, misfit, cut)
    return lax.all_to_all(changed, ("z", "y"), 0, 1, tiled=True)


def solution(mesh):
    grid = Mesh(mesh.devices.reshape(Z, Y, X, 2), ("z", "y", "x", "core"))
    mem, cell = ("z", "y"), ("x", "core")
    in_specs = (
        P(mem, cell),
        P(cell),
        P(cell),
        P(cell),
        P(None, cell),
        P(None, cell),
        P(cell, None),
        P(cell, None),
        P(cell),
        P(cell),
        P(mem, cell),
    )
    return jax.shard_map(
        body, mesh=grid, in_specs=in_specs, out_specs=P(mem, cell), check_vma=False
    )
```

```python
import math

import jax
import jax.numpy as jnp
from jax import lax
from jax.experimental import pallas as pl
from jax.experimental.pallas import tpu as pltpu
from jax.sharding import Mesh, PartitionSpec as P

STEPS = 6
BLOCK = 128
TAPS = 4
Z = 4
Y = 4
X = 4
LANES = 128
HALF = 128
TILE = 256
CHUNK = 1024
f32 = jnp.float32

ANY_VMEM = pl.BlockSpec(memory_space=pltpu.VMEM)
ANY_SMEM = pl.BlockSpec(memory_space=pltpu.SMEM)


def mm(left, right):
    return jnp.dot(left, right, precision=lax.Precision.HIGHEST, preferred_element_type=f32)


def mm_last(left, right):
    return lax.dot_general(
        left, right, (((1,), (1,)), ((), ())),
        precision=lax.Precision.HIGHEST, preferred_element_type=f32,
    )


def forward_kernel(
    effect, base, fast, slow, init, fall, taps, weights, observed, var, pred, small, resp, coef
):
    step = pl.program_id(0)
    members, cells = effect.shape
    w = slow[...]
    f = fast[...]
    left_slow = [jnp.zeros_like(w)]
    left_fast = [jnp.zeros_like(w)]
    for _ in range(STEPS):
        left_fast.append(0.7 * f + 0.3 * f * left_slow[-1] + (1.0 - f) * left_fast[-1])
        left_slow.append(w + (1.0 - w) * left_slow[-1])
    share = [0.6 + 0.4 * left_fast[STEPS - 1 - t] for t in range(STEPS)]
    for power in range(STEPS):
        total = share[power] * init[0:1, :]
        for t in range(power + 1, STEPS):
            total = total + share[t] * fall[t - 1 - power : t - power, :]
        coef[power : power + 1, :] = total
    coef[6:7, :] = init[1:2, :] * left_fast[STEPS] + init[2:3, :] * left_slow[STEPS]
    coef[7:8, :] = -base[...]

    def rows(i, _):
        at = pl.ds(pl.multiple_of(i * 8, 8), 8)
        kept = jnp.exp(coef[7:8, :] * jnp.exp(effect[at, :]))
        total = coef[5:6, :]
        for power in range(4, -1, -1):
            total = total * kept + coef[power : power + 1, :]
        resp[at, :] = coef[6:7, :] + (1.0 - kept) * total
        return 0

    lax.fori_loop(0, members // 8, rows, 0)
    position = lax.broadcasted_iota(jnp.int32, (BLOCK, LANES), 0)
    owner = lax.broadcasted_iota(jnp.int32, (members, LANES), 1) // 32
    spread = jnp.zeros((1, LANES), f32)
    for group in range(cells // (4 * BLOCK)):
        lanes = slice(group * LANES, (group + 1) * LANES)
        table = jnp.zeros((BLOCK, LANES), f32)
        for k in range(TAPS):
            table = table + jnp.where(taps[k : k + 1, lanes] == position, weights[k : k + 1, lanes], 0.0)
        stacked = jnp.concatenate(
            [resp[:, (4 * group + b) * BLOCK : (4 * group + b + 1) * BLOCK] for b in range(4)], axis=0
        )
        product = mm(stacked, table)
        out = product[:members]
        for b in range(1, 4):
            out = jnp.where(owner == b, product[b * members : (b + 1) * members], out)
        pred[:, lanes] = out
        small[0:1, pl.ds(pl.multiple_of(step * (cells // 4) + group * LANES, LANES), LANES)] = jnp.sum(
            out, axis=0, keepdims=True
        )
        residual = observed[:, lanes] - out
        spread = spread + jnp.sum(residual * residual, axis=0, keepdims=True) / var[:, lanes]
    spread = jnp.broadcast_to(jnp.sum(spread, axis=1, keepdims=True), (1, LANES))
    tail = pl.ds(small.shape[1] - LANES, LANES)

    @pl.when(step == 0)
    def _():
        small[0:1, tail] = spread

    @pl.when(step > 0)
    def _():
        small[0:1, tail] = small[0:1, tail] + spread


def forward(effect, base, fast, slow, init, fall, taps, weights, observed, var):
    members, cells = effect.shape
    obs = taps.shape[1]
    obs_chunk = CHUNK // 4

    def wide(rows, width):
        return pl.BlockSpec((rows, width), lambda i: (0, i))

    return pl.pallas_call(
        forward_kernel,
        grid=(cells // CHUNK,),
        in_specs=[
            wide(members, CHUNK), wide(1, CHUNK), wide(1, CHUNK), wide(1, CHUNK),
            wide(3, CHUNK), wide(STEPS, CHUNK), wide(TAPS, obs_chunk), wide(TAPS, obs_chunk),
            wide(1, obs_chunk), wide(1, obs_chunk),
        ],
        out_specs=[wide(members, obs_chunk), pl.BlockSpec((1, obs + LANES), lambda i: (0, 0))],
        out_shape=[
            jax.ShapeDtypeStruct((members, obs), f32),
            jax.ShapeDtypeStruct((1, obs + LANES), f32),
        ],
        scratch_shapes=[pltpu.VMEM((members, CHUNK), f32), pltpu.VMEM((8, CHUNK), f32)],
        name="forward",
    )(effect, base, fast, slow, init, fall, taps, weights, observed, var)


def gram_kernel(
    where, p0, p1, p2, p3, c1, c2, c3, noise, observed, var, sums, misfit, out,
    left, right, total,
):
    step = pl.program_id(0)
    zid, yid = where[0], where[1]
    members = p0.shape[0]
    member_count = members * Z * Y
    inv_root = 1.0 / math.sqrt(member_count - 1)
    mean = sums[...] / member_count
    inv_var = 1.0 / var[...]
    root_var = jnp.sqrt(var[...])
    for a, p in enumerate((p0, p1, p2, p3)):
        at = pl.multiple_of((yid ^ a) * members, members)
        left[pl.ds(at, members), :] = (p[...] - mean) * inv_root
        left[pl.ds(at + Y * members, members), :] = (
            observed[...] + root_var * noise[pl.ds(at, members), :] - p[...]
        )
    for b, c in enumerate((p0, c1, c2, c3)):
        at = pl.multiple_of((zid ^ b) * members, members)
        right[pl.ds(at, members), :] = (c[...] - mean) * inv_root * inv_var

    product = mm_last(left[...], right[...])

    @pl.when(step == 0)
    def _():
        total[...] = product

    @pl.when(step > 0)
    def _():
        total[...] = total[...] + product

    @pl.when(step == pl.num_programs(0) - 1)
    def _():
        for c in range(8):
            out[c, 0:32, 0:TILE] = total[c * 32 : c * 32 + 32, :]
            out[c, 0:32, TILE : 2 * TILE] = total[TILE + c * 32 : TILE + c * 32 + 32, :]
            out[c, 32:40, :] = jnp.broadcast_to(misfit[0:1, 0:1], (8, 2 * TILE))


def gram_block(where, rows, columns, noise, observed, var, sums, misfit):
    members, obs = rows[0].shape
    width = 512

    def chunk(n):
        return pl.BlockSpec((n, width), lambda i: (0, i))

    return pl.pallas_call(
        gram_kernel,
        grid=(obs // width,),
        in_specs=[ANY_SMEM] + [chunk(members)] * 7 + [chunk(members * Y)] + [chunk(1)] * 3
        + [pl.BlockSpec((1, LANES), lambda i: (0, 0))],
        out_specs=pl.BlockSpec((8, 40, 2 * TILE), lambda i: (0, 0, 0)),
        out_shape=jax.ShapeDtypeStruct((8, 40, 2 * TILE), f32),
        scratch_shapes=[
            pltpu.VMEM((2 * TILE, width), f32),
            pltpu.VMEM((TILE, width), f32),
            pltpu.VMEM((2 * TILE, TILE), f32),
        ],
        name="gram",
    )(where, *rows, *columns, noise, observed, var, sums, misfit)


def invert_block(rows):
    width = HALF
    count = width // 8
    rows = list(rows)
    lane = lax.broadcasted_iota(jnp.int32, (8, width), 1)
    sub = lax.broadcasted_iota(jnp.int32, (8, width), 0)

    def row(value, r):
        return jnp.broadcast_to(value[r : r + 1, :], (8, width))

    for block in range(count):
        low = 8 * block
        panel = rows[block]
        inside = (lane >= low) & (lane < low + 8)
        pivots = [jnp.broadcast_to(panel[:, low + p : low + p + 1], (8, width)) for p in range(8)]
        for r in range(8):
            heads = [row(pivots[p], r) for p in range(8)]
            inverse = 1.0 / heads[r]
            here = sub == r
            column = jnp.where(here, 0.0, pivots[r])
            for p in range(8):
                if p != r:
                    scaled = heads[p] * inverse
                    pivots[p] = jnp.where(here, scaled, pivots[p] - column * scaled)
            pivots[r] = jnp.where(here, inverse, -column * inverse)
        panel = jnp.where(inside, jnp.where(lane - low == sub, 1.0, 0.0), panel)
        terms = [pivots[p] * row(panel, p) for p in range(8)]
        while len(terms) > 1:
            terms = [terms[i] + terms[i + 1] for i in range(0, len(terms), 2)]
        solved = terms[0]
        heads = [row(solved, p) for p in range(8)]
        for step in range(1, count):
            i = (block + step) % count
            terms = [
                jnp.broadcast_to(rows[i][:, low + p : low + p + 1], (8, width)) * heads[p]
                for p in range(8)
            ]
            while len(terms) > 1:
                terms = [terms[j] + terms[j + 1] for j in range(0, len(terms), 2)]
            rows[i] = jnp.where(inside, 0.0, rows[i]) - terms[0]
        rows[block] = solved
    return rows


def begin_kernel(where, mine, other, misfit, system, inverses, halves, ahead, behind):
    core = where[2]
    scale = (f32(1024 * 16384) / misfit[0:1, 0:1])
    for z in range(Z):
        for y in range(Y):
            for x in range(X):
                piece = slice(((z * Y + y) * X + x) * 32, ((z * Y + y) * X + x) * 32 + 32)
                at = x * TILE + z * 64
                lanes = slice(y * TILE, (y + 1) * TILE)
                system[pl.ds(pl.multiple_of(at + core * 32, 32), 32), lanes] = mine[piece, :] * scale
                system[pl.ds(pl.multiple_of(at + 32 - core * 32, 32), 32), lanes] = other[piece, :] * scale
    eye = jnp.where(
        lax.broadcasted_iota(jnp.int32, (HALF, HALF), 0) == lax.broadcasted_iota(jnp.int32, (HALF, HALF), 1),
        1.0, 0.0,
    )
    for d in range(system.shape[0] // HALF):
        at = slice(d * HALF, (d + 1) * HALF)
        system[at, at] = system[at, at] + eye
    eliminate(system, inverses, 0, halves, ahead, behind, 0, 1)


def finish_kernel(before, system, inverses, halves, ahead, behind, arrived):
    copy = pltpu.make_async_copy(before, system, arrived)
    copy.start()
    copy.wait()
    eliminate(system, inverses, TILE, halves, ahead, behind, 1, system.shape[0] // TILE)


def eliminate(system, inverses, offset, halves, ahead, behind, start, stop):
    tiles = system.shape[0] // TILE

    def outer(k, _):
        kept = pl.multiple_of(k * TILE - offset, TILE)
        top = pl.multiple_of(k * TILE, TILE)
        low = pl.multiple_of(k * TILE + HALF, HALF)

        def half(h, _):
            at = pl.multiple_of(top + h * HALF, HALF)
            block = [system[pl.ds(at + 8 * j, 8), pl.ds(at, HALF)] for j in range(HALF // 8)]
            block = invert_block(block)
            for j in range(HALF // 8):
                halves[pl.ds(pl.multiple_of(h * HALF + 8 * j, 8), 8), :] = block[j]

            @pl.when(h == 0)
            def _():
                first = halves[0:HALF, :]
                upper = system[pl.ds(top, HALF), pl.ds(low, HALF)]
                ahead[...] = mm(first, upper)
                behind[...] = mm(system[pl.ds(low, HALF), pl.ds(top, HALF)], first)
                system[pl.ds(low, HALF), pl.ds(low, HALF)] = (
                    system[pl.ds(low, HALF), pl.ds(low, HALF)] - mm(behind[...], upper)
                )

            return 0

        lax.fori_loop(0, 2, half, 0)
        second = halves[HALF:, :]
        corner = mm(second, behind[...])
        inverses[pl.ds(kept, HALF), 0:HALF] = halves[0:HALF, :] + mm(ahead[...], corner)
        inverses[pl.ds(kept, HALF), HALF:] = -mm(ahead[...], second)
        inverses[pl.ds(kept + HALF, HALF), 0:HALF] = -corner
        inverses[pl.ds(kept + HALF, HALF), HALF:] = second

        def across(t, _):
            lanes = pl.ds(pl.multiple_of(t * TILE, TILE), TILE)
            solved = mm(inverses[pl.ds(kept, TILE), :], system[pl.ds(top, TILE), lanes])
            system[pl.ds(top, TILE), lanes] = solved

            def down(i, _):
                at = pl.ds(pl.multiple_of(i * TILE, TILE), TILE)
                system[at, lanes] = system[at, lanes] - mm(
                    system[at, pl.ds(top, TILE)], system[pl.ds(top, TILE), lanes]
                )
                return 0

            lax.fori_loop(k + 1, tiles, down, 0)
            return 0

        lax.fori_loop(k + 1, tiles, across, 0)
        return 0

    lax.fori_loop(start, stop, outer, 0)


FACTOR_SCRATCH = [
    pltpu.VMEM((TILE, HALF), f32), pltpu.VMEM((HALF, HALF), f32), pltpu.VMEM((HALF, HALF), f32),
]


def cost(flops):
    return pl.CostEstimate(flops=int(flops), bytes_accessed=int(1e7), transcendentals=0)


def factor_begin(where, mine, other, misfit):
    n = TILE * Y
    return pl.pallas_call(
        begin_kernel,
        in_specs=[ANY_SMEM, ANY_VMEM, ANY_VMEM, ANY_VMEM],
        out_specs=[ANY_VMEM, ANY_VMEM],
        out_shape=[jax.ShapeDtypeStruct((n, n), f32), jax.ShapeDtypeStruct((TILE, TILE), f32)],
        scratch_shapes=FACTOR_SCRATCH,
        cost_estimate=cost(2e10),
        name="factor_begin",
    )(where, mine, other, misfit)


def factor_finish(system):
    n = system.shape[0]
    return pl.pallas_call(
        finish_kernel,
        in_specs=[pl.BlockSpec(memory_space=pl.ANY)],
        out_specs=[ANY_VMEM, ANY_VMEM],
        out_shape=[jax.ShapeDtypeStruct((n, n), f32), jax.ShapeDtypeStruct((n - TILE, TILE), f32)],
        scratch_shapes=FACTOR_SCRATCH + [pltpu.SemaphoreType.DMA],
        cost_estimate=cost(3e10),
        name="factor_finish",
    )(system)


def update_kernel(where, system, inverse, inverses, rhs, misfit, *refs):
    blocks, out, value, work = refs[:4], refs[4], refs[5], refs[6]
    zid, yid = where[0], where[1]
    n = system.shape[0]
    tiles = n // TILE
    scale = (f32(1024 * 16384) / misfit[0:1, 0:1])
    for a in range(Y):
        for b in range(Z):
            at = pl.multiple_of((yid ^ a) * TILE + (zid ^ b) * 64, 64)
            value[pl.ds(at, 64), :] = blocks[a][b * 64 : (b + 1) * 64, :]
    mean = jnp.sum(value[...], axis=0, keepdims=True) / n
    inv_root = 1.0 / math.sqrt(n - 1)
    work[...] = (value[...] - mean) * inv_root
    for k in range(tiles):
        at = slice(k * TILE, (k + 1) * TILE)
        block = inverse[...] if k == 0 else inverses[(k - 1) * TILE : k * TILE, :]
        work[at, :] = mm(block, work[at, :])
        for i in range(k + 1, tiles):
            down = slice(i * TILE, (i + 1) * TILE)
            work[down, :] = work[down, :] - mm(system[down, at], work[at, :])
    for k in range(tiles - 2, -1, -1):
        at = slice(k * TILE, (k + 1) * TILE)
        rest = slice((k + 1) * TILE, n)
        work[at, :] = work[at, :] - mm(system[at, rest], work[rest, :])
    def combine(z, _):
        at = pl.multiple_of(z * (Y * TILE), Y * TILE)
        total = mm(rhs[pl.ds(at, TILE), :], work[0:TILE, :])
        for y in range(1, Y):
            total = total + mm(rhs[pl.ds(at + y * TILE, TILE), :], work[y * TILE : (y + 1) * TILE, :])
        for y in range(Y):
            out[pl.ds(pl.multiple_of(z * TILE + y * 64, 64), 64), :] = (
                value[pl.ds(pl.multiple_of(y * TILE + z * 64, 64), 64), :]
                + scale * total[y * 64 : (y + 1) * 64, :]
            )
        return 0

    lax.fori_loop(0, Z, combine, 0)


def update(where, system, inverse, inverses, rhs, misfit, blocks):
    n = system.shape[0]
    width = blocks[0].shape[1]
    return pl.pallas_call(
        update_kernel,
        in_specs=[ANY_SMEM] + [ANY_VMEM] * 9,
        out_specs=ANY_VMEM,
        out_shape=jax.ShapeDtypeStruct((n, width), f32),
        scratch_shapes=[pltpu.VMEM((n, width), f32), pltpu.VMEM((n, width), f32)],
        cost_estimate=cost(1e10),
        name="update",
    )(where, system, inverse, inverses, rhs, misfit, *blocks)


def swap(value, axis, size, bit):
    return lax.ppermute(value, axis, [(i, i ^ bit) for i in range(size)])


def body(
    turnover_effect,
    base_rate,
    fast_rate,
    slow_rate,
    init_pools,
    litterfall,
    obs_taps,
    obs_weights,
    observed,
    obs_var,
    obs_noise,
):
    members, cells = turnover_effect.shape
    obs = obs_taps.shape[0]
    zid, yid, core = lax.axis_index("z"), lax.axis_index("y"), lax.axis_index("core")
    where = jnp.stack([zid, yid, core]).astype(jnp.int32)
    observed = observed[None, :]
    obs_var = obs_var[None, :]
    noise = lax.all_gather(obs_noise, "y", axis=0, tiled=True)
    predicted, small = forward(
        turnover_effect, base_rate[None, :], fast_rate[None, :], slow_rate[None, :],
        init_pools, litterfall, obs_taps.T, obs_weights.T, observed, obs_var,
    )
    small = small + sum(swap(small, "y", Y, a) for a in range(1, Y))
    small, predicted = lax.optimization_barrier((small, predicted))
    rows = [predicted] + [swap(predicted, "y", Y, a) for a in range(1, Y)]
    small = small + sum(swap(small, "z", Z, b) for b in range(1, Z))
    small, ready = lax.optimization_barrier((small, predicted))
    columns = [swap(ready, "z", Z, b) for b in range(1, Z)]
    block = gram_block(where, rows, columns, noise, observed, obs_var, small[:, :obs], small[:, obs:])
    shared = jnp.sum(lax.all_to_all(block, ("x", "core"), 0, 0, tiled=False), axis=0)
    piece, right, misfit = shared[:32, :TILE], shared[:32, TILE:], shared[32:, :LANES]
    rhs = lax.all_gather(right, ("z", "y", "x", "core"), axis=0, tiled=True)
    mine = lax.all_to_all(
        jnp.broadcast_to(piece[None], (Z * Y * X, 32, TILE)), ("z", "y", "x"), 0, 0, tiled=True
    ).reshape(Z * Y * X * 32, TILE)
    effect, mine = lax.optimization_barrier((turnover_effect, mine))
    other = swap(mine, "core", 2, 1)
    wide = cells // Z
    strip = [lax.dynamic_slice_in_dim(effect, (zid ^ b) * wide, wide, 1) for b in range(Z)]
    strip = [strip[0]] + [swap(strip[b], "z", Z, b) for b in range(1, Z)]
    system, inverse = factor_begin(where, mine, other, misfit)
    strip, system = lax.optimization_barrier((strip, system))
    narrow = wide // Y
    cut = [
        jnp.concatenate(
            [lax.dynamic_slice_in_dim(part, (yid ^ a) * narrow, narrow, 1) for part in strip], axis=0
        )
        for a in range(Y)
    ]
    cut = [cut[0]] + [swap(cut[a], "y", Y, a) for a in range(1, Y)]
    system, inverses = factor_finish(system)
    changed = update(where, system, inverse, inverses, rhs, misfit, cut)
    return lax.all_to_all(changed, ("z", "y"), 0, 1, tiled=True)


def solution(mesh):
    grid = Mesh(mesh.devices.reshape(Z, Y, X, 2), ("z", "y", "x", "core"))
    mem, cell = ("z", "y"), ("x", "core")
    in_specs = (
        P(mem, cell),
        P(cell),
        P(cell),
        P(cell),
        P(None, cell),
        P(None, cell),
        P(cell, None),
        P(cell, None),
        P(cell),
        P(cell),
        P(mem, cell),
    )
    return jax.shard_map(
        body, mesh=grid, in_specs=in_specs, out_specs=P(mem, cell), check_vma=False
    )
```

```python
import math

import jax
import jax.numpy as jnp
from jax import lax
from jax.experimental import pallas as pl
from jax.experimental.pallas import tpu as pltpu
from jax.sharding import Mesh, PartitionSpec as P

STEPS = 6
BLOCK = 128
TAPS = 4
Z = 4
Y = 4
X = 4
LANES = 128
HALF = 128
TILE = 256
CHUNK = 1024
f32 = jnp.float32

ANY_VMEM = pl.BlockSpec(memory_space=pltpu.VMEM)
ANY_SMEM = pl.BlockSpec(memory_space=pltpu.SMEM)


def mm(left, right):
    return jnp.dot(left, right, precision=lax.Precision.HIGHEST, preferred_element_type=f32)


def mm_last(left, right):
    return lax.dot_general(
        left, right, (((1,), (1,)), ((), ())),
        precision=lax.Precision.HIGHEST, preferred_element_type=f32,
    )


def forward_kernel(
    effect, base, fast, slow, init, fall, taps, weights, observed, var, pred, small, resp, coef
):
    step = pl.program_id(0)
    members, cells = effect.shape
    w = slow[...]
    f = fast[...]
    left_slow = [jnp.zeros_like(w)]
    left_fast = [jnp.zeros_like(w)]
    for _ in range(STEPS):
        left_fast.append(0.7 * f + 0.3 * f * left_slow[-1] + (1.0 - f) * left_fast[-1])
        left_slow.append(w + (1.0 - w) * left_slow[-1])
    share = [0.6 + 0.4 * left_fast[STEPS - 1 - t] for t in range(STEPS)]
    for power in range(STEPS):
        total = share[power] * init[0:1, :]
        for t in range(power + 1, STEPS):
            total = total + share[t] * fall[t - 1 - power : t - power, :]
        coef[power : power + 1, :] = total
    coef[6:7, :] = init[1:2, :] * left_fast[STEPS] + init[2:3, :] * left_slow[STEPS]
    coef[7:8, :] = -base[...]

    def rows(i, _):
        at = pl.ds(pl.multiple_of(i * 8, 8), 8)
        kept = jnp.exp(coef[7:8, :] * jnp.exp(effect[at, :]))
        total = coef[5:6, :]
        for power in range(4, -1, -1):
            total = total * kept + coef[power : power + 1, :]
        resp[at, :] = coef[6:7, :] + (1.0 - kept) * total
        return 0

    lax.fori_loop(0, members // 8, rows, 0)
    position = lax.broadcasted_iota(jnp.int32, (BLOCK, LANES), 0)
    owner = lax.broadcasted_iota(jnp.int32, (members, LANES), 1) // 32
    spread = jnp.zeros((1, LANES), f32)
    for group in range(cells // (4 * BLOCK)):
        lanes = slice(group * LANES, (group + 1) * LANES)
        table = jnp.zeros((BLOCK, LANES), f32)
        for k in range(TAPS):
            table = table + jnp.where(taps[k : k + 1, lanes] == position, weights[k : k + 1, lanes], 0.0)
        stacked = jnp.concatenate(
            [resp[:, (4 * group + b) * BLOCK : (4 * group + b + 1) * BLOCK] for b in range(4)], axis=0
        )
        product = mm(stacked, table)
        out = product[:members]
        for b in range(1, 4):
            out = jnp.where(owner == b, product[b * members : (b + 1) * members], out)
        pred[:, lanes] = out
        small[0:1, pl.ds(pl.multiple_of(step * (cells // 4) + group * LANES, LANES), LANES)] = jnp.sum(
            out, axis=0, keepdims=True
        )
        residual = observed[:, lanes] - out
        spread = spread + jnp.sum(residual * residual, axis=0, keepdims=True) / var[:, lanes]
    spread = jnp.broadcast_to(jnp.sum(spread, axis=1, keepdims=True), (1, LANES))
    tail = pl.ds(small.shape[1] - LANES, LANES)

    @pl.when(step == 0)
    def _():
        small[0:1, tail] = spread

    @pl.when(step > 0)
    def _():
        small[0:1, tail] = small[0:1, tail] + spread


def forward(effect, base, fast, slow, init, fall, taps, weights, observed, var):
    members, cells = effect.shape
    obs = taps.shape[1]
    obs_chunk = CHUNK // 4

    def wide(rows, width):
        return pl.BlockSpec((rows, width), lambda i: (0, i))

    return pl.pallas_call(
        forward_kernel,
        grid=(cells // CHUNK,),
        in_specs=[
            wide(members, CHUNK), wide(1, CHUNK), wide(1, CHUNK), wide(1, CHUNK),
            wide(3, CHUNK), wide(STEPS, CHUNK), wide(TAPS, obs_chunk), wide(TAPS, obs_chunk),
            wide(1, obs_chunk), wide(1, obs_chunk),
        ],
        out_specs=[wide(members, obs_chunk), pl.BlockSpec((1, obs + LANES), lambda i: (0, 0))],
        out_shape=[
            jax.ShapeDtypeStruct((members, obs), f32),
            jax.ShapeDtypeStruct((1, obs + LANES), f32),
        ],
        scratch_shapes=[pltpu.VMEM((members, CHUNK), f32), pltpu.VMEM((8, CHUNK), f32)],
        name="forward",
    )(effect, base, fast, slow, init, fall, taps, weights, observed, var)


def gram_kernel(
    where, p1, p2, p3, e0, e1, e2, e3, noise, observed, var, out, left, right, total
):
    step = pl.program_id(0)
    zid, yid = where[0], where[1]
    members = p1.shape[0]
    member_count = members * Z * Y
    inv_root = 1.0 / math.sqrt(member_count - 1)
    tails = e0[members:, :] + e1[members:, :] + e2[members:, :] + e3[members:, :]
    mean = tails[0:1, :] / member_count
    inv_var = 1.0 / var[...]
    root_var = jnp.sqrt(var[...])
    for a, p in enumerate((e0, p1, p2, p3)):
        at = pl.multiple_of((yid ^ a) * members, members)
        left[pl.ds(at, members), :] = (p[0:members, :] - mean) * inv_root
        left[pl.ds(at + Y * members, members), :] = (
            observed[...] + root_var * noise[pl.ds(at, members), :] - p[0:members, :]
        )
    for b, e in enumerate((e0, e1, e2, e3)):
        at = pl.multiple_of((zid ^ b) * members, members)
        right[pl.ds(at, members), :] = (e[0:members, :] - mean) * inv_root * inv_var

    product = mm_last(left[...], right[...])

    @pl.when(step == 0)
    def _():
        total[...] = product

    @pl.when(step > 0)
    def _():
        total[...] = total[...] + product

    @pl.when(step == pl.num_programs(0) - 1)
    def _():
        for c in range(8):
            out[c, 0:32, 0:TILE] = total[c * 32 : c * 32 + 32, :]
            out[c, 0:32, TILE : 2 * TILE] = total[TILE + c * 32 : TILE + c * 32 + 32, :]
            out[c, 32:40, :] = jnp.broadcast_to(tails[1:2, 0:1], (8, 2 * TILE))


def gram_block(where, rows, columns, noise, observed, var):
    members, obs = rows[0].shape
    width = 512

    def chunk(n):
        return pl.BlockSpec((n, width), lambda i: (0, i))

    return pl.pallas_call(
        gram_kernel,
        grid=(obs // width,),
        in_specs=[ANY_SMEM] + [chunk(members)] * 3 + [chunk(members + 8)] * 4
        + [chunk(members * Y)] + [chunk(1)] * 2,
        out_specs=pl.BlockSpec((8, 40, 2 * TILE), lambda i: (0, 0, 0)),
        out_shape=jax.ShapeDtypeStruct((8, 40, 2 * TILE), f32),
        scratch_shapes=[
            pltpu.VMEM((2 * TILE, width), f32),
            pltpu.VMEM((TILE, width), f32),
            pltpu.VMEM((2 * TILE, TILE), f32),
        ],
        cost_estimate=cost(8e9),
        name="gram",
    )(where, *rows, *columns, noise, observed, var)


def cost(flops):
    return pl.CostEstimate(flops=int(flops), bytes_accessed=int(1e7), transcendentals=0)


def invert_block(rows):
    width = HALF
    count = width // 8
    rows = list(rows)
    lane = lax.broadcasted_iota(jnp.int32, (8, width), 1)
    sub = lax.broadcasted_iota(jnp.int32, (8, width), 0)

    def row(value, r):
        return jnp.broadcast_to(value[r : r + 1, :], (8, width))

    for block in range(count):
        low = 8 * block
        panel = rows[block]
        inside = (lane >= low) & (lane < low + 8)
        early = {
            i: [jnp.broadcast_to(rows[i][:, low + p : low + p + 1], (8, width)) for p in range(8)]
            for i in range(block + 1, min(block + 3, count))
        }
        pivots = [jnp.broadcast_to(panel[:, low + p : low + p + 1], (8, width)) for p in range(8)]
        for r in range(8):
            heads = [row(pivots[p], r) for p in range(8)]
            inverse = 1.0 / heads[r]
            here = sub == r
            column = jnp.where(here, 0.0, pivots[r])
            for p in range(8):
                if p != r:
                    scaled = heads[p] * inverse
                    pivots[p] = jnp.where(here, scaled, pivots[p] - column * scaled)
            pivots[r] = jnp.where(here, inverse, -column * inverse)
        panel = jnp.where(inside, jnp.where(lane - low == sub, 1.0, 0.0), panel)
        terms = [pivots[p] * row(panel, p) for p in range(8)]
        while len(terms) > 1:
            terms = [terms[i] + terms[i + 1] for i in range(0, len(terms), 2)]
        solved = terms[0]
        heads = [row(solved, p) for p in range(8)]
        zero = jnp.zeros((8, width), f32)
        masked = [
            zero if block <= i <= block + 2 else jnp.where(inside, rows[i], 0.0) for i in range(count)
        ]
        spread = [solved if i == block else zero for i in range(count)]
        product = mm(jnp.concatenate(masked, axis=0), jnp.concatenate(spread, axis=0))
        for i in range(count):
            if i == block:
                rows[i] = solved
            elif i in early:
                terms = [early[i][p] * heads[p] for p in range(8)]
                while len(terms) > 1:
                    terms = [terms[j] + terms[j + 1] for j in range(0, len(terms), 2)]
                rows[i] = jnp.where(inside, 0.0, rows[i]) - terms[0]
            else:
                rows[i] = jnp.where(inside, 0.0, rows[i]) - product[8 * i : 8 * i + 8]
    return rows


def begin_kernel(where, mine, other, misfit, system, inverses, last, halves, ahead, behind):
    core = where[2]
    scale = f32(1024 * 16384) / misfit[0:1, 0:1]
    for z in range(Z):
        for y in range(Y):
            for x in range(X):
                piece = slice(((z * Y + y) * X + x) * 32, ((z * Y + y) * X + x) * 32 + 32)
                at = x * TILE + z * 64
                lanes = slice(y * TILE, (y + 1) * TILE)
                system[pl.ds(pl.multiple_of(at + core * 32, 32), 32), lanes] = mine[piece, :] * scale
                system[pl.ds(pl.multiple_of(at + 32 - core * 32, 32), 32), lanes] = other[piece, :] * scale
    eye = jnp.where(
        lax.broadcasted_iota(jnp.int32, (HALF, HALF), 0) == lax.broadcasted_iota(jnp.int32, (HALF, HALF), 1),
        1.0, 0.0,
    )
    for d in range(system.shape[0] // HALF):
        at = slice(d * HALF, (d + 1) * HALF)
        system[at, at] = system[at, at] + eye
    eliminate(system, inverses, 0, last, halves, ahead, behind)


def finish_kernel(before, earlier, system, inverses, last, halves, ahead, behind, arrived):
    copy = pltpu.make_async_copy(before, system, arrived)
    copy.start()
    last[...] = earlier[TILE:, :]
    copy.wait()
    eliminate(system, inverses, 2, last, halves, ahead, behind)


def eliminate(system, inverses, start, last, halves, ahead, behind):
    tiles = system.shape[0] // TILE

    def spread(k):
        top = pl.multiple_of(k * TILE, TILE)

        def across(t, _):
            lanes = pl.ds(pl.multiple_of(t * TILE, TILE), TILE)
            system[pl.ds(top, TILE), lanes] = mm(last[...], system[pl.ds(top, TILE), lanes])

            def down(i, _):
                at = pl.ds(pl.multiple_of(i * TILE, TILE), TILE)
                system[at, lanes] = system[at, lanes] - mm(
                    system[at, pl.ds(top, TILE)], system[pl.ds(top, TILE), lanes]
                )
                return 0

            lax.fori_loop(k + 1, tiles, down, 0)
            return 0

        lax.fori_loop(k + 1, tiles, across, 0)

    def stage(k, _):
        @pl.when(k > 0)
        def _():
            spread(k - 1)

        top = pl.multiple_of(k * TILE, TILE)
        low = pl.multiple_of(k * TILE + HALF, HALF)

        def half(h, _):
            at = pl.multiple_of(top + h * HALF, HALF)
            block = [system[pl.ds(at + 8 * j, 8), pl.ds(at, HALF)] for j in range(HALF // 8)]
            block = invert_block(block)
            for j in range(HALF // 8):
                halves[pl.ds(pl.multiple_of(h * HALF + 8 * j, 8), 8), :] = block[j]

            @pl.when(h == 0)
            def _():
                first = halves[0:HALF, :]
                upper = system[pl.ds(top, HALF), pl.ds(low, HALF)]
                ahead[...] = mm(first, upper)
                behind[...] = mm(system[pl.ds(low, HALF), pl.ds(top, HALF)], first)
                system[pl.ds(low, HALF), pl.ds(low, HALF)] = (
                    system[pl.ds(low, HALF), pl.ds(low, HALF)] - mm(behind[...], upper)
                )

            return 0

        lax.fori_loop(0, 2, half, 0)
        second = halves[HALF:, :]
        corner = mm(second, behind[...])
        last[0:HALF, 0:HALF] = halves[0:HALF, :] + mm(ahead[...], corner)
        last[0:HALF, HALF:] = -mm(ahead[...], second)
        last[HALF:, 0:HALF] = -corner
        last[HALF:, HALF:] = second
        inverses[pl.ds(pl.multiple_of((k - start) * TILE, TILE), TILE), :] = last[...]
        return 0

    lax.fori_loop(start, start + 2, stage, 0)


FACTOR_SCRATCH = [
    pltpu.VMEM((TILE, TILE), f32), pltpu.VMEM((TILE, HALF), f32), pltpu.VMEM((HALF, HALF), f32),
    pltpu.VMEM((HALF, HALF), f32),
]


def factor_begin(where, mine, other, misfit):
    n = TILE * Y
    return pl.pallas_call(
        begin_kernel,
        in_specs=[ANY_SMEM, ANY_VMEM, ANY_VMEM, ANY_VMEM],
        out_specs=[ANY_VMEM, ANY_VMEM],
        out_shape=[jax.ShapeDtypeStruct((n, n), f32), jax.ShapeDtypeStruct((2 * TILE, TILE), f32)],
        scratch_shapes=FACTOR_SCRATCH,
        cost_estimate=cost(2e10),
        name="factor_begin",
    )(where, mine, other, misfit)


def factor_finish(system, earlier):
    n = system.shape[0]
    return pl.pallas_call(
        finish_kernel,
        in_specs=[pl.BlockSpec(memory_space=pl.ANY), ANY_VMEM],
        out_specs=[ANY_VMEM, ANY_VMEM],
        out_shape=[jax.ShapeDtypeStruct((n, n), f32), jax.ShapeDtypeStruct((2 * TILE, TILE), f32)],
        scratch_shapes=FACTOR_SCRATCH + [pltpu.SemaphoreType.DMA],
        cost_estimate=cost(2e10),
        name="factor_finish",
    )(system, earlier)


def solve_kernel(where, system, earlier, later, b0, b1, b2, b3, work):
    zid, yid = where[0], where[1]
    n = system.shape[0]
    tiles = n // TILE
    for a, block in enumerate((b0, b1, b2, b3)):
        for b in range(Z):
            at = pl.multiple_of((yid ^ a) * TILE + (zid ^ b) * 64, 64)
            work[pl.ds(at, 64), :] = block[b * 64 : (b + 1) * 64, :]
    mean = jnp.sum(work[...], axis=0, keepdims=True) / n
    inv_root = 1.0 / math.sqrt(n - 1)
    work[...] = (work[...] - mean) * inv_root
    for k in range(tiles):
        at = slice(k * TILE, (k + 1) * TILE)
        source = earlier if k < 2 else later
        work[at, :] = mm(source[(k % 2) * TILE : (k % 2 + 1) * TILE, :], work[at, :])
        for i in range(k + 1, tiles):
            down = slice(i * TILE, (i + 1) * TILE)
            work[down, :] = work[down, :] - mm(system[down, at], work[at, :])
    for k in range(tiles - 2, -1, -1):
        at = slice(k * TILE, (k + 1) * TILE)
        rest = slice((k + 1) * TILE, n)
        work[at, :] = work[at, :] - mm(system[at, rest], work[rest, :])


def solve(where, system, earlier, later, blocks):
    return pl.pallas_call(
        solve_kernel,
        in_specs=[ANY_SMEM] + [ANY_VMEM] * 7,
        out_specs=ANY_VMEM,
        out_shape=jax.ShapeDtypeStruct((system.shape[0], blocks[0].shape[1]), f32),
        cost_estimate=cost(5e9),
        name="solve",
    )(where, system, earlier, later, *blocks)


def combine_kernel(rhs, work, misfit, out):
    scale = f32(1024 * 16384) / misfit[0:1, 0:1]
    total = mm(rhs[0:TILE, :], work[0:TILE, :])
    for y in range(1, Y):
        total = total + mm(rhs[y * TILE : (y + 1) * TILE, :], work[y * TILE : (y + 1) * TILE, :])
    out[...] = scale * total


def combine(rhs, work, misfit):
    n, width = work.shape
    return pl.pallas_call(
        combine_kernel,
        grid=(Z,),
        in_specs=[
            pl.BlockSpec((Y * TILE, TILE), lambda z: (z, 0)), ANY_VMEM, ANY_VMEM,
        ],
        out_specs=pl.BlockSpec((TILE, width), lambda z: (z, 0)),
        out_shape=jax.ShapeDtypeStruct((n, width), f32),
        cost_estimate=cost(6e9),
        name="combine",
    )(rhs, work, misfit)


def swap(value, axis, size, bit):
    return lax.ppermute(value, axis, [(i, i ^ bit) for i in range(size)])


def body(
    turnover_effect,
    base_rate,
    fast_rate,
    slow_rate,
    init_pools,
    litterfall,
    obs_taps,
    obs_weights,
    observed,
    obs_var,
    obs_noise,
):
    members, cells = turnover_effect.shape
    obs = obs_taps.shape[0]
    zid, yid, core = lax.axis_index("z"), lax.axis_index("y"), lax.axis_index("core")
    where = jnp.stack([zid, yid, core]).astype(jnp.int32)
    observed = observed[None, :]
    obs_var = obs_var[None, :]
    noise = lax.all_gather(obs_noise, "y", axis=0, tiled=True)
    predicted, small = forward(
        turnover_effect, base_rate[None, :], fast_rate[None, :], slow_rate[None, :],
        init_pools, litterfall, obs_taps.T, obs_weights.T, observed, obs_var,
    )
    small = small + sum(swap(small, "y", Y, a) for a in range(1, Y))
    small, predicted = lax.optimization_barrier((small, predicted))
    rows = [swap(predicted, "y", Y, a) for a in range(1, Y)]
    extended = jnp.concatenate(
        [predicted, small[:, :obs], jnp.broadcast_to(small[:, obs : obs + 1], (7, obs))], axis=0
    )
    columns = [extended] + [swap(extended, "z", Z, b) for b in range(1, Z)]
    block = gram_block(where, rows, columns, noise, observed, obs_var)
    shared = jnp.sum(lax.all_to_all(block, ("x", "core"), 0, 0, tiled=False), axis=0)
    piece, right, misfit = shared[:32, :TILE], shared[:32, TILE:], shared[32:, :LANES]
    rhs = lax.all_gather(right, ("z", "y", "x", "core"), axis=0, tiled=True)
    mine = lax.all_to_all(
        jnp.broadcast_to(piece[None], (Z * Y * X, 32, TILE)), ("z", "y", "x"), 0, 0, tiled=True
    ).reshape(Z * Y * X * 32, TILE)
    effect, mine = lax.optimization_barrier((turnover_effect, mine))
    other = swap(mine, "core", 2, 1)
    wide = cells // Z
    strip = [lax.dynamic_slice_in_dim(effect, (zid ^ b) * wide, wide, 1) for b in range(Z)]
    strip = [strip[0]] + [swap(strip[b], "z", Z, b) for b in range(1, Z)]
    system, inverse = factor_begin(where, mine, other, misfit)
    strip, system = lax.optimization_barrier((strip, system))
    narrow = wide // Y
    cut = [
        jnp.concatenate(
            [lax.dynamic_slice_in_dim(part, (yid ^ a) * narrow, narrow, 1) for part in strip], axis=0
        )
        for a in range(Y)
    ]
    cut = [cut[0]] + [swap(cut[a], "y", Y, a) for a in range(1, Y)]
    system, later = factor_finish(system, inverse)
    work = solve(where, system, inverse, later, cut)
    change = combine(rhs, work, misfit)
    return turnover_effect + lax.all_to_all(change, ("z", "y"), 0, 1, tiled=True)


def solution(mesh):
    grid = Mesh(mesh.devices.reshape(Z, Y, X, 2), ("z", "y", "x", "core"))
    mem, cell = ("z", "y"), ("x", "core")
    in_specs = (
        P(mem, cell),
        P(cell),
        P(cell),
        P(cell),
        P(None, cell),
        P(None, cell),
        P(cell, None),
        P(cell, None),
        P(cell),
        P(cell),
        P(mem, cell),
    )
    return jax.shard_map(
        body, mesh=grid, in_specs=in_specs, out_specs=P(mem, cell), check_vma=False
    )
```

```python
import math

import jax
import jax.numpy as jnp
from jax import lax
from jax.experimental import pallas as pl
from jax.experimental.pallas import tpu as pltpu
from jax.sharding import Mesh, PartitionSpec as P

STEPS = 6
BLOCK = 128
TAPS = 4
Z = 4
Y = 4
X = 4
LANES = 128
HALF = 128
TILE = 256
CHUNK = 1024
f32 = jnp.float32

ANY_VMEM = pl.BlockSpec(memory_space=pltpu.VMEM)
ANY_SMEM = pl.BlockSpec(memory_space=pltpu.SMEM)


def mm(left, right):
    return jnp.dot(left, right, precision=lax.Precision.HIGHEST, preferred_element_type=f32)


def mm_last(left, right):
    return lax.dot_general(
        left, right, (((1,), (1,)), ((), ())),
        precision=lax.Precision.HIGHEST, preferred_element_type=f32,
    )


def forward_kernel(
    effect, base, fast, slow, init, fall, taps, weights, observed, var, pred, small, resp, coef
):
    step = pl.program_id(0)
    members, cells = effect.shape
    w = slow[...]
    f = fast[...]
    left_slow = [jnp.zeros_like(w)]
    left_fast = [jnp.zeros_like(w)]
    for _ in range(STEPS):
        left_fast.append(0.7 * f + 0.3 * f * left_slow[-1] + (1.0 - f) * left_fast[-1])
        left_slow.append(w + (1.0 - w) * left_slow[-1])
    share = [0.6 + 0.4 * left_fast[STEPS - 1 - t] for t in range(STEPS)]
    for power in range(STEPS):
        total = share[power] * init[0:1, :]
        for t in range(power + 1, STEPS):
            total = total + share[t] * fall[t - 1 - power : t - power, :]
        coef[power : power + 1, :] = total
    coef[6:7, :] = init[1:2, :] * left_fast[STEPS] + init[2:3, :] * left_slow[STEPS]
    coef[7:8, :] = -base[...]

    def rows(i, _):
        at = pl.ds(pl.multiple_of(i * 8, 8), 8)
        kept = jnp.exp(coef[7:8, :] * jnp.exp(effect[at, :]))
        total = coef[5:6, :]
        for power in range(4, -1, -1):
            total = total * kept + coef[power : power + 1, :]
        resp[at, :] = coef[6:7, :] + (1.0 - kept) * total
        return 0

    lax.fori_loop(0, members // 8, rows, 0)
    position = lax.broadcasted_iota(jnp.int32, (BLOCK, LANES), 0)
    owner = lax.broadcasted_iota(jnp.int32, (members, LANES), 1) // 32
    spread = jnp.zeros((1, LANES), f32)
    for group in range(cells // (4 * BLOCK)):
        lanes = slice(group * LANES, (group + 1) * LANES)
        table = jnp.zeros((BLOCK, LANES), f32)
        for k in range(TAPS):
            table = table + jnp.where(taps[k : k + 1, lanes] == position, weights[k : k + 1, lanes], 0.0)
        stacked = jnp.concatenate(
            [resp[:, (4 * group + b) * BLOCK : (4 * group + b + 1) * BLOCK] for b in range(4)], axis=0
        )
        product = mm(stacked, table)
        out = product[:members]
        for b in range(1, 4):
            out = jnp.where(owner == b, product[b * members : (b + 1) * members], out)
        pred[:, lanes] = out
        small[0:1, pl.ds(pl.multiple_of(step * (cells // 4) + group * LANES, LANES), LANES)] = jnp.sum(
            out, axis=0, keepdims=True
        )
        residual = observed[:, lanes] - out
        spread = spread + jnp.sum(residual * residual, axis=0, keepdims=True) / var[:, lanes]
    spread = jnp.broadcast_to(jnp.sum(spread, axis=1, keepdims=True), (1, LANES))
    tail = pl.ds(small.shape[1] - LANES, LANES)

    @pl.when(step == 0)
    def _():
        small[0:1, tail] = spread

    @pl.when(step > 0)
    def _():
        small[0:1, tail] = small[0:1, tail] + spread


def forward(effect, base, fast, slow, init, fall, taps, weights, observed, var):
    members, cells = effect.shape
    obs = taps.shape[1]
    obs_chunk = CHUNK // 4

    def wide(rows, width):
        return pl.BlockSpec((rows, width), lambda i: (0, i))

    return pl.pallas_call(
        forward_kernel,
        grid=(cells // CHUNK,),
        in_specs=[
            wide(members, CHUNK), wide(1, CHUNK), wide(1, CHUNK), wide(1, CHUNK),
            wide(3, CHUNK), wide(STEPS, CHUNK), wide(TAPS, obs_chunk), wide(TAPS, obs_chunk),
            wide(1, obs_chunk), wide(1, obs_chunk),
        ],
        out_specs=[wide(members, obs_chunk), pl.BlockSpec((1, obs + LANES), lambda i: (0, 0))],
        out_shape=[
            jax.ShapeDtypeStruct((members, obs), f32),
            jax.ShapeDtypeStruct((1, obs + LANES), f32),
        ],
        scratch_shapes=[pltpu.VMEM((members, CHUNK), f32), pltpu.VMEM((8, CHUNK), f32)],
        name="forward",
    )(effect, base, fast, slow, init, fall, taps, weights, observed, var)


def gram_kernel(
    where, p1, p2, p3, e0, e1, e2, e3, noise, observed, var, keep, send, left, right, total
):
    step = pl.program_id(0)
    zid, yid = where[0], where[1]
    members = p1.shape[0]
    member_count = members * Z * Y
    inv_root = 1.0 / math.sqrt(member_count - 1)
    tails = e0[members:, :] + e1[members:, :] + e2[members:, :] + e3[members:, :]
    mean = tails[0:1, :] / member_count
    inv_var = 1.0 / var[...]
    root_var = jnp.sqrt(var[...])
    for a, e in enumerate((e0, e1, e2, e3)):
        at = pl.multiple_of((yid ^ a) * members, members)
        left[pl.ds(at, members), :] = (e[0:members, :] - mean) * inv_root
        left[pl.ds(at + Y * members, members), :] = (
            observed[...] + root_var * noise[pl.ds(at, members), :] - e[0:members, :]
        )
    for b, p in enumerate((e0, p1, p2, p3)):
        at = pl.multiple_of((zid ^ b) * members, members)
        right[pl.ds(at, members), :] = (p[0:members, :] - mean) * inv_root * inv_var

    product = mm_last(left[...], right[...])

    @pl.when(step == 0)
    def _():
        total[...] = product

    @pl.when(step > 0)
    def _():
        total[...] = total[...] + product

    @pl.when(step == pl.num_programs(0) - 1)
    def _():
        core, xid = where[2], where[3]
        for part, offset in ((keep, core * 32), (send, 32 - core * 32)):
            for a in range(X):
                at = pl.multiple_of((xid ^ a) * 64 + offset, 32)
                part[a, 0:32, 0:TILE] = total[pl.ds(at, 32), :]
                part[a, 0:32, TILE : 2 * TILE] = total[pl.ds(at + TILE, 32), :]
                part[a, 32:40, :] = jnp.broadcast_to(tails[1:2, 0:1], (8, 2 * TILE))


def gram_block(where, rows, columns, noise, observed, var):
    members, obs = columns[0].shape
    width = 512

    def chunk(n):
        return pl.BlockSpec((n, width), lambda i: (0, i))

    return pl.pallas_call(
        gram_kernel,
        grid=(obs // width,),
        in_specs=[ANY_SMEM] + [chunk(members)] * 3 + [chunk(members + 8)] * 4
        + [chunk(members * Y)] + [chunk(1)] * 2,
        out_specs=[pl.BlockSpec((X, 40, 2 * TILE), lambda i: (0, 0, 0))] * 2,
        out_shape=[jax.ShapeDtypeStruct((X, 40, 2 * TILE), f32)] * 2,
        scratch_shapes=[
            pltpu.VMEM((2 * TILE, width), f32),
            pltpu.VMEM((TILE, width), f32),
            pltpu.VMEM((2 * TILE, TILE), f32),
        ],
        cost_estimate=cost(8e9),
        name="gram",
    )(where, *columns, *rows, noise, observed, var)


def cost(flops):
    return pl.CostEstimate(flops=int(flops), bytes_accessed=int(1e7), transcendentals=0)


def invert_block(rows):
    width = HALF
    count = width // 8
    rows = list(rows)
    lane = lax.broadcasted_iota(jnp.int32, (8, width), 1)
    sub = lax.broadcasted_iota(jnp.int32, (8, width), 0)

    def row(value, r):
        return jnp.broadcast_to(value[r : r + 1, :], (8, width))

    for block in range(count):
        low = 8 * block
        panel = rows[block]
        inside = (lane >= low) & (lane < low + 8)
        early = {
            i: [jnp.broadcast_to(rows[i][:, low + p : low + p + 1], (8, width)) for p in range(8)]
            for i in range(block + 1, min(block + 3, count))
        }
        pivots = [jnp.broadcast_to(panel[:, low + p : low + p + 1], (8, width)) for p in range(8)]
        for r in range(8):
            heads = [row(pivots[p], r) for p in range(8)]
            inverse = 1.0 / heads[r]
            here = sub == r
            column = jnp.where(here, 0.0, pivots[r])
            for p in range(8):
                if p != r:
                    scaled = heads[p] * inverse
                    pivots[p] = jnp.where(here, scaled, pivots[p] - column * scaled)
            pivots[r] = jnp.where(here, inverse, -column * inverse)
        panel = jnp.where(inside, jnp.where(lane - low == sub, 1.0, 0.0), panel)
        terms = [pivots[p] * row(panel, p) for p in range(8)]
        while len(terms) > 1:
            terms = [terms[i] + terms[i + 1] for i in range(0, len(terms), 2)]
        solved = terms[0]
        heads = [row(solved, p) for p in range(8)]
        zero = jnp.zeros((8, width), f32)
        masked = [
            zero if block <= i <= block + 2 else jnp.where(inside, rows[i], 0.0) for i in range(count)
        ]
        spread = [solved if i == block else zero for i in range(count)]
        product = mm(jnp.concatenate(masked, axis=0), jnp.concatenate(spread, axis=0))
        for i in range(count):
            if i == block:
                rows[i] = solved
            elif i in early:
                terms = [early[i][p] * heads[p] for p in range(8)]
                while len(terms) > 1:
                    terms = [terms[j] + terms[j + 1] for j in range(0, len(terms), 2)]
                rows[i] = jnp.where(inside, 0.0, rows[i]) - terms[0]
            else:
                rows[i] = jnp.where(inside, 0.0, rows[i]) - product[8 * i : 8 * i + 8]
    return rows


def begin_kernel(where, mine, other, misfit, system, inverses, last, halves, ahead, behind):
    core = where[2]
    scale = f32(1024 * 16384) / misfit[0:1, 0:1]
    for z in range(Z):
        for y in range(Y):
            for x in range(X):
                piece = slice(((z * Y + y) * X + x) * 32, ((z * Y + y) * X + x) * 32 + 32)
                at = x * TILE + z * 64
                lanes = slice(y * TILE, (y + 1) * TILE)
                system[pl.ds(pl.multiple_of(at + core * 32, 32), 32), lanes] = mine[piece, :] * scale
                system[pl.ds(pl.multiple_of(at + 32 - core * 32, 32), 32), lanes] = other[piece, :] * scale
    eye = jnp.where(
        lax.broadcasted_iota(jnp.int32, (HALF, HALF), 0) == lax.broadcasted_iota(jnp.int32, (HALF, HALF), 1),
        1.0, 0.0,
    )
    for d in range(system.shape[0] // HALF):
        at = slice(d * HALF, (d + 1) * HALF)
        system[at, at] = system[at, at] + eye
    eliminate(system, inverses, 0, last, halves, ahead, behind)


def finish_kernel(before, earlier, system, inverses, last, halves, ahead, behind, arrived):
    copy = pltpu.make_async_copy(before, system, arrived)
    copy.start()
    last[...] = earlier[TILE:, :]
    copy.wait()
    eliminate(system, inverses, 2, last, halves, ahead, behind)


def eliminate(system, inverses, start, last, halves, ahead, behind):
    tiles = system.shape[0] // TILE

    def spread(k):
        top = pl.multiple_of(k * TILE, TILE)

        def across(t, _):
            lanes = pl.ds(pl.multiple_of(t * TILE, TILE), TILE)
            system[pl.ds(top, TILE), lanes] = mm(last[...], system[pl.ds(top, TILE), lanes])

            def down(i, _):
                at = pl.ds(pl.multiple_of(i * TILE, TILE), TILE)
                system[at, lanes] = system[at, lanes] - mm(
                    system[at, pl.ds(top, TILE)], system[pl.ds(top, TILE), lanes]
                )
                return 0

            lax.fori_loop(k + 1, tiles, down, 0)
            return 0

        lax.fori_loop(k + 1, tiles, across, 0)

    def stage(k, _):
        @pl.when(k > 0)
        def _():
            spread(k - 1)

        top = pl.multiple_of(k * TILE, TILE)
        low = pl.multiple_of(k * TILE + HALF, HALF)

        def half(h, _):
            at = pl.multiple_of(top + h * HALF, HALF)
            block = [system[pl.ds(at + 8 * j, 8), pl.ds(at, HALF)] for j in range(HALF // 8)]
            block = invert_block(block)
            for j in range(HALF // 8):
                halves[pl.ds(pl.multiple_of(h * HALF + 8 * j, 8), 8), :] = block[j]

            @pl.when(h == 0)
            def _():
                first = halves[0:HALF, :]
                upper = system[pl.ds(top, HALF), pl.ds(low, HALF)]
                ahead[...] = mm(first, upper)
                behind[...] = mm(system[pl.ds(low, HALF), pl.ds(top, HALF)], first)
                system[pl.ds(low, HALF), pl.ds(low, HALF)] = (
                    system[pl.ds(low, HALF), pl.ds(low, HALF)] - mm(behind[...], upper)
                )

            return 0

        lax.fori_loop(0, 2, half, 0)
        second = halves[HALF:, :]
        corner = mm(second, behind[...])
        last[0:HALF, 0:HALF] = halves[0:HALF, :] + mm(ahead[...], corner)
        last[0:HALF, HALF:] = -mm(ahead[...], second)
        last[HALF:, 0:HALF] = -corner
        last[HALF:, HALF:] = second
        inverses[pl.ds(pl.multiple_of((k - start) * TILE, TILE), TILE), :] = last[...]
        return 0

    lax.fori_loop(start, start + 2, stage, 0)


FACTOR_SCRATCH = [
    pltpu.VMEM((TILE, TILE), f32), pltpu.VMEM((TILE, HALF), f32), pltpu.VMEM((HALF, HALF), f32),
    pltpu.VMEM((HALF, HALF), f32),
]


def factor_begin(where, mine, other, misfit):
    n = TILE * Y
    return pl.pallas_call(
        begin_kernel,
        in_specs=[ANY_SMEM, ANY_VMEM, ANY_VMEM, ANY_VMEM],
        out_specs=[ANY_VMEM, ANY_VMEM],
        out_shape=[jax.ShapeDtypeStruct((n, n), f32), jax.ShapeDtypeStruct((2 * TILE, TILE), f32)],
        scratch_shapes=FACTOR_SCRATCH,
        cost_estimate=cost(2e10),
        name="factor_begin",
    )(where, mine, other, misfit)


def factor_finish(system, earlier):
    n = system.shape[0]
    return pl.pallas_call(
        finish_kernel,
        in_specs=[pl.BlockSpec(memory_space=pl.ANY), ANY_VMEM],
        out_specs=[ANY_VMEM, ANY_VMEM],
        out_shape=[jax.ShapeDtypeStruct((n, n), f32), jax.ShapeDtypeStruct((2 * TILE, TILE), f32)],
        scratch_shapes=FACTOR_SCRATCH + [pltpu.SemaphoreType.DMA],
        cost_estimate=cost(2e10),
        name="factor_finish",
    )(system, earlier)


def solve_kernel(where, system, earlier, later, b0, b1, b2, b3, work):
    zid, yid = where[0], where[1]
    n = system.shape[0]
    tiles = n // TILE
    for a, block in enumerate((b0, b1, b2, b3)):
        for b in range(Z):
            at = pl.multiple_of((yid ^ a) * TILE + (zid ^ b) * 64, 64)
            work[pl.ds(at, 64), :] = block[b * 64 : (b + 1) * 64, :]
    mean = jnp.sum(work[...], axis=0, keepdims=True) / n
    inv_root = 1.0 / math.sqrt(n - 1)
    work[...] = (work[...] - mean) * inv_root
    for k in range(tiles):
        at = slice(k * TILE, (k + 1) * TILE)
        source = earlier if k < 2 else later
        work[at, :] = mm(source[(k % 2) * TILE : (k % 2 + 1) * TILE, :], work[at, :])
        for i in range(k + 1, tiles):
            down = slice(i * TILE, (i + 1) * TILE)
            work[down, :] = work[down, :] - mm(system[down, at], work[at, :])
    for k in range(tiles - 2, -1, -1):
        at = slice(k * TILE, (k + 1) * TILE)
        rest = slice((k + 1) * TILE, n)
        work[at, :] = work[at, :] - mm(system[at, rest], work[rest, :])


def solve(where, system, earlier, later, blocks):
    return pl.pallas_call(
        solve_kernel,
        in_specs=[ANY_SMEM] + [ANY_VMEM] * 7,
        out_specs=ANY_VMEM,
        out_shape=jax.ShapeDtypeStruct((system.shape[0], blocks[0].shape[1]), f32),
        cost_estimate=cost(5e9),
        name="solve",
    )(where, system, earlier, later, *blocks)


def combine_kernel(rhs, work, misfit, out):
    scale = f32(1024 * 16384) / misfit[0:1, 0:1]
    total = mm(rhs[0:TILE, :], work[0:TILE, :])
    for y in range(1, Y):
        total = total + mm(rhs[y * TILE : (y + 1) * TILE, :], work[y * TILE : (y + 1) * TILE, :])
    out[...] = scale * total


def combine(rhs, work, misfit):
    n, width = work.shape
    return pl.pallas_call(
        combine_kernel,
        grid=(Z,),
        in_specs=[
            pl.BlockSpec((Y * TILE, TILE), lambda z: (z, 0)), ANY_VMEM, ANY_VMEM,
        ],
        out_specs=pl.BlockSpec((TILE, width), lambda z: (z, 0)),
        out_shape=jax.ShapeDtypeStruct((n, width), f32),
        cost_estimate=cost(6e9),
        name="combine",
    )(rhs, work, misfit)


def swap(value, axis, size, bit):
    return lax.ppermute(value, axis, [(i, i ^ bit) for i in range(size)])


def body(
    turnover_effect,
    base_rate,
    fast_rate,
    slow_rate,
    init_pools,
    litterfall,
    obs_taps,
    obs_weights,
    observed,
    obs_var,
    obs_noise,
):
    members, cells = turnover_effect.shape
    obs = obs_taps.shape[0]
    zid, yid, core = lax.axis_index("z"), lax.axis_index("y"), lax.axis_index("core")
    where = jnp.stack([zid, yid, core, lax.axis_index("x")]).astype(jnp.int32)
    observed = observed[None, :]
    obs_var = obs_var[None, :]
    noise = lax.all_gather(obs_noise, "y", axis=0, tiled=True)
    predicted, small = forward(
        turnover_effect, base_rate[None, :], fast_rate[None, :], slow_rate[None, :],
        init_pools, litterfall, obs_taps.T, obs_weights.T, observed, obs_var,
    )
    small = small + sum(swap(small, "z", Z, b) for b in range(1, Z))
    small, predicted = lax.optimization_barrier((small, predicted))
    columns = [swap(predicted, "z", Z, b) for b in range(1, Z)]
    extended = jnp.concatenate(
        [predicted, small[:, :obs], jnp.broadcast_to(small[:, obs : obs + 1], (7, obs))], axis=0
    )
    rows = [extended] + [swap(extended, "y", Y, a) for a in range(1, Y)]
    keep, send = gram_block(where, rows, columns, noise, observed, obs_var)
    part = keep + swap(send, "core", 2, 1)
    shared = part[0] + sum(swap(part[a], "x", X, a) for a in range(1, X))
    piece, right, misfit = shared[:32, :TILE], shared[:32, TILE:], shared[32:, :LANES]
    rhs = lax.all_gather(right, ("z", "y", "x", "core"), axis=0, tiled=True)
    mine = lax.all_to_all(
        jnp.broadcast_to(piece[None], (Z * Y * X, 32, TILE)), ("z", "y", "x"), 0, 0, tiled=True
    ).reshape(Z * Y * X * 32, TILE)
    effect, mine = lax.optimization_barrier((turnover_effect, mine))
    other = swap(mine, "core", 2, 1)
    wide = cells // Z
    strip = [lax.dynamic_slice_in_dim(effect, (zid ^ b) * wide, wide, 1) for b in range(Z)]
    strip = [strip[0]] + [swap(strip[b], "z", Z, b) for b in range(1, Z)]
    system, inverse = factor_begin(where, mine, other, misfit)
    strip, system = lax.optimization_barrier((strip, system))
    narrow = wide // Y
    cut = [
        jnp.concatenate(
            [lax.dynamic_slice_in_dim(part, (yid ^ a) * narrow, narrow, 1) for part in strip], axis=0
        )
        for a in range(Y)
    ]
    cut = [cut[0]] + [swap(cut[a], "y", Y, a) for a in range(1, Y)]
    system, later = factor_finish(system, inverse)
    work = solve(where, system, inverse, later, cut)
    change = combine(rhs, work, misfit)
    return turnover_effect + lax.all_to_all(change, ("z", "y"), 0, 1, tiled=True)


def solution(mesh):
    grid = Mesh(mesh.devices.reshape(Z, Y, X, 2), ("z", "y", "x", "core"))
    mem, cell = ("z", "y"), ("x", "core")
    in_specs = (
        P(mem, cell),
        P(cell),
        P(cell),
        P(cell),
        P(None, cell),
        P(None, cell),
        P(cell, None),
        P(cell, None),
        P(cell),
        P(cell),
        P(mem, cell),
    )
    return jax.shard_map(
        body, mesh=grid, in_specs=in_specs, out_specs=P(mem, cell), check_vma=False
    )
```

```python
import math

import jax
import jax.numpy as jnp
from jax import lax
from jax.experimental import pallas as pl
from jax.experimental.pallas import tpu as pltpu
from jax.sharding import Mesh, PartitionSpec as P

STEPS = 6
BLOCK = 128
TAPS = 4
Z = 4
Y = 4
X = 4
LANES = 128
HALF = 128
TILE = 256
CHUNK = 1024
f32 = jnp.float32

ANY_VMEM = pl.BlockSpec(memory_space=pltpu.VMEM)
ANY_SMEM = pl.BlockSpec(memory_space=pltpu.SMEM)


def mm(left, right):
    return jnp.dot(left, right, precision=lax.Precision.HIGHEST, preferred_element_type=f32)


def mm_last(left, right):
    return lax.dot_general(
        left, right, (((1,), (1,)), ((), ())),
        precision=lax.Precision.HIGHEST, preferred_element_type=f32,
    )


def forward_kernel(
    effect, base, fast, slow, init, fall, taps, weights, observed, var, pred, small, resp, coef
):
    step = pl.program_id(0)
    members, cells = effect.shape
    w = slow[...]
    f = fast[...]
    left_slow = [jnp.zeros_like(w)]
    left_fast = [jnp.zeros_like(w)]
    for _ in range(STEPS):
        left_fast.append(0.7 * f + 0.3 * f * left_slow[-1] + (1.0 - f) * left_fast[-1])
        left_slow.append(w + (1.0 - w) * left_slow[-1])
    share = [0.6 + 0.4 * left_fast[STEPS - 1 - t] for t in range(STEPS)]
    for power in range(STEPS):
        total = share[power] * init[0:1, :]
        for t in range(power + 1, STEPS):
            total = total + share[t] * fall[t - 1 - power : t - power, :]
        coef[power : power + 1, :] = total
    coef[6:7, :] = init[1:2, :] * left_fast[STEPS] + init[2:3, :] * left_slow[STEPS]
    coef[7:8, :] = -base[...]

    def rows(i, _):
        at = pl.ds(pl.multiple_of(i * 8, 8), 8)
        kept = jnp.exp(coef[7:8, :] * jnp.exp(effect[at, :]))
        total = coef[5:6, :]
        for power in range(4, -1, -1):
            total = total * kept + coef[power : power + 1, :]
        resp[at, :] = coef[6:7, :] + (1.0 - kept) * total
        return 0

    lax.fori_loop(0, members // 8, rows, 0)
    position = lax.broadcasted_iota(jnp.int32, (BLOCK, LANES), 0)
    owner = lax.broadcasted_iota(jnp.int32, (members, LANES), 1) // 32
    spread = jnp.zeros((1, LANES), f32)
    for group in range(cells // (4 * BLOCK)):
        lanes = slice(group * LANES, (group + 1) * LANES)
        table = jnp.zeros((BLOCK, LANES), f32)
        for k in range(TAPS):
            table = table + jnp.where(taps[k : k + 1, lanes] == position, weights[k : k + 1, lanes], 0.0)
        stacked = jnp.concatenate(
            [resp[:, (4 * group + b) * BLOCK : (4 * group + b + 1) * BLOCK] for b in range(4)], axis=0
        )
        product = mm(stacked, table)
        out = product[:members]
        for b in range(1, 4):
            out = jnp.where(owner == b, product[b * members : (b + 1) * members], out)
        pred[:, lanes] = out
        small[0:1, pl.ds(pl.multiple_of(step * (cells // 4) + group * LANES, LANES), LANES)] = jnp.sum(
            out, axis=0, keepdims=True
        )
        residual = observed[:, lanes] - out
        spread = spread + jnp.sum(residual * residual, axis=0, keepdims=True) / var[:, lanes]
    spread = jnp.broadcast_to(jnp.sum(spread, axis=1, keepdims=True), (1, LANES))
    tail = pl.ds(small.shape[1] - LANES, LANES)

    @pl.when(step == 0)
    def _():
        small[0:1, tail] = spread

    @pl.when(step > 0)
    def _():
        small[0:1, tail] = small[0:1, tail] + spread


def forward(effect, base, fast, slow, init, fall, taps, weights, observed, var):
    members, cells = effect.shape
    obs = taps.shape[1]
    obs_chunk = CHUNK // 4

    def wide(rows, width):
        return pl.BlockSpec((rows, width), lambda i: (0, i))

    return pl.pallas_call(
        forward_kernel,
        grid=(cells // CHUNK,),
        in_specs=[
            wide(members, CHUNK), wide(1, CHUNK), wide(1, CHUNK), wide(1, CHUNK),
            wide(3, CHUNK), wide(STEPS, CHUNK), wide(TAPS, obs_chunk), wide(TAPS, obs_chunk),
            wide(1, obs_chunk), wide(1, obs_chunk),
        ],
        out_specs=[wide(members, obs_chunk), pl.BlockSpec((1, obs + LANES), lambda i: (0, 0))],
        out_shape=[
            jax.ShapeDtypeStruct((members, obs), f32),
            jax.ShapeDtypeStruct((1, obs + LANES), f32),
        ],
        scratch_shapes=[pltpu.VMEM((members, CHUNK), f32), pltpu.VMEM((8, CHUNK), f32)],
        cost_estimate=cost(2e10),
        name="forward",
    )(effect, base, fast, slow, init, fall, taps, weights, observed, var)


def gram_kernel(
    where, e0, e1, e2, e3, e4, p1, p2, p3, p4, n0, n1, n2, n3, n4, observed, var,
    keep, send, left, right, total,
):
    step = pl.program_id(0)
    zid, yid = where[0], where[1]
    members = p1.shape[0]
    half = members // 2
    member_count = members * Z * Y
    inv_root = 1.0 / math.sqrt(member_count - 1)
    tails = e0[members:, :] + e1[members:, :] + e2[members:, :] + e4[half:, :]
    mean = tails[0:1, :] / member_count
    inv_var = 1.0 / var[...]
    root_var = jnp.sqrt(var[...])

    def pieces(own, back, forth, low, high):
        return ((0, 0, own), (3, 0, back), (1, 0, forth), (2, 0, low), (2, half, high))

    for (turn, skip, e), (_, _, n) in zip(pieces(e0, e1, e2, e3, e4), pieces(n0, n1, n2, n3, n4)):
        count = n.shape[0]
        at = pl.multiple_of(((yid + turn) & 3) * members + skip, half)
        left[pl.ds(at, count), :] = (e[0:count, :] - mean) * inv_root
        left[pl.ds(at + Y * members, count), :] = observed[...] + root_var * n[...] - e[0:count, :]
    for turn, skip, p in pieces(e0, p1, p2, p3, p4):
        count = half if turn == 2 else members
        at = pl.multiple_of(((zid + turn) & 3) * members + skip, half)
        right[pl.ds(at, count), :] = (p[0:count, :] - mean) * inv_root * inv_var

    product = mm_last(left[...], right[...])

    @pl.when(step == 0)
    def _():
        total[...] = product

    @pl.when(step > 0)
    def _():
        total[...] = total[...] + product

    @pl.when(step == pl.num_programs(0) - 1)
    def _():
        core, xid = where[2], where[3]
        for part, offset in ((keep, core * 32), (send, 32 - core * 32)):
            for a in range(X):
                at = pl.multiple_of((xid ^ a) * 64 + offset, 32)
                part[a, 0:32, 0:TILE] = total[pl.ds(at, 32), :]
                part[a, 0:32, TILE : 2 * TILE] = total[pl.ds(at + TILE, 32), :]
                part[a, 32:40, :] = jnp.broadcast_to(tails[1:2, 0:1], (8, 2 * TILE))


def gram_block(where, rows, columns, noise, observed, var):
    members, obs = columns[0].shape
    half = members // 2
    width = 512

    def chunk(n):
        return pl.BlockSpec((n, width), lambda i: (0, i))

    return pl.pallas_call(
        gram_kernel,
        grid=(obs // width,),
        in_specs=[ANY_SMEM] + [chunk(members + 8)] * 3 + [chunk(half), chunk(half + 8)]
        + [chunk(members)] * 2 + [chunk(half)] * 2 + [chunk(members)] * 3 + [chunk(half)] * 2
        + [chunk(1)] * 2,
        out_specs=[pl.BlockSpec((X, 40, 2 * TILE), lambda i: (0, 0, 0))] * 2,
        out_shape=[jax.ShapeDtypeStruct((X, 40, 2 * TILE), f32)] * 2,
        scratch_shapes=[
            pltpu.VMEM((2 * TILE, width), f32),
            pltpu.VMEM((TILE, width), f32),
            pltpu.VMEM((2 * TILE, TILE), f32),
        ],
        cost_estimate=cost(8e9),
        name="gram",
    )(where, *rows, *columns, *noise, observed, var)


def cost(flops):
    return pl.CostEstimate(flops=int(flops), bytes_accessed=int(1e7), transcendentals=0)


def invert_block(rows):
    width = HALF
    count = width // 8
    rows = list(rows)
    lane = lax.broadcasted_iota(jnp.int32, (8, width), 1)
    sub = lax.broadcasted_iota(jnp.int32, (8, width), 0)

    def row(value, r):
        return jnp.broadcast_to(value[r : r + 1, :], (8, width))

    for block in range(count):
        low = 8 * block
        panel = rows[block]
        inside = (lane >= low) & (lane < low + 8)
        early = {
            i: [jnp.broadcast_to(rows[i][:, low + p : low + p + 1], (8, width)) for p in range(8)]
            for i in range(block + 1, min(block + 3, count))
        }
        pivots = [jnp.broadcast_to(panel[:, low + p : low + p + 1], (8, width)) for p in range(8)]
        for r in range(8):
            heads = [row(pivots[p], r) for p in range(8)]
            inverse = 1.0 / heads[r]
            here = sub == r
            column = jnp.where(here, 0.0, pivots[r])
            for p in range(8):
                if p != r:
                    scaled = heads[p] * inverse
                    pivots[p] = jnp.where(here, scaled, pivots[p] - column * scaled)
            pivots[r] = jnp.where(here, inverse, -column * inverse)
        panel = jnp.where(inside, jnp.where(lane - low == sub, 1.0, 0.0), panel)
        terms = [pivots[p] * row(panel, p) for p in range(8)]
        while len(terms) > 1:
            terms = [terms[i] + terms[i + 1] for i in range(0, len(terms), 2)]
        solved = terms[0]
        heads = [row(solved, p) for p in range(8)]
        zero = jnp.zeros((8, width), f32)
        masked = [
            zero if block <= i <= block + 2 else jnp.where(inside, rows[i], 0.0) for i in range(count)
        ]
        spread = [solved if i == block else zero for i in range(count)]
        product = mm(jnp.concatenate(masked, axis=0), jnp.concatenate(spread, axis=0))
        for i in range(count):
            if i == block:
                rows[i] = solved
            elif i in early:
                terms = [early[i][p] * heads[p] for p in range(8)]
                while len(terms) > 1:
                    terms = [terms[j] + terms[j + 1] for j in range(0, len(terms), 2)]
                rows[i] = jnp.where(inside, 0.0, rows[i]) - terms[0]
            else:
                rows[i] = jnp.where(inside, 0.0, rows[i]) - product[8 * i : 8 * i + 8]
    return rows


def begin_kernel(where, mine, other, misfit, system, inverses, last, halves, ahead, behind):
    core = where[2]
    scale = f32(1024 * 16384) / misfit[0:1, 0:1]
    for z in range(Z):
        for y in range(Y):
            for x in range(X):
                piece = slice(((z * Y + y) * X + x) * 32, ((z * Y + y) * X + x) * 32 + 32)
                at = x * TILE + z * 64
                lanes = slice(y * TILE, (y + 1) * TILE)
                system[pl.ds(pl.multiple_of(at + core * 32, 32), 32), lanes] = mine[piece, :] * scale
                system[pl.ds(pl.multiple_of(at + 32 - core * 32, 32), 32), lanes] = other[piece, :] * scale
    eye = jnp.where(
        lax.broadcasted_iota(jnp.int32, (HALF, HALF), 0) == lax.broadcasted_iota(jnp.int32, (HALF, HALF), 1),
        1.0, 0.0,
    )
    for d in range(system.shape[0] // HALF):
        at = slice(d * HALF, (d + 1) * HALF)
        system[at, at] = system[at, at] + eye
    eliminate(system, inverses, 0, last, halves, ahead, behind)


def finish_kernel(before, earlier, system, inverses, last, halves, ahead, behind, arrived):
    copy = pltpu.make_async_copy(before, system, arrived)
    copy.start()
    last[...] = earlier[TILE:, :]
    copy.wait()
    eliminate(system, inverses, 2, last, halves, ahead, behind)


def eliminate(system, inverses, start, last, halves, ahead, behind):
    tiles = system.shape[0] // TILE

    def spread(k):
        top = pl.multiple_of(k * TILE, TILE)

        def across(t, _):
            lanes = pl.ds(pl.multiple_of(t * TILE, TILE), TILE)
            system[pl.ds(top, TILE), lanes] = mm(last[...], system[pl.ds(top, TILE), lanes])

            def down(i, _):
                at = pl.ds(pl.multiple_of(i * TILE, TILE), TILE)
                system[at, lanes] = system[at, lanes] - mm(
                    system[at, pl.ds(top, TILE)], system[pl.ds(top, TILE), lanes]
                )
                return 0

            lax.fori_loop(k + 1, tiles, down, 0)
            return 0

        lax.fori_loop(k + 1, tiles, across, 0)

    def stage(k, _):
        @pl.when(k > 0)
        def _():
            spread(k - 1)

        top = pl.multiple_of(k * TILE, TILE)
        low = pl.multiple_of(k * TILE + HALF, HALF)

        def half(h, _):
            at = pl.multiple_of(top + h * HALF, HALF)
            block = [system[pl.ds(at + 8 * j, 8), pl.ds(at, HALF)] for j in range(HALF // 8)]
            block = invert_block(block)
            for j in range(HALF // 8):
                halves[pl.ds(pl.multiple_of(h * HALF + 8 * j, 8), 8), :] = block[j]

            @pl.when(h == 0)
            def _():
                first = halves[0:HALF, :]
                upper = system[pl.ds(top, HALF), pl.ds(low, HALF)]
                ahead[...] = mm(first, upper)
                behind[...] = mm(system[pl.ds(low, HALF), pl.ds(top, HALF)], first)
                system[pl.ds(low, HALF), pl.ds(low, HALF)] = (
                    system[pl.ds(low, HALF), pl.ds(low, HALF)] - mm(behind[...], upper)
                )

            return 0

        lax.fori_loop(0, 2, half, 0)
        second = halves[HALF:, :]
        corner = mm(second, behind[...])
        last[0:HALF, 0:HALF] = halves[0:HALF, :] + mm(ahead[...], corner)
        last[0:HALF, HALF:] = -mm(ahead[...], second)
        last[HALF:, 0:HALF] = -corner
        last[HALF:, HALF:] = second
        inverses[pl.ds(pl.multiple_of((k - start) * TILE, TILE), TILE), :] = last[...]
        return 0

    lax.fori_loop(start, start + 2, stage, 0)


FACTOR_SCRATCH = [
    pltpu.VMEM((TILE, TILE), f32), pltpu.VMEM((TILE, HALF), f32), pltpu.VMEM((HALF, HALF), f32),
    pltpu.VMEM((HALF, HALF), f32),
]


def factor_begin(where, mine, other, misfit):
    n = TILE * Y
    return pl.pallas_call(
        begin_kernel,
        in_specs=[ANY_SMEM, ANY_VMEM, ANY_VMEM, ANY_VMEM],
        out_specs=[ANY_VMEM, ANY_VMEM],
        out_shape=[jax.ShapeDtypeStruct((n, n), f32), jax.ShapeDtypeStruct((2 * TILE, TILE), f32)],
        scratch_shapes=FACTOR_SCRATCH,
        cost_estimate=cost(2e10),
        name="factor_begin",
    )(where, mine, other, misfit)


def factor_finish(system, earlier):
    n = system.shape[0]
    return pl.pallas_call(
        finish_kernel,
        in_specs=[pl.BlockSpec(memory_space=pl.ANY), ANY_VMEM],
        out_specs=[ANY_VMEM, ANY_VMEM],
        out_shape=[jax.ShapeDtypeStruct((n, n), f32), jax.ShapeDtypeStruct((2 * TILE, TILE), f32)],
        scratch_shapes=FACTOR_SCRATCH + [pltpu.SemaphoreType.DMA],
        cost_estimate=cost(2e10),
        name="factor_finish",
    )(system, earlier)


def solve_kernel(where, system, earlier, later, b0, b1, b2, b3, work):
    zid, yid = where[0], where[1]
    n = system.shape[0]
    tiles = n // TILE
    for a, block in enumerate((b0, b1, b2, b3)):
        for b in range(Z):
            at = pl.multiple_of((yid ^ a) * TILE + (zid ^ b) * 64, 64)
            work[pl.ds(at, 64), :] = block[b * 64 : (b + 1) * 64, :]
    mean = jnp.sum(work[...], axis=0, keepdims=True) / n
    inv_root = 1.0 / math.sqrt(n - 1)
    work[...] = (work[...] - mean) * inv_root
    for k in range(tiles):
        at = slice(k * TILE, (k + 1) * TILE)
        source = earlier if k < 2 else later
        work[at, :] = mm(source[(k % 2) * TILE : (k % 2 + 1) * TILE, :], work[at, :])

        def down(i, _, at=at):
            low = pl.ds(pl.multiple_of(i * TILE, TILE), TILE)
            work[low, :] = work[low, :] - mm(system[low, at], work[at, :])
            return 0

        lax.fori_loop(k + 1, tiles, down, 0)
    for k in range(tiles - 2, -1, -1):
        at = slice(k * TILE, (k + 1) * TILE)
        rest = slice((k + 1) * TILE, n)
        work[at, :] = work[at, :] - mm(system[at, rest], work[rest, :])


def solve(where, system, earlier, later, blocks):
    return pl.pallas_call(
        solve_kernel,
        in_specs=[ANY_SMEM] + [ANY_VMEM] * 7,
        out_specs=ANY_VMEM,
        out_shape=jax.ShapeDtypeStruct((system.shape[0], blocks[0].shape[1]), f32),
        cost_estimate=cost(5e9),
        name="solve",
    )(where, system, earlier, later, *blocks)


def combine_kernel(rhs, work, misfit, out):
    scale = f32(1024 * 16384) / misfit[0:1, 0:1]
    total = mm(rhs[0:TILE, :], work[0:TILE, :])
    for y in range(1, Y):
        total = total + mm(rhs[y * TILE : (y + 1) * TILE, :], work[y * TILE : (y + 1) * TILE, :])
    out[...] = scale * total


def combine(rhs, work, misfit):
    n, width = work.shape
    return pl.pallas_call(
        combine_kernel,
        grid=(Z,),
        in_specs=[
            pl.BlockSpec((Y * TILE, TILE), lambda z: (z, 0)), ANY_VMEM, ANY_VMEM,
        ],
        out_specs=pl.BlockSpec((TILE, width), lambda z: (z, 0)),
        out_shape=jax.ShapeDtypeStruct((n, width), f32),
        cost_estimate=cost(6e9),
        name="combine",
    )(rhs, work, misfit)


def neighbours(value, axis):
    back = lax.ppermute(value, axis, [(i, (i + 1) % 4) for i in range(4)])
    forth = lax.ppermute(value, axis, [(i, (i + 3) % 4) for i in range(4)])
    return back, forth


def opposite(back, forth, axis):
    half = 32
    low = lax.ppermute(back[:half], axis, [(i, (i + 1) % 4) for i in range(4)])
    high = lax.ppermute(forth[half:], axis, [(i, (i + 3) % 4) for i in range(4)])
    return low, high


def swap(value, axis, size, bit):
    return lax.ppermute(value, axis, [(i, i ^ bit) for i in range(size)])


def body(
    turnover_effect,
    base_rate,
    fast_rate,
    slow_rate,
    init_pools,
    litterfall,
    obs_taps,
    obs_weights,
    observed,
    obs_var,
    obs_noise,
):
    members, cells = turnover_effect.shape
    obs = obs_taps.shape[0]
    zid, yid, core = lax.axis_index("z"), lax.axis_index("y"), lax.axis_index("core")
    where = jnp.stack([zid, yid, core, lax.axis_index("x")]).astype(jnp.int32)
    observed = observed[None, :]
    obs_var = obs_var[None, :]
    noise = neighbours(obs_noise, "y")
    predicted, small = forward(
        turnover_effect, base_rate[None, :], fast_rate[None, :], slow_rate[None, :],
        init_pools, litterfall, obs_taps.T, obs_weights.T, observed, obs_var,
    )
    small, noise = lax.optimization_barrier((small, noise))
    noise = (obs_noise,) + noise + opposite(*noise, "y")
    small = small + sum(swap(small, "z", Z, b) for b in range(1, Z))
    small, predicted, noise = lax.optimization_barrier((small, predicted, noise))
    extended = jnp.concatenate(
        [predicted, small[:, :obs], jnp.broadcast_to(small[:, obs : obs + 1], (7, obs))], axis=0
    )
    rows = neighbours(extended, "y")
    columns = neighbours(predicted, "z")
    rows = (extended,) + rows + opposite(*rows, "y")
    columns = columns + opposite(*columns, "z")
    keep, send = gram_block(where, rows, columns, noise, observed, obs_var)
    part = keep + swap(send, "core", 2, 1)
    shared = part[0] + sum(swap(part[a], "x", X, a) for a in range(1, X))
    piece, right, misfit = shared[:32, :TILE], shared[:32, TILE:], shared[32:, :LANES]
    rhs = lax.all_gather(right, ("z", "y", "x", "core"), axis=0, tiled=True)
    mine = lax.all_to_all(
        jnp.broadcast_to(piece[None], (Z * Y * X, 32, TILE)), ("z", "y", "x"), 0, 0, tiled=True
    ).reshape(Z * Y * X * 32, TILE)
    effect, mine = lax.optimization_barrier((turnover_effect, mine))
    other = swap(mine, "core", 2, 1)
    wide = cells // Z
    strip = [lax.dynamic_slice_in_dim(effect, (zid ^ b) * wide, wide, 1) for b in range(Z)]
    strip = [strip[0]] + [swap(strip[b], "z", Z, b) for b in range(1, Z)]
    system, inverse = factor_begin(where, mine, other, misfit)
    strip, system = lax.optimization_barrier((strip, system))
    narrow = wide // Y
    cut = [
        jnp.concatenate(
            [lax.dynamic_slice_in_dim(part, (yid ^ a) * narrow, narrow, 1) for part in strip], axis=0
        )
        for a in range(Y)
    ]
    cut = [cut[0]] + [swap(cut[a], "y", Y, a) for a in range(1, Y)]
    system, later = factor_finish(system, inverse)
    work = solve(where, system, inverse, later, cut)
    change = combine(rhs, work, misfit)
    return turnover_effect + lax.all_to_all(change, ("z", "y"), 0, 1, tiled=True)


def solution(mesh):
    grid = Mesh(mesh.devices.reshape(Z, Y, X, 2), ("z", "y", "x", "core"))
    mem, cell = ("z", "y"), ("x", "core")
    in_specs = (
        P(mem, cell),
        P(cell),
        P(cell),
        P(cell),
        P(None, cell),
        P(None, cell),
        P(cell, None),
        P(cell, None),
        P(cell),
        P(cell),
        P(mem, cell),
    )
    return jax.shard_map(
        body, mesh=grid, in_specs=in_specs, out_specs=P(mem, cell), check_vma=False
    )
```

```python
import math

import jax
import jax.numpy as jnp
from jax import lax
from jax.experimental import pallas as pl
from jax.experimental.pallas import tpu as pltpu
from jax.sharding import Mesh, PartitionSpec as P

STEPS = 6
BLOCK = 128
TAPS = 4
Z = 4
Y = 4
X = 4
LANES = 128
HALF = 128
TILE = 256
CHUNK = 1024
f32 = jnp.float32

ANY_VMEM = pl.BlockSpec(memory_space=pltpu.VMEM)
ANY_SMEM = pl.BlockSpec(memory_space=pltpu.SMEM)


def mm(left, right):
    return jnp.dot(left, right, precision=lax.Precision.HIGHEST, preferred_element_type=f32)


def mm_last(left, right):
    return lax.dot_general(
        left, right, (((1,), (1,)), ((), ())),
        precision=lax.Precision.HIGHEST, preferred_element_type=f32,
    )


def forward_kernel(
    effect, base, fast, slow, init, fall, taps, weights, observed, var, pred, resp, coef
):
    members, cells = effect.shape
    w = slow[...]
    f = fast[...]
    left_slow = [jnp.zeros_like(w)]
    left_fast = [jnp.zeros_like(w)]
    for _ in range(STEPS):
        left_fast.append(0.7 * f + 0.3 * f * left_slow[-1] + (1.0 - f) * left_fast[-1])
        left_slow.append(w + (1.0 - w) * left_slow[-1])
    share = [0.6 + 0.4 * left_fast[STEPS - 1 - t] for t in range(STEPS)]
    for power in range(STEPS):
        total = share[power] * init[0:1, :]
        for t in range(power + 1, STEPS):
            total = total + share[t] * fall[t - 1 - power : t - power, :]
        coef[power : power + 1, :] = total
    coef[6:7, :] = init[1:2, :] * left_fast[STEPS] + init[2:3, :] * left_slow[STEPS]
    coef[7:8, :] = -base[...]

    def rows(i, _):
        at = pl.ds(pl.multiple_of(i * 8, 8), 8)
        kept = jnp.exp(coef[7:8, :] * jnp.exp(effect[at, :]))
        total = coef[5:6, :]
        for power in range(4, -1, -1):
            total = total * kept + coef[power : power + 1, :]
        resp[at, :] = coef[6:7, :] + (1.0 - kept) * total
        return 0

    lax.fori_loop(0, members // 8, rows, 0)
    position = lax.broadcasted_iota(jnp.int32, (BLOCK, LANES), 0)
    owner = lax.broadcasted_iota(jnp.int32, (members, LANES), 1) // 32
    for group in range(cells // (4 * BLOCK)):
        lanes = slice(group * LANES, (group + 1) * LANES)
        table = jnp.zeros((BLOCK, LANES), f32)
        for k in range(TAPS):
            table = table + jnp.where(taps[k : k + 1, lanes] == position, weights[k : k + 1, lanes], 0.0)
        stacked = jnp.concatenate(
            [resp[:, (4 * group + b) * BLOCK : (4 * group + b + 1) * BLOCK] for b in range(4)], axis=0
        )
        product = mm(stacked, table)
        out = product[:members]
        for b in range(1, 4):
            out = jnp.where(owner == b, product[b * members : (b + 1) * members], out)
        pred[0:members, lanes] = out
        residual = observed[:, lanes] - out
        spread = jnp.sum(residual * residual, axis=0, keepdims=True) / var[:, lanes]
        pred[members : members + 1, lanes] = jnp.sum(out, axis=0, keepdims=True)
        pred[members + 1 :, lanes] = jnp.broadcast_to(spread, (7, LANES))


def forward(effect, base, fast, slow, init, fall, taps, weights, observed, var):
    members, cells = effect.shape
    obs = taps.shape[1]
    obs_chunk = CHUNK // 4

    def wide(rows, width):
        return pl.BlockSpec((rows, width), lambda i: (0, i))

    return pl.pallas_call(
        forward_kernel,
        grid=(cells // CHUNK,),
        in_specs=[
            wide(members, CHUNK), wide(1, CHUNK), wide(1, CHUNK), wide(1, CHUNK),
            wide(3, CHUNK), wide(STEPS, CHUNK), wide(TAPS, obs_chunk), wide(TAPS, obs_chunk),
            wide(1, obs_chunk), wide(1, obs_chunk),
        ],
        out_specs=wide(members + 8, obs_chunk),
        out_shape=jax.ShapeDtypeStruct((members + 8, obs), f32),
        scratch_shapes=[pltpu.VMEM((members, CHUNK), f32), pltpu.VMEM((8, CHUNK), f32)],
        cost_estimate=cost(2e10),
        name="forward",
    )(effect, base, fast, slow, init, fall, taps, weights, observed, var)


def gram_kernel(
    where, e0, e1, e2, e3, e4, t0, t2, p1, p2, p3, n0, n1, n2, observed, var,
    keep, send, left, right, total, misfit,
):
    step = pl.program_id(0)
    zid, yid = where[0], where[1]
    members = n0.shape[0]
    half = members // 2
    member_count = members * Z * Y
    inv_root = 1.0 / math.sqrt(member_count - 1)
    tails = t0[...] + t2[...] + e3[half:, :] + e4[half:, :]
    shares = jnp.sum(tails[1:2, :], axis=1, keepdims=True)
    mean = tails[0:1, :] / member_count
    inv_var = 1.0 / var[...]
    root_var = jnp.sqrt(var[...])

    kept = members + 8
    for turn, skip, count, e, n, below in (
        (0, 0, members, e0, n0, 0), (3, 0, members, e1, n1, 0), (1, 0, members, e2, n2, 0),
        (2, 0, half, e3, e1, kept), (2, half, half, e4, e2, kept),
    ):
        at = pl.multiple_of(((yid + turn) & 3) * members + skip, half)
        left[pl.ds(at, count), :] = (e[0:count, :] - mean) * inv_root
        left[pl.ds(at + Y * members, count), :] = (
            observed[...] + root_var * n[below : below + count, :] - e[0:count, :]
        )
    for turn, p in ((0, e0), (3, p1), (1, p2), (2, p3)):
        at = pl.multiple_of(((zid + turn) & 3) * members, members)
        right[pl.ds(at, members), :] = (p[0:members, :] - mean) * inv_root * inv_var

    product = mm_last(left[...], right[...])

    @pl.when(step == 0)
    def _():
        total[...] = product
        misfit[...] = jnp.broadcast_to(shares, misfit.shape)

    @pl.when(step > 0)
    def _():
        total[...] = total[...] + product
        misfit[...] = misfit[...] + shares

    @pl.when(step == pl.num_programs(0) - 1)
    def _():
        core, xid = where[2], where[3]
        for part, offset in ((keep, core * 32), (send, 32 - core * 32)):
            for a in range(X):
                at = pl.multiple_of((xid ^ a) * 64 + offset, 32)
                part[a, 0:32, 0:TILE] = total[pl.ds(at, 32), :]
                part[a, 0:32, TILE : 2 * TILE] = total[pl.ds(at + TILE, 32), :]
                part[a, 32:40, :] = jnp.broadcast_to(misfit[0:1, 0:1], (8, 2 * TILE))


def gram_block(where, rows, columns, noise, observed, var):
    members, obs = noise[0].shape
    half = members // 2
    width = 512

    def chunk(n):
        return pl.BlockSpec((n, width), lambda i: (0, i))

    return pl.pallas_call(
        gram_kernel,
        grid=(obs // width,),
        in_specs=[ANY_SMEM, chunk(members + 8)] + [chunk(members + half + 8)] * 2
        + [chunk(half + 8)] * 2 + [chunk(8)] * 2 + [chunk(members + 8)] * 3 + [chunk(members)] * 3
        + [chunk(1)] * 2,
        out_specs=[pl.BlockSpec((X, 40, 2 * TILE), lambda i: (0, 0, 0))] * 2,
        out_shape=[jax.ShapeDtypeStruct((X, 40, 2 * TILE), f32)] * 2,
        scratch_shapes=[
            pltpu.VMEM((2 * TILE, width), f32),
            pltpu.VMEM((TILE, width), f32),
            pltpu.VMEM((2 * TILE, TILE), f32),
            pltpu.VMEM((8, LANES), f32),
        ],
        cost_estimate=cost(8e9),
        name="gram",
    )(where, *rows, *columns, *noise, observed, var)


def cost(flops):
    return pl.CostEstimate(flops=int(flops), bytes_accessed=int(1e7), transcendentals=0)


def invert_block(rows):
    width = HALF
    count = width // 8
    rows = list(rows)
    lane = lax.broadcasted_iota(jnp.int32, (8, width), 1)
    sub = lax.broadcasted_iota(jnp.int32, (8, width), 0)

    def row(value, r):
        return jnp.broadcast_to(value[r : r + 1, :], (8, width))

    for block in range(count):
        low = 8 * block
        panel = rows[block]
        inside = (lane >= low) & (lane < low + 8)
        early = {
            i: [jnp.broadcast_to(rows[i][:, low + p : low + p + 1], (8, width)) for p in range(8)]
            for i in range(block + 1, min(block + 3, count))
        }
        pivots = [jnp.broadcast_to(panel[:, low + p : low + p + 1], (8, width)) for p in range(8)]
        for r in range(8):
            heads = [row(pivots[p], r) for p in range(8)]
            inverse = 1.0 / heads[r]
            here = sub == r
            column = jnp.where(here, 0.0, pivots[r])
            for p in range(8):
                if p != r:
                    scaled = heads[p] * inverse
                    pivots[p] = jnp.where(here, scaled, pivots[p] - column * scaled)
            pivots[r] = jnp.where(here, inverse, -column * inverse)
        panel = jnp.where(inside, jnp.where(lane - low == sub, 1.0, 0.0), panel)
        terms = [pivots[p] * row(panel, p) for p in range(8)]
        while len(terms) > 1:
            terms = [terms[i] + terms[i + 1] for i in range(0, len(terms), 2)]
        solved = terms[0]
        heads = [row(solved, p) for p in range(8)]
        zero = jnp.zeros((8, width), f32)
        masked = [
            zero if block <= i <= block + 2 else jnp.where(inside, rows[i], 0.0) for i in range(count)
        ]
        spread = [solved if i == block else zero for i in range(count)]
        product = mm(jnp.concatenate(masked, axis=0), jnp.concatenate(spread, axis=0))
        for i in range(count):
            if i == block:
                rows[i] = solved
            elif i in early:
                terms = [early[i][p] * heads[p] for p in range(8)]
                while len(terms) > 1:
                    terms = [terms[j] + terms[j + 1] for j in range(0, len(terms), 2)]
                rows[i] = jnp.where(inside, 0.0, rows[i]) - terms[0]
            else:
                rows[i] = jnp.where(inside, 0.0, rows[i]) - product[8 * i : 8 * i + 8]
    return rows


def begin_kernel(where, mine, other, misfit, system, inverses, last, halves, ahead, behind):
    core = where[2]
    scale = f32(1024 * 16384) / misfit[0:1, 0:1]
    for z in range(Z):
        for y in range(Y):
            for x in range(X):
                piece = slice(((z * Y + y) * X + x) * 32, ((z * Y + y) * X + x) * 32 + 32)
                at = x * TILE + z * 64
                lanes = slice(y * TILE, (y + 1) * TILE)
                system[pl.ds(pl.multiple_of(at + core * 32, 32), 32), lanes] = mine[piece, :] * scale
                system[pl.ds(pl.multiple_of(at + 32 - core * 32, 32), 32), lanes] = other[piece, :] * scale
    eye = jnp.where(
        lax.broadcasted_iota(jnp.int32, (HALF, HALF), 0) == lax.broadcasted_iota(jnp.int32, (HALF, HALF), 1),
        1.0, 0.0,
    )
    for d in range(system.shape[0] // HALF):
        at = slice(d * HALF, (d + 1) * HALF)
        system[at, at] = system[at, at] + eye
    eliminate(system, inverses, 0, last, halves, ahead, behind)


def finish_kernel(before, earlier, system, inverses, last, halves, ahead, behind, arrived):
    copy = pltpu.make_async_copy(before, system, arrived)
    copy.start()
    last[...] = earlier[TILE:, :]
    copy.wait()
    eliminate(system, inverses, 2, last, halves, ahead, behind)


def eliminate(system, inverses, start, last, halves, ahead, behind):
    tiles = system.shape[0] // TILE

    def spread(k):
        top = pl.multiple_of(k * TILE, TILE)

        def across(t, _):
            lanes = pl.ds(pl.multiple_of(t * TILE, TILE), TILE)
            system[pl.ds(top, TILE), lanes] = mm(last[...], system[pl.ds(top, TILE), lanes])

            def down(i, _):
                at = pl.ds(pl.multiple_of(i * TILE, TILE), TILE)
                system[at, lanes] = system[at, lanes] - mm(
                    system[at, pl.ds(top, TILE)], system[pl.ds(top, TILE), lanes]
                )
                return 0

            lax.fori_loop(k + 1, tiles, down, 0)
            return 0

        lax.fori_loop(k + 1, tiles, across, 0)

    def stage(k, _):
        @pl.when(k > 0)
        def _():
            spread(k - 1)

        top = pl.multiple_of(k * TILE, TILE)
        low = pl.multiple_of(k * TILE + HALF, HALF)

        def half(h, _):
            at = pl.multiple_of(top + h * HALF, HALF)
            block = [system[pl.ds(at + 8 * j, 8), pl.ds(at, HALF)] for j in range(HALF // 8)]
            block = invert_block(block)
            for j in range(HALF // 8):
                halves[pl.ds(pl.multiple_of(h * HALF + 8 * j, 8), 8), :] = block[j]

            @pl.when(h == 0)
            def _():
                first = halves[0:HALF, :]
                upper = system[pl.ds(top, HALF), pl.ds(low, HALF)]
                ahead[...] = mm(first, upper)
                behind[...] = mm(system[pl.ds(low, HALF), pl.ds(top, HALF)], first)
                system[pl.ds(low, HALF), pl.ds(low, HALF)] = (
                    system[pl.ds(low, HALF), pl.ds(low, HALF)] - mm(behind[...], upper)
                )

            return 0

        lax.fori_loop(0, 2, half, 0)
        second = halves[HALF:, :]
        corner = mm(second, behind[...])
        last[0:HALF, 0:HALF] = halves[0:HALF, :] + mm(ahead[...], corner)
        last[0:HALF, HALF:] = -mm(ahead[...], second)
        last[HALF:, 0:HALF] = -corner
        last[HALF:, HALF:] = second
        inverses[pl.ds(pl.multiple_of((k - start) * TILE, TILE), TILE), :] = last[...]
        return 0

    lax.fori_loop(start, start + 2, stage, 0)


FACTOR_SCRATCH = [
    pltpu.VMEM((TILE, TILE), f32), pltpu.VMEM((TILE, HALF), f32), pltpu.VMEM((HALF, HALF), f32),
    pltpu.VMEM((HALF, HALF), f32),
]


def factor_begin(where, mine, other, misfit):
    n = TILE * Y
    return pl.pallas_call(
        begin_kernel,
        in_specs=[ANY_SMEM, ANY_VMEM, ANY_VMEM, ANY_VMEM],
        out_specs=[ANY_VMEM, ANY_VMEM],
        out_shape=[jax.ShapeDtypeStruct((n, n), f32), jax.ShapeDtypeStruct((2 * TILE, TILE), f32)],
        scratch_shapes=FACTOR_SCRATCH,
        cost_estimate=cost(2e10),
        name="factor_begin",
    )(where, mine, other, misfit)


def factor_finish(system, earlier):
    n = system.shape[0]
    return pl.pallas_call(
        finish_kernel,
        in_specs=[pl.BlockSpec(memory_space=pl.ANY), ANY_VMEM],
        out_specs=[ANY_VMEM, ANY_VMEM],
        out_shape=[jax.ShapeDtypeStruct((n, n), f32), jax.ShapeDtypeStruct((2 * TILE, TILE), f32)],
        scratch_shapes=FACTOR_SCRATCH + [pltpu.SemaphoreType.DMA],
        cost_estimate=cost(2e10),
        name="factor_finish",
    )(system, earlier)


def solve_kernel(where, system, earlier, later, b0, b1, b2, b3, work):
    zid, yid = where[0], where[1]
    n = system.shape[0]
    tiles = n // TILE
    for a, block in enumerate((b0, b1, b2, b3)):
        for b in range(Z):
            at = pl.multiple_of((yid ^ a) * TILE + (zid ^ b) * 64, 64)
            work[pl.ds(at, 64), :] = block[b * 64 : (b + 1) * 64, :]
    mean = jnp.sum(work[...], axis=0, keepdims=True) / n
    inv_root = 1.0 / math.sqrt(n - 1)
    work[...] = (work[...] - mean) * inv_root
    for k in range(tiles):
        at = slice(k * TILE, (k + 1) * TILE)
        source = earlier if k < 2 else later
        work[at, :] = mm(source[(k % 2) * TILE : (k % 2 + 1) * TILE, :], work[at, :])

        def down(i, _, at=at):
            low = pl.ds(pl.multiple_of(i * TILE, TILE), TILE)
            work[low, :] = work[low, :] - mm(system[low, at], work[at, :])
            return 0

        lax.fori_loop(k + 1, tiles, down, 0)
    for k in range(tiles - 2, -1, -1):
        at = slice(k * TILE, (k + 1) * TILE)
        rest = slice((k + 1) * TILE, n)
        work[at, :] = work[at, :] - mm(system[at, rest], work[rest, :])


def solve(where, system, earlier, later, blocks):
    return pl.pallas_call(
        solve_kernel,
        in_specs=[ANY_SMEM] + [ANY_VMEM] * 7,
        out_specs=ANY_VMEM,
        out_shape=jax.ShapeDtypeStruct((system.shape[0], blocks[0].shape[1]), f32),
        cost_estimate=cost(5e9),
        name="solve",
    )(where, system, earlier, later, *blocks)


def combine_kernel(rhs, work, misfit, out):
    scale = f32(1024 * 16384) / misfit[0:1, 0:1]
    total = mm(rhs[0:TILE, :], work[0:TILE, :])
    for y in range(1, Y):
        total = total + mm(rhs[y * TILE : (y + 1) * TILE, :], work[y * TILE : (y + 1) * TILE, :])
    out[...] = scale * total


def combine(rhs, work, misfit):
    n, width = work.shape
    return pl.pallas_call(
        combine_kernel,
        grid=(Z,),
        in_specs=[
            pl.BlockSpec((Y * TILE, TILE), lambda z: (z, 0)), ANY_VMEM, ANY_VMEM,
        ],
        out_specs=pl.BlockSpec((TILE, width), lambda z: (z, 0)),
        out_shape=jax.ShapeDtypeStruct((n, width), f32),
        cost_estimate=cost(6e9),
        name="combine",
    )(rhs, work, misfit)


def onward(low, high, axis):
    low = lax.ppermute(low, axis, [(i, (i + 1) % 4) for i in range(4)])
    high = lax.ppermute(high, axis, [(i, (i + 3) % 4) for i in range(4)])
    return low, high


def swap(value, axis, size, bit):
    return lax.ppermute(value, axis, [(i, i ^ bit) for i in range(size)])


def body(
    turnover_effect,
    base_rate,
    fast_rate,
    slow_rate,
    init_pools,
    litterfall,
    obs_taps,
    obs_weights,
    observed,
    obs_var,
    obs_noise,
):
    members, cells = turnover_effect.shape
    obs = obs_taps.shape[0]
    zid, yid, core = lax.axis_index("z"), lax.axis_index("y"), lax.axis_index("core")
    where = jnp.stack([zid, yid, core, lax.axis_index("x")]).astype(jnp.int32)
    observed = observed[None, :]
    obs_var = obs_var[None, :]
    noise = onward(obs_noise, obs_noise, "y")
    predicted = forward(
        turnover_effect, base_rate[None, :], fast_rate[None, :], slow_rate[None, :],
        init_pools, litterfall, obs_taps.T, obs_weights.T, observed, obs_var,
    )
    predicted, noise = lax.optimization_barrier((predicted, noise))
    half = members // 2
    columns = onward(predicted, predicted, "z") + (swap(predicted, "z", Z, 2),)
    back, forth = onward(
        jnp.concatenate([predicted, noise[0][:half]], axis=0),
        jnp.concatenate([predicted, noise[1][half:]], axis=0),
        "y",
    )
    sums = sum((block[members:] for block in columns), predicted[members:])
    sums, back, forth = lax.optimization_barrier((sums, back, forth))
    rows = (predicted, back, forth) + onward(
        jnp.concatenate([back[:half], sums], axis=0),
        jnp.concatenate([forth[half:members], sums], axis=0),
        "y",
    ) + (sums, swap(sums, "y", Y, 2))
    noise = (obs_noise,) + noise
    keep, send = gram_block(where, rows, columns, noise, observed, obs_var)
    part = keep + swap(send, "core", 2, 1)
    shared = part[0] + sum(swap(part[a], "x", X, a) for a in range(1, X))
    piece, right, misfit = shared[:32, :TILE], shared[:32, TILE:], shared[32:, :LANES]
    rhs = lax.all_gather(right, ("z", "y", "x", "core"), axis=0, tiled=True)
    mine = lax.all_to_all(
        jnp.broadcast_to(piece[None], (Z * Y * X, 32, TILE)), ("z", "y", "x"), 0, 0, tiled=True
    ).reshape(Z * Y * X * 32, TILE)
    effect, mine = lax.optimization_barrier((turnover_effect, mine))
    other = swap(mine, "core", 2, 1)
    wide = cells // Z
    strip = [lax.dynamic_slice_in_dim(effect, (zid ^ b) * wide, wide, 1) for b in range(Z)]
    strip = [strip[0]] + [swap(strip[b], "z", Z, b) for b in range(1, Z)]
    system, inverse = factor_begin(where, mine, other, misfit)
    strip, system = lax.optimization_barrier((strip, system))
    narrow = wide // Y
    cut = [
        jnp.concatenate(
            [lax.dynamic_slice_in_dim(part, (yid ^ a) * narrow, narrow, 1) for part in strip], axis=0
        )
        for a in range(Y)
    ]
    cut = [cut[0]] + [swap(cut[a], "y", Y, a) for a in range(1, Y)]
    system, later = factor_finish(system, inverse)
    work = solve(where, system, inverse, later, cut)
    change = combine(rhs, work, misfit)
    return turnover_effect + lax.all_to_all(change, ("z", "y"), 0, 1, tiled=True)


def solution(mesh):
    grid = Mesh(mesh.devices.reshape(Z, Y, X, 2), ("z", "y", "x", "core"))
    mem, cell = ("z", "y"), ("x", "core")
    in_specs = (
        P(mem, cell),
        P(cell),
        P(cell),
        P(cell),
        P(None, cell),
        P(None, cell),
        P(cell, None),
        P(cell, None),
        P(cell),
        P(cell),
        P(mem, cell),
    )
    return jax.shard_map(
        body, mesh=grid, in_specs=in_specs, out_specs=P(mem, cell), check_vma=False
    )
```

```python
import math

import jax
import jax.numpy as jnp
from jax import lax
from jax.experimental import pallas as pl
from jax.experimental.pallas import tpu as pltpu
from jax.sharding import Mesh, PartitionSpec as P

STEPS = 6
BLOCK = 128
TAPS = 4
Z = 4
Y = 4
X = 4
LANES = 128
HALF = 128
TILE = 256
CHUNK = 1024
f32 = jnp.float32

ANY_VMEM = pl.BlockSpec(memory_space=pltpu.VMEM)
ANY_SMEM = pl.BlockSpec(memory_space=pltpu.SMEM)


def mm(left, right):
    return jnp.dot(left, right, precision=lax.Precision.HIGHEST, preferred_element_type=f32)


def mm_last(left, right):
    return lax.dot_general(
        left, right, (((1,), (1,)), ((), ())),
        precision=lax.Precision.HIGHEST, preferred_element_type=f32,
    )


def forward_kernel(
    effect, base, fast, slow, init, fall, taps, weights, observed, var, pred, resp, coef
):
    members, cells = effect.shape
    w = slow[...]
    f = fast[...]
    left_slow = [jnp.zeros_like(w)]
    left_fast = [jnp.zeros_like(w)]
    for _ in range(STEPS):
        left_fast.append(0.7 * f + 0.3 * f * left_slow[-1] + (1.0 - f) * left_fast[-1])
        left_slow.append(w + (1.0 - w) * left_slow[-1])
    share = [0.6 + 0.4 * left_fast[STEPS - 1 - t] for t in range(STEPS)]
    for power in range(STEPS):
        total = share[power] * init[0:1, :]
        for t in range(power + 1, STEPS):
            total = total + share[t] * fall[t - 1 - power : t - power, :]
        coef[power : power + 1, :] = total
    coef[6:7, :] = init[1:2, :] * left_fast[STEPS] + init[2:3, :] * left_slow[STEPS]
    coef[7:8, :] = -base[...]

    def rows(i, _):
        at = pl.ds(pl.multiple_of(i * 8, 8), 8)
        kept = jnp.exp(coef[7:8, :] * jnp.exp(effect[at, :]))
        total = coef[5:6, :]
        for power in range(4, -1, -1):
            total = total * kept + coef[power : power + 1, :]
        resp[at, :] = coef[6:7, :] + (1.0 - kept) * total
        return 0

    lax.fori_loop(0, members // 8, rows, 0)
    position = lax.broadcasted_iota(jnp.int32, (BLOCK, LANES), 0)
    owner = lax.broadcasted_iota(jnp.int32, (members, LANES), 1) // 32
    for group in range(cells // (4 * BLOCK)):
        lanes = slice(group * LANES, (group + 1) * LANES)
        table = jnp.zeros((BLOCK, LANES), f32)
        for k in range(TAPS):
            table = table + jnp.where(taps[k : k + 1, lanes] == position, weights[k : k + 1, lanes], 0.0)
        stacked = jnp.concatenate(
            [resp[:, (4 * group + b) * BLOCK : (4 * group + b + 1) * BLOCK] for b in range(4)], axis=0
        )
        product = mm(stacked, table)
        out = product[:members]
        for b in range(1, 4):
            out = jnp.where(owner == b, product[b * members : (b + 1) * members], out)
        pred[0:members, lanes] = out
        residual = observed[:, lanes] - out
        spread = jnp.sum(residual * residual, axis=0, keepdims=True) / var[:, lanes]
        pred[members : members + 1, lanes] = jnp.sum(out, axis=0, keepdims=True)
        pred[members + 1 :, lanes] = jnp.broadcast_to(spread, (7, LANES))


def forward(effect, base, fast, slow, init, fall, taps, weights, observed, var):
    members, cells = effect.shape
    obs = taps.shape[1]
    obs_chunk = CHUNK // 4

    def wide(rows, width):
        return pl.BlockSpec((rows, width), lambda i: (0, i))

    return pl.pallas_call(
        forward_kernel,
        grid=(cells // CHUNK,),
        in_specs=[
            wide(members, CHUNK), wide(1, CHUNK), wide(1, CHUNK), wide(1, CHUNK),
            wide(3, CHUNK), wide(STEPS, CHUNK), wide(TAPS, obs_chunk), wide(TAPS, obs_chunk),
            wide(1, obs_chunk), wide(1, obs_chunk),
        ],
        out_specs=wide(members + 8, obs_chunk),
        out_shape=jax.ShapeDtypeStruct((members + 8, obs), f32),
        scratch_shapes=[pltpu.VMEM((members, CHUNK), f32), pltpu.VMEM((8, CHUNK), f32)],
        cost_estimate=cost(2e10),
        name="forward",
    )(effect, base, fast, slow, init, fall, taps, weights, observed, var)


def gram_kernel(
    where, e0, e1, e2, e3, e4, t0, t2, p1, p2, p3, n0, n1, n2, observed, var,
    keep, send, left, right, total, misfit,
):
    step = pl.program_id(0)
    zid, yid = where[0], where[1]
    members = n0.shape[0]
    half = members // 2
    member_count = members * Z * Y
    inv_root = 1.0 / math.sqrt(member_count - 1)
    tails = t0[...] + t2[...] + e3[half:, :] + e4[half:, :]
    shares = jnp.sum(tails[1:2, :], axis=1, keepdims=True)
    mean = tails[0:1, :] / member_count
    inv_var = 1.0 / var[...]
    root_var = jnp.sqrt(var[...])

    kept = members + 8
    for turn, skip, count, e, n, below in (
        (0, 0, members, e0, n0, 0), (3, 0, members, e1, n1, 0), (1, 0, members, e2, n2, 0),
        (2, 0, half, e3, e1, kept), (2, half, half, e4, e2, kept),
    ):
        at = pl.multiple_of(((yid + turn) & 3) * members + skip, half)
        left[pl.ds(at, count), :] = (e[0:count, :] - mean) * inv_root
        left[pl.ds(at + Y * members, count), :] = (
            observed[...] + root_var * n[below : below + count, :] - e[0:count, :]
        )
    for turn, p in ((0, e0), (3, p1), (1, p2), (2, p3)):
        at = pl.multiple_of(((zid + turn) & 3) * members, members)
        right[pl.ds(at, members), :] = (p[0:members, :] - mean) * inv_root * inv_var

    product = mm_last(left[...], right[...])

    @pl.when(step == 0)
    def _():
        total[...] = product
        misfit[...] = jnp.broadcast_to(shares, misfit.shape)

    @pl.when(step > 0)
    def _():
        total[...] = total[...] + product
        misfit[...] = misfit[...] + shares

    @pl.when(step == pl.num_programs(0) - 1)
    def _():
        core, xid = where[2], where[3]
        for part, offset in ((keep, core * 32), (send, 32 - core * 32)):
            for a in range(X):
                at = pl.multiple_of((xid ^ a) * 64 + offset, 32)
                part[a, 0:32, 0:TILE] = total[pl.ds(at, 32), :]
                part[a, 0:32, TILE : 2 * TILE] = total[pl.ds(at + TILE, 32), :]
                part[a, 32:40, :] = jnp.broadcast_to(misfit[0:1, 0:1], (8, 2 * TILE))


def gram_block(where, rows, columns, noise, observed, var):
    members, obs = noise[0].shape
    half = members // 2
    width = 512

    def chunk(n):
        return pl.BlockSpec((n, width), lambda i: (0, i))

    return pl.pallas_call(
        gram_kernel,
        grid=(obs // width,),
        in_specs=[ANY_SMEM, chunk(members + 8)] + [chunk(members + half + 8)] * 2
        + [chunk(half + 8)] * 2 + [chunk(8)] * 2 + [chunk(members + 8)] * 3 + [chunk(members)] * 3
        + [chunk(1)] * 2,
        out_specs=[pl.BlockSpec((X, 40, 2 * TILE), lambda i: (0, 0, 0))] * 2,
        out_shape=[jax.ShapeDtypeStruct((X, 40, 2 * TILE), f32)] * 2,
        scratch_shapes=[
            pltpu.VMEM((2 * TILE, width), f32),
            pltpu.VMEM((TILE, width), f32),
            pltpu.VMEM((2 * TILE, TILE), f32),
            pltpu.VMEM((8, LANES), f32),
        ],
        cost_estimate=cost(8e9),
        name="gram",
    )(where, *rows, *columns, *noise, observed, var)


def cost(flops):
    return pl.CostEstimate(flops=int(flops), bytes_accessed=int(1e7), transcendentals=0)


def invert_block(rows):
    width = HALF
    count = width // 8
    rows = list(rows)
    lane = lax.broadcasted_iota(jnp.int32, (8, width), 1)
    sub = lax.broadcasted_iota(jnp.int32, (8, width), 0)

    def row(value, r):
        return jnp.broadcast_to(value[r : r + 1, :], (8, width))

    for block in range(count):
        low = 8 * block
        panel = rows[block]
        inside = (lane >= low) & (lane < low + 8)
        early = {
            i: [jnp.broadcast_to(rows[i][:, low + p : low + p + 1], (8, width)) for p in range(8)]
            for i in range(block + 1, min(block + 3, count))
        }
        pivots = [jnp.broadcast_to(panel[:, low + p : low + p + 1], (8, width)) for p in range(8)]
        for r in range(8):
            heads = [row(pivots[p], r) for p in range(8)]
            inverse = 1.0 / heads[r]
            here = sub == r
            column = jnp.where(here, 0.0, pivots[r])
            for p in range(8):
                if p != r:
                    scaled = heads[p] * inverse
                    pivots[p] = jnp.where(here, scaled, pivots[p] - column * scaled)
            pivots[r] = jnp.where(here, inverse, -column * inverse)
        panel = jnp.where(inside, jnp.where(lane - low == sub, 1.0, 0.0), panel)
        terms = [pivots[p] * row(panel, p) for p in range(8)]
        while len(terms) > 1:
            terms = [terms[i] + terms[i + 1] for i in range(0, len(terms), 2)]
        solved = terms[0]
        heads = [row(solved, p) for p in range(8)]
        zero = jnp.zeros((8, width), f32)
        masked = [
            zero if block <= i <= block + 2 else jnp.where(inside, rows[i], 0.0) for i in range(count)
        ]
        spread = [solved if i == block else zero for i in range(count)]
        product = mm(jnp.concatenate(masked, axis=0), jnp.concatenate(spread, axis=0))
        for i in range(count):
            if i == block:
                rows[i] = solved
            elif i in early:
                terms = [early[i][p] * heads[p] for p in range(8)]
                while len(terms) > 1:
                    terms = [terms[j] + terms[j + 1] for j in range(0, len(terms), 2)]
                rows[i] = jnp.where(inside, 0.0, rows[i]) - terms[0]
            else:
                rows[i] = jnp.where(inside, 0.0, rows[i]) - product[8 * i : 8 * i + 8]
    return rows


def begin_kernel(where, mine, other, misfit, system, inverses, last, halves, ahead, behind):
    core = where[2]
    scale = f32(1024 * 16384) / misfit[0:1, 0:1]
    for z in range(Z):
        for y in range(Y):
            for x in range(X):
                piece = slice(((z * Y + y) * X + x) * 32, ((z * Y + y) * X + x) * 32 + 32)
                at = x * TILE + z * 64
                lanes = slice(y * TILE, (y + 1) * TILE)
                system[pl.ds(pl.multiple_of(at + core * 32, 32), 32), lanes] = mine[piece, :] * scale
                system[pl.ds(pl.multiple_of(at + 32 - core * 32, 32), 32), lanes] = other[piece, :] * scale
    eye = jnp.where(
        lax.broadcasted_iota(jnp.int32, (HALF, HALF), 0) == lax.broadcasted_iota(jnp.int32, (HALF, HALF), 1),
        1.0, 0.0,
    )
    for d in range(system.shape[0] // HALF):
        at = slice(d * HALF, (d + 1) * HALF)
        system[at, at] = system[at, at] + eye
    eliminate(system, inverses, 0, last, halves, ahead, behind)


def finish_kernel(before, earlier, system, inverses, last, halves, ahead, behind, arrived):
    copy = pltpu.make_async_copy(before, system, arrived)
    copy.start()
    last[...] = earlier[TILE:, :]
    copy.wait()
    eliminate(system, inverses, 2, last, halves, ahead, behind)


def eliminate(system, inverses, start, last, halves, ahead, behind):
    tiles = system.shape[0] // TILE

    def spread(k):
        top = pl.multiple_of(k * TILE, TILE)

        def across(t, _):
            lanes = pl.ds(pl.multiple_of(t * TILE, TILE), TILE)
            system[pl.ds(top, TILE), lanes] = mm(last[...], system[pl.ds(top, TILE), lanes])

            def down(i, _):
                at = pl.ds(pl.multiple_of(i * TILE, TILE), TILE)
                system[at, lanes] = system[at, lanes] - mm(
                    system[at, pl.ds(top, TILE)], system[pl.ds(top, TILE), lanes]
                )
                return 0

            lax.fori_loop(k + 1, tiles, down, 0)
            return 0

        lax.fori_loop(k + 1, tiles, across, 0)

    def stage(k, _):
        @pl.when(k > 0)
        def _():
            spread(k - 1)

        top = pl.multiple_of(k * TILE, TILE)
        low = pl.multiple_of(k * TILE + HALF, HALF)

        def half(h, _):
            at = pl.multiple_of(top + h * HALF, HALF)
            block = [system[pl.ds(at + 8 * j, 8), pl.ds(at, HALF)] for j in range(HALF // 8)]
            block = invert_block(block)
            for j in range(HALF // 8):
                halves[pl.ds(pl.multiple_of(h * HALF + 8 * j, 8), 8), :] = block[j]

            @pl.when(h == 0)
            def _():
                first = halves[0:HALF, :]
                upper = system[pl.ds(top, HALF), pl.ds(low, HALF)]
                ahead[...] = mm(first, upper)
                behind[...] = mm(system[pl.ds(low, HALF), pl.ds(top, HALF)], first)
                system[pl.ds(low, HALF), pl.ds(low, HALF)] = (
                    system[pl.ds(low, HALF), pl.ds(low, HALF)] - mm(behind[...], upper)
                )

            return 0

        lax.fori_loop(0, 2, half, 0)
        second = halves[HALF:, :]
        corner = mm(second, behind[...])
        last[0:HALF, 0:HALF] = halves[0:HALF, :] + mm(ahead[...], corner)
        last[0:HALF, HALF:] = -mm(ahead[...], second)
        last[HALF:, 0:HALF] = -corner
        last[HALF:, HALF:] = second
        inverses[pl.ds(pl.multiple_of((k - start) * TILE, TILE), TILE), :] = last[...]
        return 0

    lax.fori_loop(start, start + 2, stage, 0)


FACTOR_SCRATCH = [
    pltpu.VMEM((TILE, TILE), f32), pltpu.VMEM((TILE, HALF), f32), pltpu.VMEM((HALF, HALF), f32),
    pltpu.VMEM((HALF, HALF), f32),
]


def factor_begin(where, mine, other, misfit):
    n = TILE * Y
    return pl.pallas_call(
        begin_kernel,
        in_specs=[ANY_SMEM, ANY_VMEM, ANY_VMEM, ANY_VMEM],
        out_specs=[ANY_VMEM, ANY_VMEM],
        out_shape=[jax.ShapeDtypeStruct((n, n), f32), jax.ShapeDtypeStruct((2 * TILE, TILE), f32)],
        scratch_shapes=FACTOR_SCRATCH,
        cost_estimate=cost(2e10),
        name="factor_begin",
    )(where, mine, other, misfit)


def factor_finish(system, earlier):
    n = system.shape[0]
    return pl.pallas_call(
        finish_kernel,
        in_specs=[pl.BlockSpec(memory_space=pl.ANY), ANY_VMEM],
        out_specs=[ANY_VMEM, ANY_VMEM],
        out_shape=[jax.ShapeDtypeStruct((n, n), f32), jax.ShapeDtypeStruct((2 * TILE, TILE), f32)],
        scratch_shapes=FACTOR_SCRATCH + [pltpu.SemaphoreType.DMA],
        cost_estimate=cost(2e10),
        name="factor_finish",
    )(system, earlier)


def solve_kernel(where, system, earlier, later, b0, b1, b2, b3, work):
    zid, yid = where[0], where[1]
    n = system.shape[0]
    tiles = n // TILE
    for a, block in enumerate((b0, b1, b2, b3)):
        for b in range(Z):
            at = pl.multiple_of((yid ^ a) * TILE + (zid ^ b) * 64, 64)
            work[pl.ds(at, 64), :] = block[b * 64 : (b + 1) * 64, :]
    mean = jnp.sum(work[...], axis=0, keepdims=True) / n
    inv_root = 1.0 / math.sqrt(n - 1)
    work[...] = (work[...] - mean) * inv_root
    for k in range(tiles):
        at = slice(k * TILE, (k + 1) * TILE)
        source = earlier if k < 2 else later
        work[at, :] = mm(source[(k % 2) * TILE : (k % 2 + 1) * TILE, :], work[at, :])

        def down(i, _, at=at):
            low = pl.ds(pl.multiple_of(i * TILE, TILE), TILE)
            work[low, :] = work[low, :] - mm(system[low, at], work[at, :])
            return 0

        lax.fori_loop(k + 1, tiles, down, 0)
    for k in range(tiles - 2, -1, -1):
        at = slice(k * TILE, (k + 1) * TILE)
        rest = slice((k + 1) * TILE, n)
        work[at, :] = work[at, :] - mm(system[at, rest], work[rest, :])


def solve(where, system, earlier, later, blocks):
    return pl.pallas_call(
        solve_kernel,
        in_specs=[ANY_SMEM] + [ANY_VMEM] * 7,
        out_specs=ANY_VMEM,
        out_shape=jax.ShapeDtypeStruct((system.shape[0], blocks[0].shape[1]), f32),
        cost_estimate=cost(5e9),
        name="solve",
    )(where, system, earlier, later, *blocks)


def combine_kernel(where, mine, other, work, misfit, out):
    core = where[2]
    scale = f32(1024 * 16384) / misfit[0:1, 0:1]
    rows = TILE // 2
    total = jnp.zeros((TILE, work.shape[1]), f32)
    for y in range(Y):
        at = slice(y * rows, (y + 1) * rows)
        block = jnp.concatenate([mine[at, :], other[at, :]], axis=0)
        total = total + mm(block, work[y * TILE : (y + 1) * TILE, :])
    total = scale * total
    for c, offset in enumerate((core * 32, 32 - core * 32)):
        for x in range(X):
            low = c * rows + x * 32
            out[pl.ds(pl.multiple_of(x * 64 + offset, 32), 32), :] = total[low : low + 32, :]


def combine(where, mine, other, work, misfit):
    n, width = work.shape
    rows = pl.BlockSpec((Y * TILE // 2, TILE), lambda z: (z, 0))
    return pl.pallas_call(
        combine_kernel,
        grid=(Z,),
        in_specs=[ANY_SMEM, rows, rows, ANY_VMEM, ANY_VMEM],
        out_specs=pl.BlockSpec((TILE, width), lambda z: (z, 0)),
        out_shape=jax.ShapeDtypeStruct((n, width), f32),
        cost_estimate=cost(6e9),
        name="combine",
    )(where, mine, other, work, misfit)


def collect(piece):
    pieces = lax.all_to_all(
        jnp.broadcast_to(piece[None], (Z * Y * X,) + piece.shape), ("z", "y", "x"), 0, 0, tiled=True
    )
    return pieces.reshape(Z * Y * X * piece.shape[0], piece.shape[1])


def onward(low, high, axis):
    low = lax.ppermute(low, axis, [(i, (i + 1) % 4) for i in range(4)])
    high = lax.ppermute(high, axis, [(i, (i + 3) % 4) for i in range(4)])
    return low, high


def swap(value, axis, size, bit):
    return lax.ppermute(value, axis, [(i, i ^ bit) for i in range(size)])


def body(
    turnover_effect,
    base_rate,
    fast_rate,
    slow_rate,
    init_pools,
    litterfall,
    obs_taps,
    obs_weights,
    observed,
    obs_var,
    obs_noise,
):
    members, cells = turnover_effect.shape
    obs = obs_taps.shape[0]
    zid, yid, core = lax.axis_index("z"), lax.axis_index("y"), lax.axis_index("core")
    where = jnp.stack([zid, yid, core, lax.axis_index("x")]).astype(jnp.int32)
    observed = observed[None, :]
    obs_var = obs_var[None, :]
    noise = onward(obs_noise, obs_noise, "y")
    predicted = forward(
        turnover_effect, base_rate[None, :], fast_rate[None, :], slow_rate[None, :],
        init_pools, litterfall, obs_taps.T, obs_weights.T, observed, obs_var,
    )
    predicted, noise = lax.optimization_barrier((predicted, noise))
    half = members // 2
    columns = onward(predicted, predicted, "z") + (swap(predicted, "z", Z, 2),)
    back, forth = onward(
        jnp.concatenate([predicted, noise[0][:half]], axis=0),
        jnp.concatenate([predicted, noise[1][half:]], axis=0),
        "y",
    )
    sums = sum((block[members:] for block in columns), predicted[members:])
    sums, back, forth = lax.optimization_barrier((sums, back, forth))
    rows = (predicted, back, forth) + onward(
        jnp.concatenate([back[:half], sums], axis=0),
        jnp.concatenate([forth[half:members], sums], axis=0),
        "y",
    ) + (sums, swap(sums, "y", Y, 2))
    noise = (obs_noise,) + noise
    keep, send = gram_block(where, rows, columns, noise, observed, obs_var)
    part = keep + swap(send, "core", 2, 1)
    shared = part[0] + sum(swap(part[a], "x", X, a) for a in range(1, X))
    piece, right, misfit = shared[:32, :TILE], shared[:32, TILE:], shared[32:, :LANES]
    mine = collect(piece)
    effect, right, mine = lax.optimization_barrier((turnover_effect, right, mine))
    right = collect(right)
    other = swap(mine, "core", 2, 1)
    wide = cells // Z
    strip = [lax.dynamic_slice_in_dim(effect, (zid ^ b) * wide, wide, 1) for b in range(Z)]
    strip = [strip[0]] + [swap(strip[b], "z", Z, b) for b in range(1, Z)]
    system, inverse = factor_begin(where, mine, other, misfit)
    strip, system = lax.optimization_barrier((strip, system))
    narrow = wide // Y
    cut = [
        jnp.concatenate(
            [lax.dynamic_slice_in_dim(part, (yid ^ a) * narrow, narrow, 1) for part in strip], axis=0
        )
        for a in range(Y)
    ]
    cut = [cut[0]] + [swap(cut[a], "y", Y, a) for a in range(1, Y)]
    system, later = factor_finish(system, inverse)
    right, cut, system = lax.optimization_barrier((right, cut, system))
    work = solve(where, system, inverse, later, cut)
    change = combine(where, right, swap(right, "core", 2, 1), work, misfit)
    return turnover_effect + lax.all_to_all(change, ("z", "y"), 0, 1, tiled=True)


def solution(mesh):
    grid = Mesh(mesh.devices.reshape(Z, Y, X, 2), ("z", "y", "x", "core"))
    mem, cell = ("z", "y"), ("x", "core")
    in_specs = (
        P(mem, cell),
        P(cell),
        P(cell),
        P(cell),
        P(None, cell),
        P(None, cell),
        P(cell, None),
        P(cell, None),
        P(cell),
        P(cell),
        P(mem, cell),
    )
    return jax.shard_map(
        body, mesh=grid, in_specs=in_specs, out_specs=P(mem, cell), check_vma=False
    )
```

```python
import math

import jax
import jax.numpy as jnp
from jax import lax
from jax.experimental import pallas as pl
from jax.experimental.pallas import tpu as pltpu
from jax.sharding import Mesh, PartitionSpec as P

STEPS = 6
BLOCK = 128
TAPS = 4
Z = 4
Y = 4
X = 4
LANES = 128
HALF = 128
TILE = 256
CHUNK = 1024
f32 = jnp.float32

ANY_VMEM = pl.BlockSpec(memory_space=pltpu.VMEM)
ANY_SMEM = pl.BlockSpec(memory_space=pltpu.SMEM)


def mm(left, right):
    return jnp.dot(left, right, precision=lax.Precision.HIGHEST, preferred_element_type=f32)


def mm_last(left, right):
    return lax.dot_general(
        left, right, (((1,), (1,)), ((), ())),
        precision=lax.Precision.HIGHEST, preferred_element_type=f32,
    )


def forward_kernel(
    effect, base, fast, slow, init, fall, taps, weights, observed, var, pred, resp, coef
):
    members, cells = effect.shape
    w = slow[...]
    f = fast[...]
    left_slow = [jnp.zeros_like(w)]
    left_fast = [jnp.zeros_like(w)]
    for _ in range(STEPS):
        left_fast.append(0.7 * f + 0.3 * f * left_slow[-1] + (1.0 - f) * left_fast[-1])
        left_slow.append(w + (1.0 - w) * left_slow[-1])
    share = [0.6 + 0.4 * left_fast[STEPS - 1 - t] for t in range(STEPS)]
    for power in range(STEPS):
        total = share[power] * init[0:1, :]
        for t in range(power + 1, STEPS):
            total = total + share[t] * fall[t - 1 - power : t - power, :]
        coef[power : power + 1, :] = total
    coef[6:7, :] = init[1:2, :] * left_fast[STEPS] + init[2:3, :] * left_slow[STEPS]
    coef[7:8, :] = -base[...]

    def rows(i, _):
        at = pl.ds(pl.multiple_of(i * 8, 8), 8)
        kept = jnp.exp(coef[7:8, :] * jnp.exp(effect[at, :]))
        total = coef[5:6, :]
        for power in range(4, -1, -1):
            total = total * kept + coef[power : power + 1, :]
        resp[at, :] = coef[6:7, :] + (1.0 - kept) * total
        return 0

    lax.fori_loop(0, members // 8, rows, 0)
    position = lax.broadcasted_iota(jnp.int32, (BLOCK, LANES), 0)
    owner = lax.broadcasted_iota(jnp.int32, (members, LANES), 1) // 32
    for group in range(cells // (4 * BLOCK)):
        lanes = slice(group * LANES, (group + 1) * LANES)
        table = jnp.zeros((BLOCK, LANES), f32)
        for k in range(TAPS):
            table = table + jnp.where(taps[k : k + 1, lanes] == position, weights[k : k + 1, lanes], 0.0)
        stacked = jnp.concatenate(
            [resp[:, (4 * group + b) * BLOCK : (4 * group + b + 1) * BLOCK] for b in range(4)], axis=0
        )
        product = mm(stacked, table)
        out = product[:members]
        for b in range(1, 4):
            out = jnp.where(owner == b, product[b * members : (b + 1) * members], out)
        pred[0:members, lanes] = out
        residual = observed[:, lanes] - out
        spread = jnp.sum(residual * residual, axis=0, keepdims=True) / var[:, lanes]
        pred[members : members + 1, lanes] = jnp.sum(out, axis=0, keepdims=True)
        pred[members + 1 :, lanes] = jnp.broadcast_to(spread, (7, LANES))


def forward(effect, base, fast, slow, init, fall, taps, weights, observed, var):
    members, cells = effect.shape
    obs = taps.shape[1]
    obs_chunk = CHUNK // 4

    def wide(rows, width):
        return pl.BlockSpec((rows, width), lambda i: (0, i))

    return pl.pallas_call(
        forward_kernel,
        grid=(cells // CHUNK,),
        in_specs=[
            wide(members, CHUNK), wide(1, CHUNK), wide(1, CHUNK), wide(1, CHUNK),
            wide(3, CHUNK), wide(STEPS, CHUNK), wide(TAPS, obs_chunk), wide(TAPS, obs_chunk),
            wide(1, obs_chunk), wide(1, obs_chunk),
        ],
        out_specs=wide(members + 8, obs_chunk),
        out_shape=jax.ShapeDtypeStruct((members + 8, obs), f32),
        scratch_shapes=[pltpu.VMEM((members, CHUNK), f32), pltpu.VMEM((8, CHUNK), f32)],
        cost_estimate=cost(2e10),
        name="forward",
    )(effect, base, fast, slow, init, fall, taps, weights, observed, var)


def gram_kernel(
    where, e0, e1, e2, e3, e4, t0, t2, p1, p2, p3, n0, n1, n2, observed, var,
    keep, send, left, right, total, misfit,
):
    step = pl.program_id(0)
    zid, yid = where[0], where[1]
    members = n0.shape[0]
    half = members // 2
    member_count = members * Z * Y
    inv_root = 1.0 / math.sqrt(member_count - 1)
    tails = t0[...] + t2[...] + e3[half:, :] + e4[half:, :]
    shares = jnp.sum(tails[1:2, :], axis=1, keepdims=True)
    mean = tails[0:1, :] / member_count
    inv_var = 1.0 / var[...]
    root_var = jnp.sqrt(var[...])

    kept = members + 8
    for turn, skip, count, e, n, below in (
        (0, 0, members, e0, n0, 0), (3, 0, members, e1, n1, 0), (1, 0, members, e2, n2, 0),
        (2, 0, half, e3, e1, kept), (2, half, half, e4, e2, kept),
    ):
        at = pl.multiple_of(((yid + turn) & 3) * members + skip, half)
        left[pl.ds(at, count), :] = (e[0:count, :] - mean) * inv_root
        left[pl.ds(at + Y * members, count), :] = (
            observed[...] + root_var * n[below : below + count, :] - e[0:count, :]
        )
    for turn, p in ((0, e0), (3, p1), (1, p2), (2, p3)):
        at = pl.multiple_of(((zid + turn) & 3) * members, members)
        right[pl.ds(at, members), :] = (p[0:members, :] - mean) * inv_root * inv_var

    product = mm_last(left[...], right[...])

    @pl.when(step == 0)
    def _():
        total[...] = product
        misfit[...] = jnp.broadcast_to(shares, misfit.shape)

    @pl.when(step > 0)
    def _():
        total[...] = total[...] + product
        misfit[...] = misfit[...] + shares

    @pl.when(step == pl.num_programs(0) - 1)
    def _():
        core, xid = where[2], where[3]
        for part, offset in ((keep, core * 32), (send, 32 - core * 32)):
            for a in range(X):
                at = pl.multiple_of((xid ^ a) * 64 + offset, 32)
                part[a, 0:32, 0:TILE] = total[pl.ds(at, 32), :]
                part[a, 0:32, TILE : 2 * TILE] = total[pl.ds(at + TILE, 32), :]
                part[a, 32:40, :] = jnp.broadcast_to(misfit[0:1, 0:1], (8, 2 * TILE))


def gram_block(where, rows, columns, noise, observed, var):
    members, obs = noise[0].shape
    half = members // 2
    width = 512

    def chunk(n):
        return pl.BlockSpec((n, width), lambda i: (0, i))

    return pl.pallas_call(
        gram_kernel,
        grid=(obs // width,),
        in_specs=[ANY_SMEM, chunk(members + 8)] + [chunk(members + half + 8)] * 2
        + [chunk(half + 8)] * 2 + [chunk(8)] * 2 + [chunk(members + 8)] * 3 + [chunk(members)] * 3
        + [chunk(1)] * 2,
        out_specs=[pl.BlockSpec((X, 40, 2 * TILE), lambda i: (0, 0, 0))] * 2,
        out_shape=[jax.ShapeDtypeStruct((X, 40, 2 * TILE), f32)] * 2,
        scratch_shapes=[
            pltpu.VMEM((2 * TILE, width), f32),
            pltpu.VMEM((TILE, width), f32),
            pltpu.VMEM((2 * TILE, TILE), f32),
            pltpu.VMEM((8, LANES), f32),
        ],
        cost_estimate=cost(8e9),
        name="gram",
    )(where, *rows, *columns, *noise, observed, var)


def cost(flops):
    return pl.CostEstimate(flops=int(flops), bytes_accessed=int(1e7), transcendentals=0)


def invert_block(rows):
    width = HALF
    count = width // 8
    rows = list(rows)
    lane = lax.broadcasted_iota(jnp.int32, (8, width), 1)
    sub = lax.broadcasted_iota(jnp.int32, (8, width), 0)

    def row(value, r):
        return jnp.broadcast_to(value[r : r + 1, :], (8, width))

    for block in range(count):
        low = 8 * block
        panel = rows[block]
        inside = (lane >= low) & (lane < low + 8)
        early = {
            i: [jnp.broadcast_to(rows[i][:, low + p : low + p + 1], (8, width)) for p in range(8)]
            for i in range(block + 1, min(block + 3, count))
        }
        pivots = [jnp.broadcast_to(panel[:, low + p : low + p + 1], (8, width)) for p in range(8)]
        for r in range(8):
            heads = [row(pivots[p], r) for p in range(8)]
            inverse = 1.0 / heads[r]
            here = sub == r
            column = jnp.where(here, 0.0, pivots[r])
            for p in range(8):
                if p != r:
                    scaled = heads[p] * inverse
                    pivots[p] = jnp.where(here, scaled, pivots[p] - column * scaled)
            pivots[r] = jnp.where(here, inverse, -column * inverse)
        panel = jnp.where(inside, jnp.where(lane - low == sub, 1.0, 0.0), panel)
        terms = [pivots[p] * row(panel, p) for p in range(8)]
        while len(terms) > 1:
            terms = [terms[i] + terms[i + 1] for i in range(0, len(terms), 2)]
        solved = terms[0]
        heads = [row(solved, p) for p in range(8)]
        zero = jnp.zeros((8, width), f32)
        masked = [
            zero if block <= i <= block + 2 else jnp.where(inside, rows[i], 0.0) for i in range(count)
        ]
        spread = [solved if i == block else zero for i in range(count)]
        product = mm(jnp.concatenate(masked, axis=0), jnp.concatenate(spread, axis=0))
        for i in range(count):
            if i == block:
                rows[i] = solved
            elif i in early:
                terms = [early[i][p] * heads[p] for p in range(8)]
                while len(terms) > 1:
                    terms = [terms[j] + terms[j + 1] for j in range(0, len(terms), 2)]
                rows[i] = jnp.where(inside, 0.0, rows[i]) - terms[0]
            else:
                rows[i] = jnp.where(inside, 0.0, rows[i]) - product[8 * i : 8 * i + 8]
    return rows


def begin_kernel(where, mine, other, misfit, system, inverses, last, halves, ahead, behind):
    core = where[2]
    scale = f32(1024 * 16384) / misfit[0:1, 0:1]
    for z in range(Z):
        for y in range(Y):
            for x in range(X):
                piece = slice(((z * Y + y) * X + x) * 32, ((z * Y + y) * X + x) * 32 + 32)
                at = x * TILE + z * 64
                lanes = slice(y * TILE, (y + 1) * TILE)
                system[pl.ds(pl.multiple_of(at + core * 32, 32), 32), lanes] = mine[piece, :] * scale
                system[pl.ds(pl.multiple_of(at + 32 - core * 32, 32), 32), lanes] = other[piece, :] * scale
    eye = jnp.where(
        lax.broadcasted_iota(jnp.int32, (HALF, HALF), 0) == lax.broadcasted_iota(jnp.int32, (HALF, HALF), 1),
        1.0, 0.0,
    )
    for d in range(system.shape[0] // HALF):
        at = slice(d * HALF, (d + 1) * HALF)
        system[at, at] = system[at, at] + eye
    eliminate(system, inverses, 0, last, halves, ahead, behind)


def finish_kernel(before, earlier, system, inverses, last, halves, ahead, behind, arrived):
    copy = pltpu.make_async_copy(before, system, arrived)
    copy.start()
    last[...] = earlier[TILE:, :]
    copy.wait()
    eliminate(system, inverses, 2, last, halves, ahead, behind)


def eliminate(system, inverses, start, last, halves, ahead, behind):
    tiles = system.shape[0] // TILE

    def spread(k):
        top = pl.multiple_of(k * TILE, TILE)

        def across(t, _):
            lanes = pl.ds(pl.multiple_of(t * TILE, TILE), TILE)
            system[pl.ds(top, TILE), lanes] = mm(last[...], system[pl.ds(top, TILE), lanes])

            def down(i, _):
                at = pl.ds(pl.multiple_of(i * TILE, TILE), TILE)
                system[at, lanes] = system[at, lanes] - mm(
                    system[at, pl.ds(top, TILE)], system[pl.ds(top, TILE), lanes]
                )
                return 0

            lax.fori_loop(k + 1, tiles, down, 0)
            return 0

        lax.fori_loop(k + 1, tiles, across, 0)

    def stage(k, _):
        @pl.when(k > 0)
        def _():
            spread(k - 1)

        top = pl.multiple_of(k * TILE, TILE)
        low = pl.multiple_of(k * TILE + HALF, HALF)

        def half(h, _):
            at = pl.multiple_of(top + h * HALF, HALF)
            block = [system[pl.ds(at + 8 * j, 8), pl.ds(at, HALF)] for j in range(HALF // 8)]
            block = invert_block(block)
            for j in range(HALF // 8):
                halves[pl.ds(pl.multiple_of(h * HALF + 8 * j, 8), 8), :] = block[j]

            @pl.when(h == 0)
            def _():
                first = halves[0:HALF, :]
                upper = system[pl.ds(top, HALF), pl.ds(low, HALF)]
                ahead[...] = mm(first, upper)
                behind[...] = mm(system[pl.ds(low, HALF), pl.ds(top, HALF)], first)
                system[pl.ds(low, HALF), pl.ds(low, HALF)] = (
                    system[pl.ds(low, HALF), pl.ds(low, HALF)] - mm(behind[...], upper)
                )

            return 0

        lax.fori_loop(0, 2, half, 0)
        second = halves[HALF:, :]
        corner = mm(second, behind[...])
        last[0:HALF, 0:HALF] = halves[0:HALF, :] + mm(ahead[...], corner)
        last[0:HALF, HALF:] = -mm(ahead[...], second)
        last[HALF:, 0:HALF] = -corner
        last[HALF:, HALF:] = second
        inverses[pl.ds(pl.multiple_of((k - start) * TILE, TILE), TILE), :] = last[...]
        return 0

    lax.fori_loop(start, start + 2, stage, 0)


FACTOR_SCRATCH = [
    pltpu.VMEM((TILE, TILE), f32), pltpu.VMEM((TILE, HALF), f32), pltpu.VMEM((HALF, HALF), f32),
    pltpu.VMEM((HALF, HALF), f32),
]


def factor_begin(where, mine, other, misfit):
    n = TILE * Y
    return pl.pallas_call(
        begin_kernel,
        in_specs=[ANY_SMEM, ANY_VMEM, ANY_VMEM, ANY_VMEM],
        out_specs=[ANY_VMEM, ANY_VMEM],
        out_shape=[jax.ShapeDtypeStruct((n, n), f32), jax.ShapeDtypeStruct((2 * TILE, TILE), f32)],
        scratch_shapes=FACTOR_SCRATCH,
        cost_estimate=cost(2e10),
        name="factor_begin",
    )(where, mine, other, misfit)


def factor_finish(system, earlier):
    n = system.shape[0]
    return pl.pallas_call(
        finish_kernel,
        in_specs=[pl.BlockSpec(memory_space=pl.ANY), ANY_VMEM],
        out_specs=[ANY_VMEM, ANY_VMEM],
        out_shape=[jax.ShapeDtypeStruct((n, n), f32), jax.ShapeDtypeStruct((2 * TILE, TILE), f32)],
        scratch_shapes=FACTOR_SCRATCH + [pltpu.SemaphoreType.DMA],
        cost_estimate=cost(2e10),
        name="factor_finish",
    )(system, earlier)


def solve_kernel(where, system, earlier, later, b0, b1, b2, b3, work):
    zid, yid = where[0], where[1]
    n = system.shape[0]
    tiles = n // TILE
    for a, block in enumerate((b0, b1, b2, b3)):
        for b in range(Z):
            at = pl.multiple_of((yid ^ a) * TILE + (zid ^ b) * 64, 64)
            work[pl.ds(at, 64), :] = block[b * 64 : (b + 1) * 64, :]
    mean = jnp.sum(work[...], axis=0, keepdims=True) / n
    inv_root = 1.0 / math.sqrt(n - 1)
    work[...] = (work[...] - mean) * inv_root
    for k in range(tiles):
        at = slice(k * TILE, (k + 1) * TILE)
        source = earlier if k < 2 else later
        work[at, :] = mm(source[(k % 2) * TILE : (k % 2 + 1) * TILE, :], work[at, :])

        def down(i, _, at=at):
            low = pl.ds(pl.multiple_of(i * TILE, TILE), TILE)
            work[low, :] = work[low, :] - mm(system[low, at], work[at, :])
            return 0

        lax.fori_loop(k + 1, tiles, down, 0)
    for k in range(tiles - 2, -1, -1):
        at = slice(k * TILE, (k + 1) * TILE)
        rest = slice((k + 1) * TILE, n)
        work[at, :] = work[at, :] - mm(system[at, rest], work[rest, :])


def solve(where, system, earlier, later, blocks):
    return pl.pallas_call(
        solve_kernel,
        in_specs=[ANY_SMEM] + [ANY_VMEM] * 7,
        out_specs=ANY_VMEM,
        out_shape=jax.ShapeDtypeStruct((system.shape[0], blocks[0].shape[1]), f32),
        cost_estimate=cost(5e9),
        name="solve",
    )(where, system, earlier, later, *blocks)


def combine_kernel(where, mine, other, work, misfit, out):
    core = where[2]
    scale = f32(1024 * 16384) / misfit[0:1, 0:1]
    rows = TILE // 2
    total = jnp.zeros((TILE, work.shape[1]), f32)
    for y in range(Y):
        at = slice(y * rows, (y + 1) * rows)
        block = jnp.concatenate([mine[at, :], other[at, :]], axis=0)
        total = total + mm(block, work[y * TILE : (y + 1) * TILE, :])
    total = scale * total
    for c, offset in enumerate((core * 32, 32 - core * 32)):
        for x in range(X):
            low = c * rows + x * 32
            out[pl.ds(pl.multiple_of(x * 64 + offset, 32), 32), :] = total[low : low + 32, :]


def combine(where, mine, other, work, misfit):
    n, width = work.shape
    rows = pl.BlockSpec((Y * TILE // 2, TILE), lambda z: (z, 0))
    return pl.pallas_call(
        combine_kernel,
        grid=(Z,),
        in_specs=[ANY_SMEM, rows, rows, ANY_VMEM, ANY_VMEM],
        out_specs=pl.BlockSpec((TILE, width), lambda z: (z, 0)),
        out_shape=jax.ShapeDtypeStruct((n, width), f32),
        cost_estimate=cost(6e9),
        name="combine",
    )(where, mine, other, work, misfit)


def collect(piece):
    pieces = lax.all_to_all(
        jnp.broadcast_to(piece[None], (Z * Y * X,) + piece.shape), ("z", "y", "x"), 0, 0, tiled=True
    )
    return pieces.reshape(Z * Y * X * piece.shape[0], piece.shape[1])


def onward(low, high, axis):
    low = lax.ppermute(low, axis, [(i, (i + 1) % 4) for i in range(4)])
    high = lax.ppermute(high, axis, [(i, (i + 3) % 4) for i in range(4)])
    return low, high


def swap(value, axis, size, bit):
    return lax.ppermute(value, axis, [(i, i ^ bit) for i in range(size)])


def body(
    turnover_effect,
    base_rate,
    fast_rate,
    slow_rate,
    init_pools,
    litterfall,
    obs_taps,
    obs_weights,
    observed,
    obs_var,
    obs_noise,
):
    members, cells = turnover_effect.shape
    obs = obs_taps.shape[0]
    zid, yid, core = lax.axis_index("z"), lax.axis_index("y"), lax.axis_index("core")
    where = jnp.stack([zid, yid, core, lax.axis_index("x")]).astype(jnp.int32)
    observed = observed[None, :]
    obs_var = obs_var[None, :]
    noise = onward(obs_noise, obs_noise, "y")
    predicted = forward(
        turnover_effect, base_rate[None, :], fast_rate[None, :], slow_rate[None, :],
        init_pools, litterfall, obs_taps.T, obs_weights.T, observed, obs_var,
    )
    predicted, noise = lax.optimization_barrier((predicted, noise))
    half = members // 2
    columns = onward(predicted, predicted, "z") + (swap(predicted, "z", Z, 2),)
    back, forth = onward(
        jnp.concatenate([predicted, noise[0][:half]], axis=0),
        jnp.concatenate([predicted, noise[1][half:]], axis=0),
        "y",
    )
    sums = sum((block[members:] for block in columns), predicted[members:])
    sums, back, forth = lax.optimization_barrier((sums, back, forth))
    rows = (predicted, back, forth) + onward(
        jnp.concatenate([back[:half], sums], axis=0),
        jnp.concatenate([forth[half:members], sums], axis=0),
        "y",
    ) + (sums, swap(sums, "y", Y, 2))
    noise = (obs_noise,) + noise
    keep, send = gram_block(where, rows, columns, noise, observed, obs_var)
    part = keep + swap(send, "core", 2, 1)
    shared = part[0] + sum(swap(part[a], "x", X, a) for a in range(1, X))
    piece, right, misfit = shared[:32, :TILE], shared[:32, TILE:], shared[32:, :LANES]
    mine = collect(piece)
    effect, mine = lax.optimization_barrier((turnover_effect, mine))
    other = swap(mine, "core", 2, 1)
    wide = cells // Z
    strip = [lax.dynamic_slice_in_dim(effect, (zid ^ b) * wide, wide, 1) for b in range(Z)]
    strip = [strip[0]] + [swap(strip[b], "z", Z, b) for b in range(1, Z)]
    system, inverse = factor_begin(where, mine, other, misfit)
    strip, right, system = lax.optimization_barrier((strip, right, system))
    right = collect(right)
    narrow = wide // Y
    cut = [
        jnp.concatenate(
            [lax.dynamic_slice_in_dim(part, (yid ^ a) * narrow, narrow, 1) for part in strip], axis=0
        )
        for a in range(Y)
    ]
    cut = [cut[0]] + [swap(cut[a], "y", Y, a) for a in range(1, Y)]
    system, later = factor_finish(system, inverse)
    cut, system = lax.optimization_barrier((cut, system))
    work = solve(where, system, inverse, later, cut)
    right, work = lax.optimization_barrier((right, work))
    change = combine(where, right, swap(right, "core", 2, 1), work, misfit)
    return turnover_effect + lax.all_to_all(change, ("z", "y"), 0, 1, tiled=True)


def solution(mesh):
    grid = Mesh(mesh.devices.reshape(Z, Y, X, 2), ("z", "y", "x", "core"))
    mem, cell = ("z", "y"), ("x", "core")
    in_specs = (
        P(mem, cell),
        P(cell),
        P(cell),
        P(cell),
        P(None, cell),
        P(None, cell),
        P(cell, None),
        P(cell, None),
        P(cell),
        P(cell),
        P(mem, cell),
    )
    return jax.shard_map(
        body, mesh=grid, in_specs=in_specs, out_specs=P(mem, cell), check_vma=False
    )
```

```python
import math

import jax
import jax.numpy as jnp
from jax import lax
from jax.experimental import pallas as pl
from jax.experimental.pallas import tpu as pltpu
from jax.sharding import Mesh, PartitionSpec as P

STEPS = 6
BLOCK = 128
TAPS = 4
Z = 4
Y = 4
X = 4
LANES = 128
HALF = 128
TILE = 256
CHUNK = 1024
f32 = jnp.float32

ANY_VMEM = pl.BlockSpec(memory_space=pltpu.VMEM)
ANY_SMEM = pl.BlockSpec(memory_space=pltpu.SMEM)


def mm(left, right):
    return jnp.dot(left, right, precision=lax.Precision.HIGHEST, preferred_element_type=f32)


def mm_last(left, right):
    return lax.dot_general(
        left, right, (((1,), (1,)), ((), ())),
        precision=lax.Precision.HIGHEST, preferred_element_type=f32,
    )


def forward_kernel(
    effect, base, fast, slow, init, fall, taps, weights, observed, var, pred, resp, coef
):
    members, cells = effect.shape
    w = slow[...]
    f = fast[...]
    left_slow = [jnp.zeros_like(w)]
    left_fast = [jnp.zeros_like(w)]
    for _ in range(STEPS):
        left_fast.append(0.7 * f + 0.3 * f * left_slow[-1] + (1.0 - f) * left_fast[-1])
        left_slow.append(w + (1.0 - w) * left_slow[-1])
    share = [0.6 + 0.4 * left_fast[STEPS - 1 - t] for t in range(STEPS)]
    for power in range(STEPS):
        total = share[power] * init[0:1, :]
        for t in range(power + 1, STEPS):
            total = total + share[t] * fall[t - 1 - power : t - power, :]
        coef[power : power + 1, :] = total
    coef[6:7, :] = init[1:2, :] * left_fast[STEPS] + init[2:3, :] * left_slow[STEPS]
    coef[7:8, :] = -base[...]

    def rows(i, _):
        at = pl.ds(pl.multiple_of(i * 8, 8), 8)
        kept = jnp.exp(coef[7:8, :] * jnp.exp(effect[at, :]))
        total = coef[5:6, :]
        for power in range(4, -1, -1):
            total = total * kept + coef[power : power + 1, :]
        resp[at, :] = coef[6:7, :] + (1.0 - kept) * total
        return 0

    lax.fori_loop(0, members // 8, rows, 0)
    position = lax.broadcasted_iota(jnp.int32, (BLOCK, LANES), 0)
    owner = lax.broadcasted_iota(jnp.int32, (members, LANES), 1) // 32
    for group in range(cells // (4 * BLOCK)):
        lanes = slice(group * LANES, (group + 1) * LANES)
        table = jnp.zeros((BLOCK, LANES), f32)
        for k in range(TAPS):
            table = table + jnp.where(taps[k : k + 1, lanes] == position, weights[k : k + 1, lanes], 0.0)
        stacked = jnp.concatenate(
            [resp[:, (4 * group + b) * BLOCK : (4 * group + b + 1) * BLOCK] for b in range(4)], axis=0
        )
        product = mm(stacked, table)
        out = product[:members]
        for b in range(1, 4):
            out = jnp.where(owner == b, product[b * members : (b + 1) * members], out)
        pred[0:members, lanes] = out
        residual = observed[:, lanes] - out
        spread = jnp.sum(residual * residual, axis=0, keepdims=True) / var[:, lanes]
        pred[members : members + 1, lanes] = jnp.sum(out, axis=0, keepdims=True)
        pred[members + 1 :, lanes] = jnp.broadcast_to(spread, (7, LANES))


def forward(effect, base, fast, slow, init, fall, taps, weights, observed, var):
    members, cells = effect.shape
    obs = taps.shape[1]
    obs_chunk = CHUNK // 4

    def wide(rows, width):
        return pl.BlockSpec((rows, width), lambda i: (0, i))

    return pl.pallas_call(
        forward_kernel,
        grid=(cells // CHUNK,),
        in_specs=[
            wide(members, CHUNK), wide(1, CHUNK), wide(1, CHUNK), wide(1, CHUNK),
            wide(3, CHUNK), wide(STEPS, CHUNK), wide(TAPS, obs_chunk), wide(TAPS, obs_chunk),
            wide(1, obs_chunk), wide(1, obs_chunk),
        ],
        out_specs=wide(members + 8, obs_chunk),
        out_shape=jax.ShapeDtypeStruct((members + 8, obs), f32),
        scratch_shapes=[pltpu.VMEM((members, CHUNK), f32), pltpu.VMEM((8, CHUNK), f32)],
        cost_estimate=cost(2e10),
        name="forward",
    )(effect, base, fast, slow, init, fall, taps, weights, observed, var)


def gram_kernel(
    where, e0, e1, e2, e3, e4, t0, t2, p1, p2, p3, n0, n1, n2, observed, var,
    keep, send, left, right, total, misfit,
):
    step = pl.program_id(0)
    zid, yid = where[0], where[1]
    members = n0.shape[0]
    half = members // 2
    member_count = members * Z * Y
    inv_root = 1.0 / math.sqrt(member_count - 1)
    tails = t0[...] + t2[...] + e3[half:, :] + e4[half:, :]
    shares = jnp.sum(tails[1:2, :], axis=1, keepdims=True)
    mean = tails[0:1, :] / member_count
    inv_var = 1.0 / var[...]
    root_var = jnp.sqrt(var[...])

    kept = members + 8
    for turn, skip, count, e, n, below in (
        (0, 0, members, e0, n0, 0), (3, 0, members, e1, n1, 0), (1, 0, members, e2, n2, 0),
        (2, 0, half, e3, e1, kept), (2, half, half, e4, e2, kept),
    ):
        at = pl.multiple_of(((yid + turn) & 3) * members + skip, half)
        left[pl.ds(at, count), :] = (e[0:count, :] - mean) * inv_root
        left[pl.ds(at + Y * members, count), :] = (
            observed[...] + root_var * n[below : below + count, :] - e[0:count, :]
        )
    for turn, p in ((0, e0), (3, p1), (1, p2), (2, p3)):
        at = pl.multiple_of(((zid + turn) & 3) * members, members)
        right[pl.ds(at, members), :] = (p[0:members, :] - mean) * inv_root * inv_var

    product = mm_last(left[...], right[...])

    @pl.when(step == 0)
    def _():
        total[...] = product
        misfit[...] = jnp.broadcast_to(shares, misfit.shape)

    @pl.when(step > 0)
    def _():
        total[...] = total[...] + product
        misfit[...] = misfit[...] + shares

    @pl.when(step == pl.num_programs(0) - 1)
    def _():
        core, xid = where[2], where[3]
        for part, offset in ((keep, core * 32), (send, 32 - core * 32)):
            for a in range(X):
                at = pl.multiple_of((xid ^ a) * 64 + offset, 32)
                part[a, 0:32, 0:TILE] = total[pl.ds(at, 32), :]
                part[a, 0:32, TILE : 2 * TILE] = total[pl.ds(at + TILE, 32), :]
                part[a, 32:40, :] = jnp.broadcast_to(misfit[0:1, 0:1], (8, 2 * TILE))


def gram_block(where, rows, columns, noise, observed, var):
    members, obs = noise[0].shape
    half = members // 2
    width = 512

    def chunk(n):
        return pl.BlockSpec((n, width), lambda i: (0, i))

    return pl.pallas_call(
        gram_kernel,
        grid=(obs // width,),
        in_specs=[ANY_SMEM, chunk(members + 8)] + [chunk(members + half + 8)] * 2
        + [chunk(half + 8)] * 2 + [chunk(8)] * 2 + [chunk(members + 8)] * 3 + [chunk(members)] * 3
        + [chunk(1)] * 2,
        out_specs=[pl.BlockSpec((X, 40, 2 * TILE), lambda i: (0, 0, 0))] * 2,
        out_shape=[jax.ShapeDtypeStruct((X, 40, 2 * TILE), f32)] * 2,
        scratch_shapes=[
            pltpu.VMEM((2 * TILE, width), f32),
            pltpu.VMEM((TILE, width), f32),
            pltpu.VMEM((2 * TILE, TILE), f32),
            pltpu.VMEM((8, LANES), f32),
        ],
        cost_estimate=cost(8e9),
        name="gram",
    )(where, *rows, *columns, *noise, observed, var)


def cost(flops):
    return pl.CostEstimate(flops=int(flops), bytes_accessed=int(1e7), transcendentals=0)


def invert_block(rows):
    width = HALF
    count = width // 8
    rows = list(rows)
    lane = lax.broadcasted_iota(jnp.int32, (8, width), 1)
    sub = lax.broadcasted_iota(jnp.int32, (8, width), 0)

    def row(value, r):
        return jnp.broadcast_to(value[r : r + 1, :], (8, width))

    for block in range(count):
        low = 8 * block
        panel = rows[block]
        inside = (lane >= low) & (lane < low + 8)
        early = {
            i: [jnp.broadcast_to(rows[i][:, low + p : low + p + 1], (8, width)) for p in range(8)]
            for i in range(block + 1, min(block + 3, count))
        }
        pivots = [jnp.broadcast_to(panel[:, low + p : low + p + 1], (8, width)) for p in range(8)]
        for r in range(8):
            heads = [row(pivots[p], r) for p in range(8)]
            inverse = 1.0 / heads[r]
            here = sub == r
            column = jnp.where(here, 0.0, pivots[r])
            for p in range(8):
                if p != r:
                    scaled = heads[p] * inverse
                    pivots[p] = jnp.where(here, scaled, pivots[p] - column * scaled)
            pivots[r] = jnp.where(here, inverse, -column * inverse)
        panel = jnp.where(inside, jnp.where(lane - low == sub, 1.0, 0.0), panel)
        terms = [pivots[p] * row(panel, p) for p in range(8)]
        while len(terms) > 1:
            terms = [terms[i] + terms[i + 1] for i in range(0, len(terms), 2)]
        solved = terms[0]
        heads = [row(solved, p) for p in range(8)]
        zero = jnp.zeros((8, width), f32)
        masked = [
            zero if block <= i <= block + 2 else jnp.where(inside, rows[i], 0.0) for i in range(count)
        ]
        spread = [solved if i == block else zero for i in range(count)]
        product = mm(jnp.concatenate(masked, axis=0), jnp.concatenate(spread, axis=0))
        for i in range(count):
            if i == block:
                rows[i] = solved
            elif i in early:
                terms = [early[i][p] * heads[p] for p in range(8)]
                while len(terms) > 1:
                    terms = [terms[j] + terms[j + 1] for j in range(0, len(terms), 2)]
                rows[i] = jnp.where(inside, 0.0, rows[i]) - terms[0]
            else:
                rows[i] = jnp.where(inside, 0.0, rows[i]) - product[8 * i : 8 * i + 8]
    return rows


def begin_kernel(where, mine, other, misfit, system, inverses, last, halves, ahead, behind):
    core = where[2]
    scale = f32(1024 * 16384) / misfit[0:1, 0:1]
    for z in range(Z):
        for y in range(Y):
            for x in range(X):
                piece = slice(((z * Y + y) * X + x) * 32, ((z * Y + y) * X + x) * 32 + 32)
                at = x * TILE + z * 64
                lanes = slice(y * TILE, (y + 1) * TILE)
                system[pl.ds(pl.multiple_of(at + core * 32, 32), 32), lanes] = mine[piece, :] * scale
                system[pl.ds(pl.multiple_of(at + 32 - core * 32, 32), 32), lanes] = other[piece, :] * scale
    eye = jnp.where(
        lax.broadcasted_iota(jnp.int32, (HALF, HALF), 0) == lax.broadcasted_iota(jnp.int32, (HALF, HALF), 1),
        1.0, 0.0,
    )
    for d in range(system.shape[0] // HALF):
        at = slice(d * HALF, (d + 1) * HALF)
        system[at, at] = system[at, at] + eye
    eliminate(system, inverses, 0, last, halves, ahead, behind)


def finish_kernel(before, earlier, system, inverses, last, halves, ahead, behind, arrived):
    copy = pltpu.make_async_copy(before, system, arrived)
    copy.start()
    last[...] = earlier[TILE:, :]
    copy.wait()
    eliminate(system, inverses, 2, last, halves, ahead, behind)


def eliminate(system, inverses, start, last, halves, ahead, behind):
    tiles = system.shape[0] // TILE

    def spread(k):
        top = pl.multiple_of(k * TILE, TILE)

        def across(t, _):
            lanes = pl.ds(pl.multiple_of(t * TILE, TILE), TILE)
            system[pl.ds(top, TILE), lanes] = mm(last[...], system[pl.ds(top, TILE), lanes])

            def down(i, _):
                at = pl.ds(pl.multiple_of(i * TILE, TILE), TILE)
                system[at, lanes] = system[at, lanes] - mm(
                    system[at, pl.ds(top, TILE)], system[pl.ds(top, TILE), lanes]
                )
                return 0

            lax.fori_loop(k + 1, tiles, down, 0)
            return 0

        lax.fori_loop(k + 1, tiles, across, 0)

    def stage(k, _):
        @pl.when(k > 0)
        def _():
            spread(k - 1)

        top = pl.multiple_of(k * TILE, TILE)
        low = pl.multiple_of(k * TILE + HALF, HALF)

        def half(h, _):
            at = pl.multiple_of(top + h * HALF, HALF)
            block = [system[pl.ds(at + 8 * j, 8), pl.ds(at, HALF)] for j in range(HALF // 8)]
            block = invert_block(block)
            for j in range(HALF // 8):
                halves[pl.ds(pl.multiple_of(h * HALF + 8 * j, 8), 8), :] = block[j]

            @pl.when(h == 0)
            def _():
                first = halves[0:HALF, :]
                upper = system[pl.ds(top, HALF), pl.ds(low, HALF)]
                ahead[...] = mm(first, upper)
                behind[...] = mm(system[pl.ds(low, HALF), pl.ds(top, HALF)], first)
                system[pl.ds(low, HALF), pl.ds(low, HALF)] = (
                    system[pl.ds(low, HALF), pl.ds(low, HALF)] - mm(behind[...], upper)
                )

            return 0

        lax.fori_loop(0, 2, half, 0)
        second = halves[HALF:, :]
        corner = mm(second, behind[...])
        last[0:HALF, 0:HALF] = halves[0:HALF, :] + mm(ahead[...], corner)
        last[0:HALF, HALF:] = -mm(ahead[...], second)
        last[HALF:, 0:HALF] = -corner
        last[HALF:, HALF:] = second
        inverses[pl.ds(pl.multiple_of((k - start) * TILE, TILE), TILE), :] = last[...]
        return 0

    lax.fori_loop(start, start + 2, stage, 0)


FACTOR_SCRATCH = [
    pltpu.VMEM((TILE, TILE), f32), pltpu.VMEM((TILE, HALF), f32), pltpu.VMEM((HALF, HALF), f32),
    pltpu.VMEM((HALF, HALF), f32),
]


def factor_begin(where, mine, other, misfit):
    n = TILE * Y
    return pl.pallas_call(
        begin_kernel,
        in_specs=[ANY_SMEM, ANY_VMEM, ANY_VMEM, ANY_VMEM],
        out_specs=[ANY_VMEM, ANY_VMEM],
        out_shape=[jax.ShapeDtypeStruct((n, n), f32), jax.ShapeDtypeStruct((2 * TILE, TILE), f32)],
        scratch_shapes=FACTOR_SCRATCH,
        cost_estimate=cost(2e10),
        compiler_params=pltpu.CompilerParams(vmem_limit_bytes=24 << 20),
        name="factor_begin",
    )(where, mine, other, misfit)


def factor_finish(system, earlier):
    n = system.shape[0]
    return pl.pallas_call(
        finish_kernel,
        in_specs=[pl.BlockSpec(memory_space=pl.ANY), ANY_VMEM],
        out_specs=[ANY_VMEM, ANY_VMEM],
        out_shape=[jax.ShapeDtypeStruct((n, n), f32), jax.ShapeDtypeStruct((2 * TILE, TILE), f32)],
        scratch_shapes=FACTOR_SCRATCH + [pltpu.SemaphoreType.DMA],
        cost_estimate=cost(2e10),
        compiler_params=pltpu.CompilerParams(vmem_limit_bytes=24 << 20),
        name="factor_finish",
    )(system, earlier)


def solve_kernel(where, system, earlier, later, b0, b1, b2, b3, work):
    zid, yid = where[0], where[1]
    n = system.shape[0]
    tiles = n // TILE
    for a, block in enumerate((b0, b1, b2, b3)):
        for b in range(Z):
            at = pl.multiple_of((yid ^ a) * TILE + (zid ^ b) * 64, 64)
            work[pl.ds(at, 64), :] = block[b * 64 : (b + 1) * 64, :]
    mean = jnp.sum(work[...], axis=0, keepdims=True) / n
    inv_root = 1.0 / math.sqrt(n - 1)
    work[...] = (work[...] - mean) * inv_root
    for k in range(tiles):
        at = slice(k * TILE, (k + 1) * TILE)
        source = earlier if k < 2 else later
        work[at, :] = mm(source[(k % 2) * TILE : (k % 2 + 1) * TILE, :], work[at, :])
        for i in range(k + 1, tiles):
            down = slice(i * TILE, (i + 1) * TILE)
            work[down, :] = work[down, :] - mm(system[down, at], work[at, :])
    for k in range(tiles - 2, -1, -1):
        at = slice(k * TILE, (k + 1) * TILE)
        rest = slice((k + 1) * TILE, n)
        work[at, :] = work[at, :] - mm(system[at, rest], work[rest, :])


def solve(where, system, earlier, later, blocks):
    return pl.pallas_call(
        solve_kernel,
        in_specs=[ANY_SMEM] + [ANY_VMEM] * 7,
        out_specs=ANY_VMEM,
        out_shape=jax.ShapeDtypeStruct((system.shape[0], blocks[0].shape[1]), f32),
        cost_estimate=cost(5e9),
        compiler_params=pltpu.CompilerParams(vmem_limit_bytes=24 << 20),
        name="solve",
    )(where, system, earlier, later, *blocks)


def combine_kernel(rhs, work, misfit, out):
    scale = f32(1024 * 16384) / misfit[0:1, 0:1]
    total = mm(rhs[0:TILE, :], work[0:TILE, :])
    for y in range(1, Y):
        total = total + mm(rhs[y * TILE : (y + 1) * TILE, :], work[y * TILE : (y + 1) * TILE, :])
    out[...] = scale * total


def combine(rhs, work, misfit):
    n, width = work.shape
    return pl.pallas_call(
        combine_kernel,
        grid=(Z,),
        in_specs=[
            pl.BlockSpec((Y * TILE, TILE), lambda z: (z, 0)), ANY_VMEM, ANY_VMEM,
        ],
        out_specs=pl.BlockSpec((TILE, width), lambda z: (z, 0)),
        out_shape=jax.ShapeDtypeStruct((n, width), f32),
        cost_estimate=cost(6e9),
        name="combine",
    )(rhs, work, misfit)


def onward(low, high, axis):
    low = lax.ppermute(low, axis, [(i, (i + 1) % 4) for i in range(4)])
    high = lax.ppermute(high, axis, [(i, (i + 3) % 4) for i in range(4)])
    return low, high


def swap(value, axis, size, bit):
    return lax.ppermute(value, axis, [(i, i ^ bit) for i in range(size)])


def body(
    turnover_effect,
    base_rate,
    fast_rate,
    slow_rate,
    init_pools,
    litterfall,
    obs_taps,
    obs_weights,
    observed,
    obs_var,
    obs_noise,
):
    members, cells = turnover_effect.shape
    obs = obs_taps.shape[0]
    zid, yid, core = lax.axis_index("z"), lax.axis_index("y"), lax.axis_index("core")
    where = jnp.stack([zid, yid, core, lax.axis_index("x")]).astype(jnp.int32)
    observed = observed[None, :]
    obs_var = obs_var[None, :]
    noise = onward(obs_noise, obs_noise, "y")
    predicted = forward(
        turnover_effect, base_rate[None, :], fast_rate[None, :], slow_rate[None, :],
        init_pools, litterfall, obs_taps.T, obs_weights.T, observed, obs_var,
    )
    predicted, noise = lax.optimization_barrier((predicted, noise))
    half = members // 2
    columns = onward(predicted, predicted, "z") + (swap(predicted, "z", Z, 2),)
    back, forth = onward(
        jnp.concatenate([predicted, noise[0][:half]], axis=0),
        jnp.concatenate([predicted, noise[1][half:]], axis=0),
        "y",
    )
    sums = sum((block[members:] for block in columns), predicted[members:])
    sums, back, forth = lax.optimization_barrier((sums, back, forth))
    rows = (predicted, back, forth) + onward(
        jnp.concatenate([back[:half], sums], axis=0),
        jnp.concatenate([forth[half:members], sums], axis=0),
        "y",
    ) + (sums, swap(sums, "y", Y, 2))
    noise = (obs_noise,) + noise
    keep, send = gram_block(where, rows, columns, noise, observed, obs_var)
    part = keep + swap(send, "core", 2, 1)
    shared = part[0] + sum(swap(part[a], "x", X, a) for a in range(1, X))
    piece, right, misfit = shared[:32, :TILE], shared[:32, TILE:], shared[32:, :LANES]
    rhs = lax.all_gather(right, ("z", "y", "x", "core"), axis=0, tiled=True)
    mine = lax.all_to_all(
        jnp.broadcast_to(piece[None], (Z * Y * X, 32, TILE)), ("z", "y", "x"), 0, 0, tiled=True
    ).reshape(Z * Y * X * 32, TILE)
    effect, mine = lax.optimization_barrier((turnover_effect, mine))
    other = swap(mine, "core", 2, 1)
    wide = cells // Z
    strip = [lax.dynamic_slice_in_dim(effect, (zid ^ b) * wide, wide, 1) for b in range(Z)]
    strip = [strip[0]] + [swap(strip[b], "z", Z, b) for b in range(1, Z)]
    system, inverse = factor_begin(where, mine, other, misfit)
    strip, system = lax.optimization_barrier((strip, system))
    narrow = wide // Y
    cut = [
        jnp.concatenate(
            [lax.dynamic_slice_in_dim(part, (yid ^ a) * narrow, narrow, 1) for part in strip], axis=0
        )
        for a in range(Y)
    ]
    cut = [cut[0]] + [swap(cut[a], "y", Y, a) for a in range(1, Y)]
    system, later = factor_finish(system, inverse)
    work = solve(where, system, inverse, later, cut)
    change = combine(rhs, work, misfit)
    return turnover_effect + lax.all_to_all(change, ("z", "y"), 0, 1, tiled=True)


def solution(mesh):
    grid = Mesh(mesh.devices.reshape(Z, Y, X, 2), ("z", "y", "x", "core"))
    mem, cell = ("z", "y"), ("x", "core")
    in_specs = (
        P(mem, cell),
        P(cell),
        P(cell),
        P(cell),
        P(None, cell),
        P(None, cell),
        P(cell, None),
        P(cell, None),
        P(cell),
        P(cell),
        P(mem, cell),
    )
    return jax.shard_map(
        body, mesh=grid, in_specs=in_specs, out_specs=P(mem, cell), check_vma=False
    )
```

```python
import math

import jax
import jax.numpy as jnp
from jax import lax
from jax.experimental import pallas as pl
from jax.experimental.pallas import tpu as pltpu
from jax.sharding import Mesh, PartitionSpec as P

STEPS = 6
BLOCK = 128
TAPS = 4
Z = 4
Y = 4
X = 4
LANES = 128
HALF = 128
TILE = 256
CHUNK = 2048
f32 = jnp.float32

ANY_VMEM = pl.BlockSpec(memory_space=pltpu.VMEM)
ANY_SMEM = pl.BlockSpec(memory_space=pltpu.SMEM)


def mm(left, right):
    return jnp.dot(left, right, precision=lax.Precision.HIGHEST, preferred_element_type=f32)


def mm_last(left, right):
    return lax.dot_general(
        left, right, (((1,), (1,)), ((), ())),
        precision=lax.Precision.HIGHEST, preferred_element_type=f32,
    )


def forward_kernel(
    effect, base, fast, slow, init, fall, taps, weights, observed, var, pred, resp, coef
):
    members, cells = effect.shape
    w = slow[...]
    f = fast[...]
    left_slow = [jnp.zeros_like(w)]
    left_fast = [jnp.zeros_like(w)]
    for _ in range(STEPS):
        left_fast.append(0.7 * f + 0.3 * f * left_slow[-1] + (1.0 - f) * left_fast[-1])
        left_slow.append(w + (1.0 - w) * left_slow[-1])
    share = [0.6 + 0.4 * left_fast[STEPS - 1 - t] for t in range(STEPS)]
    for power in range(STEPS):
        total = share[power] * init[0:1, :]
        for t in range(power + 1, STEPS):
            total = total + share[t] * fall[t - 1 - power : t - power, :]
        coef[power : power + 1, :] = total
    coef[6:7, :] = init[1:2, :] * left_fast[STEPS] + init[2:3, :] * left_slow[STEPS]
    coef[7:8, :] = -base[...]

    def rows(i, _):
        at = pl.ds(pl.multiple_of(i * 8, 8), 8)
        kept = jnp.exp(coef[7:8, :] * jnp.exp(effect[at, :]))
        total = coef[5:6, :]
        for power in range(4, -1, -1):
            total = total * kept + coef[power : power + 1, :]
        resp[at, :] = coef[6:7, :] + (1.0 - kept) * total
        return 0

    lax.fori_loop(0, members // 8, rows, 0)
    position = lax.broadcasted_iota(jnp.int32, (BLOCK, LANES), 0)
    owner = lax.broadcasted_iota(jnp.int32, (members, LANES), 1) // 32
    for group in range(cells // (4 * BLOCK)):
        lanes = slice(group * LANES, (group + 1) * LANES)
        table = jnp.zeros((BLOCK, LANES), f32)
        for k in range(TAPS):
            table = table + jnp.where(taps[k : k + 1, lanes] == position, weights[k : k + 1, lanes], 0.0)
        stacked = jnp.concatenate(
            [resp[:, (4 * group + b) * BLOCK : (4 * group + b + 1) * BLOCK] for b in range(4)], axis=0
        )
        product = mm(stacked, table)
        out = product[:members]
        for b in range(1, 4):
            out = jnp.where(owner == b, product[b * members : (b + 1) * members], out)
        pred[0:members, lanes] = out
        residual = observed[:, lanes] - out
        spread = jnp.sum(residual * residual, axis=0, keepdims=True) / var[:, lanes]
        pred[members : members + 1, lanes] = jnp.sum(out, axis=0, keepdims=True)
        pred[members + 1 :, lanes] = jnp.broadcast_to(spread, (7, LANES))


def forward(effect, base, fast, slow, init, fall, taps, weights, observed, var):
    members, cells = effect.shape
    obs = taps.shape[1]
    obs_chunk = CHUNK // 4

    def wide(rows, width):
        return pl.BlockSpec((rows, width), lambda i: (0, i))

    return pl.pallas_call(
        forward_kernel,
        grid=(cells // CHUNK,),
        in_specs=[
            wide(members, CHUNK), wide(1, CHUNK), wide(1, CHUNK), wide(1, CHUNK),
            wide(3, CHUNK), wide(STEPS, CHUNK), wide(TAPS, obs_chunk), wide(TAPS, obs_chunk),
            wide(1, obs_chunk), wide(1, obs_chunk),
        ],
        out_specs=wide(members + 8, obs_chunk),
        out_shape=jax.ShapeDtypeStruct((members + 8, obs), f32),
        scratch_shapes=[pltpu.VMEM((members, CHUNK), f32), pltpu.VMEM((8, CHUNK), f32)],
        cost_estimate=cost(2e10),
        name="forward",
    )(effect, base, fast, slow, init, fall, taps, weights, observed, var)


def gram_kernel(
    where, e0, e1, e2, e3, e4, t0, t2, p1, p2, p3, n0, n1, n2, observed, var,
    keep, send, left, right, total, misfit,
):
    step = pl.program_id(0)
    zid, yid = where[0], where[1]
    members = n0.shape[0]
    half = members // 2
    member_count = members * Z * Y
    inv_root = 1.0 / math.sqrt(member_count - 1)
    tails = t0[...] + t2[...] + e3[half:, :] + e4[half:, :]
    shares = jnp.sum(tails[1:2, :], axis=1, keepdims=True)
    mean = tails[0:1, :] / member_count
    inv_var = 1.0 / var[...]
    root_var = jnp.sqrt(var[...])

    kept = members + 8
    for turn, skip, count, e, n, below in (
        (0, 0, members, e0, n0, 0), (3, 0, members, e1, n1, 0), (1, 0, members, e2, n2, 0),
        (2, 0, half, e3, e1, kept), (2, half, half, e4, e2, kept),
    ):
        at = pl.multiple_of(((yid + turn) & 3) * members + skip, half)
        left[pl.ds(at, count), :] = (e[0:count, :] - mean) * inv_root
        left[pl.ds(at + Y * members, count), :] = (
            observed[...] + root_var * n[below : below + count, :] - e[0:count, :]
        )
    for turn, p in ((0, e0), (3, p1), (1, p2), (2, p3)):
        at = pl.multiple_of(((zid + turn) & 3) * members, members)
        right[pl.ds(at, members), :] = (p[0:members, :] - mean) * inv_root * inv_var

    product = mm_last(left[...], right[...])

    @pl.when(step == 0)
    def _():
        total[...] = product
        misfit[...] = jnp.broadcast_to(shares, misfit.shape)

    @pl.when(step > 0)
    def _():
        total[...] = total[...] + product
        misfit[...] = misfit[...] + shares

    @pl.when(step == pl.num_programs(0) - 1)
    def _():
        core, xid = where[2], where[3]
        for part, offset in ((keep, core * 32), (send, 32 - core * 32)):
            for a in range(X):
                at = pl.multiple_of((xid ^ a) * 64 + offset, 32)
                part[a, 0:32, 0:TILE] = total[pl.ds(at, 32), :]
                part[a, 0:32, TILE : 2 * TILE] = total[pl.ds(at + TILE, 32), :]
                part[a, 32:40, :] = jnp.broadcast_to(misfit[0:1, 0:1], (8, 2 * TILE))


def gram_block(where, rows, columns, noise, observed, var):
    members, obs = noise[0].shape
    half = members // 2
    width = 512

    def chunk(n):
        return pl.BlockSpec((n, width), lambda i: (0, i))

    return pl.pallas_call(
        gram_kernel,
        grid=(obs // width,),
        in_specs=[ANY_SMEM, chunk(members + 8)] + [chunk(members + half + 8)] * 2
        + [chunk(half + 8)] * 2 + [chunk(8)] * 2 + [chunk(members + 8)] * 3 + [chunk(members)] * 3
        + [chunk(1)] * 2,
        out_specs=[pl.BlockSpec((X, 40, 2 * TILE), lambda i: (0, 0, 0))] * 2,
        out_shape=[jax.ShapeDtypeStruct((X, 40, 2 * TILE), f32)] * 2,
        scratch_shapes=[
            pltpu.VMEM((2 * TILE, width), f32),
            pltpu.VMEM((TILE, width), f32),
            pltpu.VMEM((2 * TILE, TILE), f32),
            pltpu.VMEM((8, LANES), f32),
        ],
        cost_estimate=cost(8e9),
        name="gram",
    )(where, *rows, *columns, *noise, observed, var)


def cost(flops):
    return pl.CostEstimate(flops=int(flops), bytes_accessed=int(1e7), transcendentals=0)


def invert_block(rows):
    width = HALF
    count = width // 8
    rows = list(rows)
    lane = lax.broadcasted_iota(jnp.int32, (8, width), 1)
    sub = lax.broadcasted_iota(jnp.int32, (8, width), 0)

    def row(value, r):
        return jnp.broadcast_to(value[r : r + 1, :], (8, width))

    for block in range(count):
        low = 8 * block
        panel = rows[block]
        inside = (lane >= low) & (lane < low + 8)
        early = {
            i: [jnp.broadcast_to(rows[i][:, low + p : low + p + 1], (8, width)) for p in range(8)]
            for i in range(block + 1, min(block + 3, count))
        }
        pivots = [jnp.broadcast_to(panel[:, low + p : low + p + 1], (8, width)) for p in range(8)]
        for r in range(8):
            heads = [row(pivots[p], r) for p in range(8)]
            inverse = 1.0 / heads[r]
            here = sub == r
            column = jnp.where(here, 0.0, pivots[r])
            for p in range(8):
                if p != r:
                    scaled = heads[p] * inverse
                    pivots[p] = jnp.where(here, scaled, pivots[p] - column * scaled)
            pivots[r] = jnp.where(here, inverse, -column * inverse)
        panel = jnp.where(inside, jnp.where(lane - low == sub, 1.0, 0.0), panel)
        terms = [pivots[p] * row(panel, p) for p in range(8)]
        while len(terms) > 1:
            terms = [terms[i] + terms[i + 1] for i in range(0, len(terms), 2)]
        solved = terms[0]
        heads = [row(solved, p) for p in range(8)]
        zero = jnp.zeros((8, width), f32)
        masked = [
            zero if block <= i <= block + 2 else jnp.where(inside, rows[i], 0.0) for i in range(count)
        ]
        spread = [solved if i == block else zero for i in range(count)]
        product = mm(jnp.concatenate(masked, axis=0), jnp.concatenate(spread, axis=0))
        for i in range(count):
            if i == block:
                rows[i] = solved
            elif i in early:
                terms = [early[i][p] * heads[p] for p in range(8)]
                while len(terms) > 1:
                    terms = [terms[j] + terms[j + 1] for j in range(0, len(terms), 2)]
                rows[i] = jnp.where(inside, 0.0, rows[i]) - terms[0]
            else:
                rows[i] = jnp.where(inside, 0.0, rows[i]) - product[8 * i : 8 * i + 8]
    return rows


def begin_kernel(where, mine, other, misfit, system, inverses, last, halves, ahead, behind):
    core = where[2]
    scale = f32(1024 * 16384) / misfit[0:1, 0:1]
    for z in range(Z):
        for y in range(Y):
            for x in range(X):
                piece = slice(((z * Y + y) * X + x) * 32, ((z * Y + y) * X + x) * 32 + 32)
                at = x * TILE + z * 64
                lanes = slice(y * TILE, (y + 1) * TILE)
                system[pl.ds(pl.multiple_of(at + core * 32, 32), 32), lanes] = mine[piece, :] * scale
                system[pl.ds(pl.multiple_of(at + 32 - core * 32, 32), 32), lanes] = other[piece, :] * scale
    eye = jnp.where(
        lax.broadcasted_iota(jnp.int32, (HALF, HALF), 0) == lax.broadcasted_iota(jnp.int32, (HALF, HALF), 1),
        1.0, 0.0,
    )
    for d in range(system.shape[0] // HALF):
        at = slice(d * HALF, (d + 1) * HALF)
        system[at, at] = system[at, at] + eye
    eliminate(system, inverses, 0, last, halves, ahead, behind)


def finish_kernel(before, earlier, system, inverses, last, halves, ahead, behind, arrived):
    copy = pltpu.make_async_copy(before, system, arrived)
    copy.start()
    last[...] = earlier[TILE:, :]
    copy.wait()
    eliminate(system, inverses, 2, last, halves, ahead, behind)


def eliminate(system, inverses, start, last, halves, ahead, behind):
    tiles = system.shape[0] // TILE

    def spread(k):
        top = pl.multiple_of(k * TILE, TILE)

        def across(t, _):
            lanes = pl.ds(pl.multiple_of(t * TILE, TILE), TILE)
            system[pl.ds(top, TILE), lanes] = mm(last[...], system[pl.ds(top, TILE), lanes])

            def down(i, _):
                at = pl.ds(pl.multiple_of(i * TILE, TILE), TILE)
                system[at, lanes] = system[at, lanes] - mm(
                    system[at, pl.ds(top, TILE)], system[pl.ds(top, TILE), lanes]
                )
                return 0

            lax.fori_loop(k + 1, tiles, down, 0)
            return 0

        lax.fori_loop(k + 1, tiles, across, 0)

    def stage(k, _):
        @pl.when(k > 0)
        def _():
            spread(k - 1)

        top = pl.multiple_of(k * TILE, TILE)
        low = pl.multiple_of(k * TILE + HALF, HALF)

        def half(h, _):
            at = pl.multiple_of(top + h * HALF, HALF)
            block = [system[pl.ds(at + 8 * j, 8), pl.ds(at, HALF)] for j in range(HALF // 8)]
            block = invert_block(block)
            for j in range(HALF // 8):
                halves[pl.ds(pl.multiple_of(h * HALF + 8 * j, 8), 8), :] = block[j]

            @pl.when(h == 0)
            def _():
                first = halves[0:HALF, :]
                upper = system[pl.ds(top, HALF), pl.ds(low, HALF)]
                ahead[...] = mm(first, upper)
                behind[...] = mm(system[pl.ds(low, HALF), pl.ds(top, HALF)], first)
                system[pl.ds(low, HALF), pl.ds(low, HALF)] = (
                    system[pl.ds(low, HALF), pl.ds(low, HALF)] - mm(behind[...], upper)
                )

            return 0

        lax.fori_loop(0, 2, half, 0)
        second = halves[HALF:, :]
        corner = mm(second, behind[...])
        last[0:HALF, 0:HALF] = halves[0:HALF, :] + mm(ahead[...], corner)
        last[0:HALF, HALF:] = -mm(ahead[...], second)
        last[HALF:, 0:HALF] = -corner
        last[HALF:, HALF:] = second
        inverses[pl.ds(pl.multiple_of((k - start) * TILE, TILE), TILE), :] = last[...]
        return 0

    lax.fori_loop(start, start + 2, stage, 0)


FACTOR_SCRATCH = [
    pltpu.VMEM((TILE, TILE), f32), pltpu.VMEM((TILE, HALF), f32), pltpu.VMEM((HALF, HALF), f32),
    pltpu.VMEM((HALF, HALF), f32),
]


def factor_begin(where, mine, other, misfit):
    n = TILE * Y
    return pl.pallas_call(
        begin_kernel,
        in_specs=[ANY_SMEM, ANY_VMEM, ANY_VMEM, ANY_VMEM],
        out_specs=[ANY_VMEM, ANY_VMEM],
        out_shape=[jax.ShapeDtypeStruct((n, n), f32), jax.ShapeDtypeStruct((2 * TILE, TILE), f32)],
        scratch_shapes=FACTOR_SCRATCH,
        cost_estimate=cost(2e10),
        compiler_params=pltpu.CompilerParams(vmem_limit_bytes=24 << 20),
        name="factor_begin",
    )(where, mine, other, misfit)


def factor_finish(system, earlier):
    n = system.shape[0]
    return pl.pallas_call(
        finish_kernel,
        in_specs=[pl.BlockSpec(memory_space=pl.ANY), ANY_VMEM],
        out_specs=[ANY_VMEM, ANY_VMEM],
        out_shape=[jax.ShapeDtypeStruct((n, n), f32), jax.ShapeDtypeStruct((2 * TILE, TILE), f32)],
        scratch_shapes=FACTOR_SCRATCH + [pltpu.SemaphoreType.DMA],
        cost_estimate=cost(2e10),
        compiler_params=pltpu.CompilerParams(vmem_limit_bytes=24 << 20),
        name="factor_finish",
    )(system, earlier)


def solve_kernel(where, system, earlier, later, b0, b1, b2, b3, work):
    zid, yid = where[0], where[1]
    n = system.shape[0]
    tiles = n // TILE
    for a, block in enumerate((b0, b1, b2, b3)):
        for b in range(Z):
            at = pl.multiple_of((yid ^ a) * TILE + (zid ^ b) * 64, 64)
            work[pl.ds(at, 64), :] = block[b * 64 : (b + 1) * 64, :]
    mean = jnp.sum(work[...], axis=0, keepdims=True) / n
    inv_root = 1.0 / math.sqrt(n - 1)
    work[...] = (work[...] - mean) * inv_root
    for k in range(tiles):
        at = slice(k * TILE, (k + 1) * TILE)
        source = earlier if k < 2 else later
        work[at, :] = mm(source[(k % 2) * TILE : (k % 2 + 1) * TILE, :], work[at, :])
        for i in range(k + 1, tiles):
            down = slice(i * TILE, (i + 1) * TILE)
            work[down, :] = work[down, :] - mm(system[down, at], work[at, :])
    for k in range(tiles - 2, -1, -1):
        at = slice(k * TILE, (k + 1) * TILE)
        rest = slice((k + 1) * TILE, n)
        work[at, :] = work[at, :] - mm(system[at, rest], work[rest, :])


def solve(where, system, earlier, later, blocks):
    return pl.pallas_call(
        solve_kernel,
        in_specs=[ANY_SMEM] + [ANY_VMEM] * 7,
        out_specs=ANY_VMEM,
        out_shape=jax.ShapeDtypeStruct((system.shape[0], blocks[0].shape[1]), f32),
        cost_estimate=cost(5e9),
        compiler_params=pltpu.CompilerParams(vmem_limit_bytes=24 << 20),
        name="solve",
    )(where, system, earlier, later, *blocks)


def combine_kernel(rhs, work, misfit, out):
    scale = f32(1024 * 16384) / misfit[0:1, 0:1]
    total = mm(rhs[0:TILE, :], work[0:TILE, :])
    for y in range(1, Y):
        total = total + mm(rhs[y * TILE : (y + 1) * TILE, :], work[y * TILE : (y + 1) * TILE, :])
    out[...] = scale * total


def combine(rhs, work, misfit):
    n, width = work.shape
    return pl.pallas_call(
        combine_kernel,
        grid=(Z,),
        in_specs=[
            pl.BlockSpec((Y * TILE, TILE), lambda z: (z, 0)), ANY_VMEM, ANY_VMEM,
        ],
        out_specs=pl.BlockSpec((TILE, width), lambda z: (z, 0)),
        out_shape=jax.ShapeDtypeStruct((n, width), f32),
        cost_estimate=cost(6e9),
        name="combine",
    )(rhs, work, misfit)


def onward(low, high, axis):
    low = lax.ppermute(low, axis, [(i, (i + 1) % 4) for i in range(4)])
    high = lax.ppermute(high, axis, [(i, (i + 3) % 4) for i in range(4)])
    return low, high


def swap(value, axis, size, bit):
    return lax.ppermute(value, axis, [(i, i ^ bit) for i in range(size)])


def body(
    turnover_effect,
    base_rate,
    fast_rate,
    slow_rate,
    init_pools,
    litterfall,
    obs_taps,
    obs_weights,
    observed,
    obs_var,
    obs_noise,
):
    members, cells = turnover_effect.shape
    obs = obs_taps.shape[0]
    zid, yid, core = lax.axis_index("z"), lax.axis_index("y"), lax.axis_index("core")
    where = jnp.stack([zid, yid, core, lax.axis_index("x")]).astype(jnp.int32)
    observed = observed[None, :]
    obs_var = obs_var[None, :]
    noise = onward(obs_noise, obs_noise, "y")
    predicted = forward(
        turnover_effect, base_rate[None, :], fast_rate[None, :], slow_rate[None, :],
        init_pools, litterfall, obs_taps.T, obs_weights.T, observed, obs_var,
    )
    predicted, noise = lax.optimization_barrier((predicted, noise))
    half = members // 2
    columns = onward(predicted, predicted, "z") + (swap(predicted, "z", Z, 2),)
    back, forth = onward(
        jnp.concatenate([predicted, noise[0][:half]], axis=0),
        jnp.concatenate([predicted, noise[1][half:]], axis=0),
        "y",
    )
    sums = sum((block[members:] for block in columns), predicted[members:])
    sums, back, forth = lax.optimization_barrier((sums, back, forth))
    rows = (predicted, back, forth) + onward(
        jnp.concatenate([back[:half], sums], axis=0),
        jnp.concatenate([forth[half:members], sums], axis=0),
        "y",
    ) + (sums, swap(sums, "y", Y, 2))
    noise = (obs_noise,) + noise
    keep, send = gram_block(where, rows, columns, noise, observed, obs_var)
    part = keep + swap(send, "core", 2, 1)
    shared = part[0] + sum(swap(part[a], "x", X, a) for a in range(1, X))
    piece, right, misfit = shared[:32, :TILE], shared[:32, TILE:], shared[32:, :LANES]
    rhs = lax.all_gather(right, ("z", "y", "x", "core"), axis=0, tiled=True)
    mine = lax.all_to_all(
        jnp.broadcast_to(piece[None], (Z * Y * X, 32, TILE)), ("z", "y", "x"), 0, 0, tiled=True
    ).reshape(Z * Y * X * 32, TILE)
    effect, mine = lax.optimization_barrier((turnover_effect, mine))
    other = swap(mine, "core", 2, 1)
    wide = cells // Z
    strip = [lax.dynamic_slice_in_dim(effect, (zid ^ b) * wide, wide, 1) for b in range(Z)]
    strip = [strip[0]] + [swap(strip[b], "z", Z, b) for b in range(1, Z)]
    system, inverse = factor_begin(where, mine, other, misfit)
    strip, system = lax.optimization_barrier((strip, system))
    narrow = wide // Y
    cut = [
        jnp.concatenate(
            [lax.dynamic_slice_in_dim(part, (yid ^ a) * narrow, narrow, 1) for part in strip], axis=0
        )
        for a in range(Y)
    ]
    cut = [cut[0]] + [swap(cut[a], "y", Y, a) for a in range(1, Y)]
    system, later = factor_finish(system, inverse)
    work = solve(where, system, inverse, later, cut)
    change = combine(rhs, work, misfit)
    return turnover_effect + lax.all_to_all(change, ("z", "y"), 0, 1, tiled=True)


def solution(mesh):
    grid = Mesh(mesh.devices.reshape(Z, Y, X, 2), ("z", "y", "x", "core"))
    mem, cell = ("z", "y"), ("x", "core")
    in_specs = (
        P(mem, cell),
        P(cell),
        P(cell),
        P(cell),
        P(None, cell),
        P(None, cell),
        P(cell, None),
        P(cell, None),
        P(cell),
        P(cell),
        P(mem, cell),
    )
    return jax.shard_map(
        body, mesh=grid, in_specs=in_specs, out_specs=P(mem, cell), check_vma=False
    )
```
